256 devices in a mesh: gx: 16 (over z_hi, y, core), gy: 16 (over z_lo, x).
Axes of the slice: x: 4, y: 4, z: 8 (z_hi: 2, z_lo: 4; z = z_hi * 4 + z_lo), core: 2. Of those that a mesh axis runs over, the one named last changes fastest.
Arguments:
- skip_input: bfloat16 [32, 64, 4096], P(None, 'gx', 'gy'), may hold values from -6 to 6
- w_encoder: bfloat16 [64, 864], replicated, may hold values from -0.625 to 0.625
- w_bottom: bfloat16 [128, 1728], P('gx'), may hold values from -0.3125 to 0.3125
- w_middle: bfloat16 [64, 5184], replicated, may hold values from -0.15625 to 0.15625
- w_upper: bfloat16 [32, 2592], replicated, may hold values from -0.21875 to 0.21875
- cotangent: bfloat16 [32, 64, 4096], P(None, 'gx', 'gy'), may hold values from -6 to 6
Outputs:
- features: bfloat16 [32, 64, 4096], P(None, 'gx', 'gy')
- grad_skip: bfloat16 [32, 64, 4096], P(None, 'gx', 'gy')
- grad_encoder: float32 [64, 864], replicated
- grad_bottom: float32 [128, 1728], P('gx')
- grad_middle: float32 [64, 5184], replicated
- grad_upper: float32 [32, 2592], replicated
The draws below stay inside these ranges and needn't reach their ends.
All inputs are finite; a program needn't handle non-finite values.
Results may differ from the reference program's by a relative error of at most 0.017.
Values may be sent and summed in bfloat16 or wider, within the bound.
No kernel may reach another device: no remote copies, remote signals or barrier semaphores. Data moves between devices by JAX's collectives and lax.ppermute only.
A program may use at most 64 MiB of HBM per device.

```python
import math
import jax
import jax.numpy as jnp
from jax import lax

C0 = 32
C1 = 64
C2 = 128
Z = 16
X0 = 64
Y0 = 256


def levels(stream_key, extent, pieces, low, top_value):
    factor_of = 1.0
    for position, blocks in pieces:
        steps = jax.random.uniform(jax.random.fold_in(jax.random.fold_in(stream_key, 6), position), (blocks,), jnp.float32, low / len(pieces), top_value / len(pieces))
        factor_of = factor_of * jnp.repeat(jnp.exp(steps), extent[position] // blocks).reshape((-1,) + (1,) * (len(extent) - 1 - position))
    return factor_of


def noise(stream_key, shape, width, bound, shards=(), held_as=jnp.bfloat16):
    entries = jax.random.normal(stream_key, shape, jnp.float32) * width
    if len(shards) > 0:
        entries = levels(stream_key, shape, shards, -0.22, 0.18) * entries
    return jnp.clip(entries, min=-bound, max=bound).astype(held_as)


def setup_inputs(seed: int = 0) -> dict:
    splits = jax.random.split(jax.random.key(seed), 7)
    return {
        "skip_input": noise(splits[0], (C0, X0, Y0 * Z), 1.0, 6.0, ((1, 16), (2, 16))),
        "w_encoder": noise(splits[1], (C1, 27 * C0), (27 * C0 // 8) ** -0.5, 0.625),
        "w_bottom": noise(splits[2], (C2, 27 * C1), (27 * C1 // 4) ** -0.5, 0.3125, ((0, 16),)),
        "w_middle": noise(splits[3], (C1, 27 * (C2 + C1)), (27 * C1) ** -0.5, 0.15625),
        "w_upper": noise(splits[4], (C0, 27 * (C1 + C0)), (27 * C0) ** -0.5, 0.21875),
        "cotangent": noise(splits[5], (C0, X0, Y0 * Z), 1.0, 6.0, ((1, 16), (2, 16))),
    }


def z_shift(extended, z_step, z_depth):
    length = extended.shape[2]
    padded = jnp.pad(extended, ((0, 0), (0, 0), (1, 1)))
    shifted = padded[:, :, 1 + z_step:1 + z_step + length]
    z_index = lax.broadcasted_iota(jnp.int32, (1, 1, length), 2) % z_depth + z_step
    inside = (z_index >= 0) & (z_index < z_depth)
    return jnp.where(inside, shifted, jnp.zeros_like(shifted))

def tap_piece(shifted_set, a, b, c, row_count, col_count, z_depth, flipped):
    x_off, y_off, z_off = (2 - a, 2 - b, 2 - c) if flipped else (a, b, c)
    source = shifted_set[z_off]
    tap_slice = source[:, x_off:x_off + row_count, y_off * z_depth:(y_off + col_count) * z_depth]
    return tap_slice.reshape(source.shape[0], row_count * col_count * z_depth)

def conv_forward(extended, weight, row_count, col_count, z_depth):
    in_chan = extended.shape[0]
    shifted_set = [z_shift(extended, z_step, z_depth) for z_step in (-1, 0, 1)]
    total_sum = jnp.zeros((weight.shape[0], row_count * col_count * z_depth), jnp.float32)
    for a in range(3):
        for b in range(3):
            for c in range(3):
                tap_number = 9 * a + 3 * b + c
                total_sum = total_sum + jnp.dot(weight[:, tap_number * in_chan:(tap_number + 1) * in_chan], tap_piece(shifted_set, a, b, c, row_count, col_count, z_depth, False), preferred_element_type=jnp.float32)
    return total_sum

def conv_backward(extended, weight, row_count, col_count, z_depth):
    in_chan = weight.shape[1] // 27
    shifted_set = [z_shift(extended, z_step, z_depth) for z_step in (-1, 0, 1)]
    total_sum = jnp.zeros((in_chan, row_count * col_count * z_depth), jnp.float32)
    for a in range(3):
        for b in range(3):
            for c in range(3):
                tap_number = 9 * a + 3 * b + c
                total_sum = total_sum + lax.dot_general(weight[:, tap_number * in_chan:(tap_number + 1) * in_chan], tap_piece(shifted_set, a, b, c, row_count, col_count, z_depth, True), (((0,), (0,)), ((), ())), preferred_element_type=jnp.float32)
    return total_sum

def weight_grad(extended, error_flat, row_count, col_count, z_depth):
    shifted_set = [z_shift(extended, z_step, z_depth) for z_step in (-1, 0, 1)]
    blocks = []
    for a in range(3):
        for b in range(3):
            for c in range(3):
                blocks.append(lax.dot_general(error_flat, tap_piece(shifted_set, a, b, c, row_count, col_count, z_depth, False), (((1,), (1,)), ((), ())), preferred_element_type=jnp.float32))
    return jnp.concatenate(blocks, axis=1)

def pool_mean(values, z_depth):
    channels, row_count, length = values.shape
    col_count = length // z_depth
    shaped = values.astype(jnp.float32).reshape(channels, row_count // 2, 2, col_count // 2, 2, z_depth // 2, 2)
    return shaped.mean(axis=(2, 4, 6)).reshape(channels, row_count // 2, col_count // 2 * (z_depth // 2))

def block_sum(values, z_depth):
    channels, row_count, length = values.shape
    col_count = length // z_depth
    shaped = values.reshape(channels, row_count // 2, 2, col_count // 2, 2, z_depth // 2, 2)
    return shaped.sum(axis=(2, 4, 6)).reshape(channels, row_count // 2, col_count // 2 * (z_depth // 2))

def upsample(values, z_depth):
    channels, row_count, length = values.shape
    col_count = length // z_depth
    shaped = values.reshape(channels, row_count, 1, col_count, 1, z_depth, 1)
    shaped = jnp.broadcast_to(shaped, (channels, row_count, 2, col_count, 2, z_depth, 2))
    return shaped.reshape(channels, 2 * row_count, 4 * col_count * z_depth)

def silu_slope(values):
    s_value = jax.nn.sigmoid(values)
    return s_value * (1.0 + values * (1.0 - s_value))

def pad_grid(values, z_depth):
    return jnp.pad(values, ((0, 0), (1, 1), (z_depth, z_depth)))

def reference(skip_input, w_encoder, w_bottom, w_middle, w_upper, cotangent):
    rows_fine, cols_fine = (X0, Y0)
    rows_mid, cols_mid, depth_mid = (X0 // 2, Y0 // 2, Z // 2)
    rows_low, cols_low, depth_low = (X0 // 4, Y0 // 4, Z // 4)
    cells_fine = X0 * Y0 * Z
    scale_fine = 1.0 / math.sqrt(cells_fine)
    scale_mid = 1.0 / math.sqrt(cells_fine // 8)
    scale_low = 1.0 / math.sqrt(cells_fine // 64)
    pool_top = pool_mean(skip_input, Z).astype(jnp.bfloat16)
    ext_pool = pad_grid(pool_top, depth_mid)
    pre_one = conv_forward(ext_pool, w_encoder, rows_mid, cols_mid, depth_mid)
    act_one = jax.nn.silu(pre_one).astype(jnp.bfloat16).reshape(-1, rows_mid, cols_mid * depth_mid)
    pool_mid = pool_mean(act_one, depth_mid).astype(jnp.bfloat16)
    ext_low = pad_grid(pool_mid, depth_low)
    pre_two = conv_forward(ext_low, w_bottom, rows_low, cols_low, depth_low)
    act_two = jax.nn.silu(pre_two).astype(jnp.bfloat16).reshape(-1, rows_low, cols_low * depth_low)
    cat_mid = jnp.concatenate([upsample(act_two, depth_low), act_one], axis=0)
    ext_mid = pad_grid(cat_mid, depth_mid)
    pre_three = conv_forward(ext_mid, w_middle, rows_mid, cols_mid, depth_mid)
    act_three = jax.nn.silu(pre_three).astype(jnp.bfloat16).reshape(-1, rows_mid, cols_mid * depth_mid)
    cat_top = jnp.concatenate([upsample(act_three, depth_mid), skip_input], axis=0)
    ext_top = pad_grid(cat_top, Z)
    pre_four = conv_forward(ext_top, w_upper, rows_fine, cols_fine, Z)
    top_chan = skip_input.shape[0]
    features = jax.nn.silu(pre_four).astype(jnp.bfloat16).reshape(top_chan, rows_fine, cols_fine * Z)
    err_four = (cotangent.reshape(top_chan, -1).astype(jnp.float32) * silu_slope(pre_four)).astype(jnp.bfloat16)
    grad_upper = weight_grad(ext_top, err_four, rows_fine, cols_fine, Z) * scale_fine
    dcat_top = conv_backward(pad_grid(err_four.reshape(top_chan, rows_fine, cols_fine * Z), Z), w_upper, rows_fine, cols_fine, Z).reshape(-1, rows_fine, cols_fine * Z)
    mid_chan = act_three.shape[0]
    err_three = (block_sum(dcat_top[:mid_chan], Z).reshape(mid_chan, -1) * silu_slope(pre_three)).astype(jnp.bfloat16)
    grad_middle = weight_grad(ext_mid, err_three, rows_mid, cols_mid, depth_mid) * scale_mid
    dcat_mid = conv_backward(pad_grid(err_three.reshape(mid_chan, rows_mid, cols_mid * depth_mid), depth_mid), w_middle, rows_mid, cols_mid, depth_mid).reshape(-1, rows_mid, cols_mid * depth_mid)
    low_chan = act_two.shape[0]
    err_two = (block_sum(dcat_mid[:low_chan], depth_mid).reshape(low_chan, -1) * silu_slope(pre_two)).astype(jnp.bfloat16)
    grad_bottom = weight_grad(ext_low, err_two, rows_low, cols_low, depth_low) * scale_low
    dpool_mid = conv_backward(pad_grid(err_two.reshape(low_chan, rows_low, cols_low * depth_low), depth_low), w_bottom, rows_low, cols_low, depth_low).reshape(-1, rows_low, cols_low * depth_low)
    dact_one = dcat_mid[low_chan:] + upsample(dpool_mid, depth_low) / 8.0
    err_one = (dact_one.reshape(mid_chan, -1) * silu_slope(pre_one)).astype(jnp.bfloat16)
    grad_encoder = weight_grad(ext_pool, err_one, rows_mid, cols_mid, depth_mid) * scale_mid
    dpool_top = conv_backward(pad_grid(err_one.reshape(mid_chan, rows_mid, cols_mid * depth_mid), depth_mid), w_encoder, rows_mid, cols_mid, depth_mid).reshape(-1, rows_mid, cols_mid * depth_mid)
    grad_skip = (dcat_top[mid_chan:] + upsample(dpool_top, depth_mid) / 8.0).astype(jnp.bfloat16)
    return (features, grad_skip, grad_encoder, grad_bottom, grad_middle, grad_upper)
```

```python
import math

import jax
import jax.numpy as jnp
import numpy as np
from jax import lax
from jax.experimental import pallas as pl
from jax.experimental.pallas import tpu as pltpu
from jax.sharding import PartitionSpec as P

BF = jnp.bfloat16
F32 = jnp.float32


def columns(lanes, depth, split):
    col = np.arange(lanes) // depth
    return np.where(col >= split, col - lanes // depth, col), np.arange(lanes) % depth


def upsampling(coarse, fine):
    (col_c, z_c), (col_f, z_f) = (columns(*coarse), columns(*fine))
    hit = (col_c[:, None] == col_f[None, :] // 2) & (z_c[:, None] == z_f[None, :] // 2)
    return hit.astype(np.float32)


TOP = (384, 16, 20)
WIDE = (256, 8, 16)
MID = (128, 8, 12)
LOW = (128, 4, 16)


def constants():
    low_mid = upsampling(LOW, MID)
    mid_top = upsampling(MID, TOP)
    wide_low = upsampling(LOW, WIDE).T / 8.0
    tile_pool = mid_top[:64, :256].T / 8.0
    tile_pool = np.concatenate([tile_pool, tile_pool], axis=1)
    return {
        "up_low": low_mid,
        "sum_low": low_mid.T,
        "up_mid": mid_top,
        "sum_mid": mid_top.T,
        "pool_low": wide_low,
        "pool_tile": tile_pool,
    }


def dot(a, b):
    return jnp.dot(a, b, preferred_element_type=F32)


def dot_nt(a, b):
    return lax.dot_general(a, b, (((1,), (1,)), ((), ())), preferred_element_type=F32)


def dot_split(a, b):
    head = a.astype(BF)
    rest = (a - head.astype(F32)).astype(BF)
    return dot(head, b) + dot(rest, b)


def loop(count, body):
    def step(i, carry):
        body(i)
        return carry

    lax.fori_loop(0, count, step, 0)


def lane(length):
    return lax.broadcasted_iota(jnp.int32, (1, length), 1)


def inside(region, tile_cols, total_cols, index):
    lanes, depth, split = region
    col = lane(lanes) // depth
    col = jnp.where(col >= split, col - lanes // depth, col) + index * tile_cols
    return jnp.where((col >= 0) & (col < total_cols), 1.0, 0.0)


def row_ok(row, total):
    return jnp.where((row >= 0) & (row < total), 1.0, 0.0)


def depth_masks(shape, depth):
    z = lax.broadcasted_iota(jnp.int32, shape, 1) % depth
    below = jnp.where(z == depth - 1, 0.0, 1.0).astype(BF)
    above = jnp.where(z == 0, 0.0, 1.0).astype(BF)
    return below, above


def put_taps(dst, row, first, width, value, depth):
    chans, lanes = value.shape
    below, above = depth_masks(value.shape, depth)
    kinds = (value * below, value, value * above)
    for b in range(3):
        for e in range(3):
            shift = (b - 1) * depth + (e - 1)
            piece = kinds[e]
            if shift:
                piece = pltpu.roll(piece, (-shift) % lanes, 1)
            start = (3 * b + e) * width + first
            dst[row, start : start + chans, :] = piece


def sigmoid(v):
    return 1.0 / (1.0 + jnp.exp(-v))


def silu(v):
    return v * sigmoid(v)


def slope(v):
    s = sigmoid(v)
    return s * (1.0 + v * (1.0 - s))


def row_sum(ref, row, chans):
    return (
        ref[row, 0:chans, :]
        + ref[row + 1, chans : 2 * chans, :]
        + ref[row + 2, 2 * chans : 3 * chans, :]
    )


def pool_kernel(skip, cot, pool_tile, to_left, to_right):
    for r in range(4):
        to_left[r] = skip[r, :, 0:128]
        to_left[4 + r] = cot[r, :, 0:128]
        to_right[r] = skip[r, :, 128:256]
        to_right[4 + r] = cot[r, :, 128:256]
    for q in range(2):
        pooled = dot(skip[2 * q], pool_tile[...]) + dot(skip[2 * q + 1], pool_tile[...])
        pooled = pooled.astype(BF)
        to_left[8 + q] = pooled
        to_right[8 + q] = pooled


def widen_kernel(skip, cot, own, right, left, out):
    first = jnp.where(lax.broadcasted_iota(jnp.int32, (32, 128), 1) < 64, 1.0, 0.0)
    head = first.astype(BF)
    tail = (1.0 - first).astype(BF)
    for r in range(4):
        for k, tile in enumerate((skip, cot)):
            base = 12 * k + 3 * r
            out[base] = tile[r, :, 0:128]
            out[base + 1] = tile[r, :, 128:256]
            out[base + 2] = right[4 * k + r] * head + left[4 * k + r] * tail
    for q in range(2):
        out[24 + 2 * q] = own[8 + q] * head + right[8 + q] * tail
        out[25 + 2 * q] = left[8 + q] * tail


def main_kernel(sizes, scales, *refs):
    (ids, own, up, down, far_up, far_down) = refs[:6]
    (w_enc, w_bot, w_mid, w_top, t_top, t_mid) = refs[6:12]
    (up_low, sum_low, up_mid, sum_mid, pool_low) = refs[12:17]
    (feat, dskip, packed, pre_one, taps_out, g_top, g_mid, g_bot) = refs[17:25]
    (pool_s, taps_a, sum_a, act_a, pool_l, taps_b, sum_b, act_b) = refs[25:33]
    (taps_c, sum_c, act_c, pre_c, taps_d, sum_d, err_d) = refs[33:40]
    (taps_e, sum_e, err_c, stack, taps_f, sum_f) = refs[40:46]
    (rows_all, cols_all) = sizes
    (scale_top, scale_mid, scale_low) = scales
    gx, gy = ids[0], ids[1]
    rows_mid, rows_low = rows_all // 2, rows_all // 4

    sources = (
        [(far_up, 2 * k) for k in range(1, 6)]
        + [(up, 24), (up, 26), (own, 24), (own, 26), (down, 24), (down, 26)]
        + [(far_down, 2 * k) for k in range(5)]
    )
    for k, (ref, slab) in enumerate(sources):
        keep = jnp.full((32, 128), row_ok(gx * 2 + k - 7, rows_mid)).astype(BF)
        pool_s[k, :, 0:128] = ref[slab] * keep
        pool_s[k, :, 128:256] = ref[slab + 1] * keep

    def enc_taps(k):
        put_taps(taps_a, k, 0, 32, pool_s[k], 8)
        sum_a[k] = dot(w_enc[...], taps_a[k])

    loop(16, enc_taps)
    wide_in = inside(WIDE, 8, cols_all // 2, gy)

    def enc_act(k):
        value = silu(row_sum(sum_a, k, 64)) * (wide_in * row_ok(gx * 2 + k - 6, rows_mid))
        act_a[k] = value.astype(BF)

    loop(14, enc_act)
    for m in range(4):
        pre = row_sum(sum_a, m + 5, 64)
        pre_one[m] = jnp.where(lane(128) < 96, pre[:, 0:128], pre[:, 128:256])
        taps_out[m] = taps_a[m + 6, :, 0:128]

    def low_taps(k):
        pooled = dot(act_a[2 * k], pool_low[...]) + dot(act_a[2 * k + 1], pool_low[...])
        put_taps(taps_b, k, 0, 64, pooled.astype(BF), 4)
        sum_b[k] = dot(w_bot[...], taps_b[k])

    loop(7, low_taps)
    low_in = inside(LOW, 4, cols_all // 4, gy)
    mid_in = inside(MID, 8, cols_all // 2, gy)
    pick = jnp.where(lax.broadcasted_iota(jnp.int32, (64, 128), 1) < 96, 1.0, 0.0)
    near = pick.astype(BF)
    away = (1.0 - pick).astype(BF)

    def low_act(k):
        value = silu(row_sum(sum_b, k, 128)) * (low_in * row_ok(gx + k - 2, rows_low))
        act_b[k] = dot(value.astype(BF), up_low[...]).astype(BF)

    loop(5, low_act)

    def mid_taps(k):
        put_taps(taps_c, k, 0, 192, act_b[(k + 1) // 2], 8)
        narrow = act_a[k + 3, :, 0:128] * near + act_a[k + 3, :, 128:256] * away
        put_taps(taps_c, k, 128, 192, narrow, 8)
        sum_c[k] = dot(w_mid[...], taps_c[k])

    loop(8, mid_taps)

    def mid_act(k):
        pre = row_sum(sum_c, k, 64)
        pre_c[k] = pre
        value = silu(pre) * (mid_in * row_ok(gx * 2 + k - 2, rows_mid))
        act_c[k] = dot(value.astype(BF), up_mid[...]).astype(BF)

    loop(6, mid_act)

    def skip_row(kind, k):
        part = (up, own, down)[k // 4]
        base = 12 * kind + 3 * (k % 4)
        row = jnp.concatenate([part[base], part[base + 1], part[base + 2]], axis=1)
        if 4 <= k < 8:
            return row
        return row * jnp.full((32, 384), row_ok(gx * 4 + k - 4, rows_all)).astype(BF)

    for k in range(12):
        put_taps(taps_d, k, 64, 96, skip_row(0, k), 16)

    def top_taps(j):
        for half in range(2):
            put_taps(taps_d, 2 * j + half, 0, 96, act_c[j], 16)
            sum_d[2 * j + half] = dot(w_top[...], taps_d[2 * j + half])

    loop(6, top_taps)
    for k in range(10):
        pre = row_sum(sum_d, k, 32)
        s = sigmoid(pre)
        if 3 <= k < 7:
            feat[k - 3] = (pre * s)[:, 0:256].astype(BF)
        cot = skip_row(1, k + 1).astype(F32)
        err_d[k] = (cot * (s * (1.0 + pre * (1.0 - s)))).astype(BF)

    def top_back(k):
        put_taps(taps_e, k, 0, 32, err_d[k], 16)
        sum_e[k] = dot(t_top[...], taps_e[k])

    loop(10, top_back)

    total = None
    for k in range(6):
        parts = []
        for a in range(3):
            r = k - a
            own_row = 0 <= r < 4
            parts.append(err_d[r + 3, :, 0:256] if own_row else jnp.zeros((32, 256), BF))
        term = dot_nt(jnp.concatenate(parts, axis=0), taps_d[k + 3, :, 0:256])
        total = term if total is None else total + term
    g_top[...] = (total * scale_top).astype(BF)

    def mid_err(m):
        one = row_sum(sum_e, 2 * m, 96)
        two = row_sum(sum_e, 2 * m + 1, 96)
        whole = dot_split(one[0:64] + two[0:64], sum_mid[...])
        keep = mid_in * row_ok(gx * 2 + m - 1, rows_mid)
        err_c[m] = (whole * slope(pre_c[m + 1]) * keep).astype(BF)

    loop(4, mid_err)
    for r in range(4):
        dskip[r] = row_sum(sum_e, r + 2, 96)[64:96, 0:256]

    def mid_back(m):
        put_taps(taps_f, m, 0, 64, err_c[m], 8)
        sum_f[m] = dot(t_mid[...], taps_f[m])

    loop(4, mid_back)
    own_mid = jnp.where(lax.broadcasted_iota(jnp.int32, (64, 128), 1) < 64, 1.0, 0.0).astype(BF)
    for k in range(4):
        for a in range(3):
            r = k - a
            piece = err_c[r + 1] * own_mid if 0 <= r < 2 else jnp.zeros((64, 128), BF)
            stack[k, 64 * a : 64 * a + 64, :] = piece
    total = None
    for k in range(4):
        term = dot_nt(stack[k], taps_c[k + 2])
        total = term if total is None else total + term
    g_mid[...] = (total * scale_mid).astype(BF)

    one = row_sum(sum_f, 0, 192)
    two = row_sum(sum_f, 1, 192)
    whole = dot_split(one[0:128] + two[0:128], sum_low[...])
    keep = jnp.where(lane(128) < 16, 1.0, 0.0)
    err_low = (whole * slope(row_sum(sum_b, 2, 128)) * keep).astype(BF)
    packed[0:128, :] = err_low
    both = jnp.where(lane(128) < 64, one[128:192], pltpu.roll(two[128:192], 64, 1))
    packed[128:192, :] = both.astype(BF)
    for a in range(3):
        g_bot[128 * a : 128 * a + 128, :] = (dot_nt(err_low, taps_b[a + 2]) * scale_low).astype(BF)


def tail_kernel(sizes, scale_mid, *refs):
    (ids, own, up, down, up_two, down_two, pre_one, taps_in, dskip) = refs[:9]
    (t_bot, t_enc, up_low, up_mid) = refs[9:13]
    (grad_skip, g_enc) = refs[13:15]
    (taps_a, sum_a, err_s, taps_b, sum_b) = refs[15:20]
    (rows_all, cols_all) = sizes
    gx, gy = ids[0], ids[1]
    rows_mid = rows_all // 2
    mid_in = inside(MID, 8, cols_all // 2, gy)

    for k, ref in enumerate((up_two, up, own, down, down_two)):
        value = (
            ref[0, 0:128, :].astype(F32)
            + pltpu.roll(ref[2, 0:128, :].astype(F32), 16, 1)
            + pltpu.roll(ref[1, 0:128, :].astype(F32), 112, 1)
        )
        put_taps(taps_a, k, 0, 128, value.astype(BF), 4)
        sum_a[k] = dot(t_bot[...], taps_a[k])
    ups = [dot_split(row_sum(sum_a, k, 64), up_low[...]) * 0.125 for k in range(3)]
    for m in range(4):
        ref = (up, own, own, down)[m]
        odd = m % 2 == 0
        tiles = [ref[k, 128:192, :].astype(F32) for k in range(3)]
        mine, left, right = tiles
        if odd:
            mine = pltpu.roll(mine, 64, 1)
        else:
            left, right = pltpu.roll(left, 64, 1), pltpu.roll(right, 64, 1)
        at = lane(128)
        part = jnp.where(at < 64, mine, jnp.where(at < 96, right, left))
        keep = mid_in * row_ok(gx * 2 + m - 1, rows_mid)
        err = (part + ups[(m + 1) // 2]) * slope(pre_one[m]) * keep
        err = err.astype(BF)
        err_s[m] = err
        put_taps(taps_b, m, 0, 64, err, 8)
        sum_b[m] = dot(t_enc[...], taps_b[m])
    own_mid = jnp.where(lax.broadcasted_iota(jnp.int32, (64, 128), 1) < 64, 1.0, 0.0).astype(BF)
    total = None
    for k in range(4):
        parts = []
        for a in range(3):
            r = k - a
            parts.append(err_s[r + 1] * own_mid if 0 <= r < 2 else jnp.zeros((64, 128), BF))
        term = dot_nt(jnp.concatenate(parts, axis=0), taps_in[k])
        total = term if total is None else total + term
    g_enc[...] = (total * scale_mid).astype(BF)
    for q in range(2):
        fine = dot_split(row_sum(sum_b, q, 32), up_mid[:, 0:256]) * 0.125
        for half in range(2):
            r = 2 * q + half
            grad_skip[r] = (dskip[r] + fine).astype(BF)


VMEM = pl.BlockSpec(memory_space=pltpu.VMEM)
SMEM = pl.BlockSpec(memory_space=pltpu.SMEM)


def call(kernel, name, outs, scratch, scalars, *args):
    return pl.pallas_call(
        kernel,
        name=name,
        out_shape=[jax.ShapeDtypeStruct(s, d) for s, d in outs],
        in_specs=[SMEM] * scalars + [VMEM] * (len(args) - scalars),
        out_specs=[VMEM] * len(outs),
        scratch_shapes=[pltpu.VMEM(s, d) for s, d in scratch],
        compiler_params=pltpu.CompilerParams(vmem_limit_bytes=56 * 1024 * 1024),
    )(*args)


def shift(value, axis, count, step):
    return lax.ppermute(value, axis, [(i, i + step) for i in range(count) if 0 <= i + step < count])


def turn(value, axis, count, step):
    return lax.ppermute(value, axis, [(i, (i + step) % count) for i in range(count)])


def forward_weight(w):
    out, width = w.shape
    return w.reshape(out, 3, width // 3).transpose(1, 0, 2).reshape(3 * out, width // 3)


def backward_weight(w):
    out, width = w.shape
    chans = width // 27
    taps = w.reshape(out, 27, chans)[:, ::-1, :].reshape(out, 3, 9, chans)
    return taps.transpose(1, 3, 2, 0).reshape(3 * chans, 9 * out)


def tiles_of(g):
    rows, width = g.shape
    pad = -width % 128
    g = jnp.pad(g, ((0, 0), (0, pad)))
    wide = (width + pad) // 128
    return g.reshape(rows // 8, 8, wide, 128).transpose(0, 2, 1, 3).reshape(-1, 8, 128)


def from_tiles(tiles, rows, width):
    wide = -(-width // 128)
    g = tiles.reshape(rows // 8, wide, 8, 128).transpose(0, 2, 1, 3).reshape(rows, wide * 128)
    return g[:, :width]


def full_gradient(g):
    rows, width = g.shape
    out = rows // 3
    return jnp.concatenate([g[out * a : out * a + out] for a in range(3)], axis=1).astype(F32)


def solution(mesh):
    ngx, ngy = mesh.shape["gx"], mesh.shape["gy"]
    devices = ngx * ngy
    const = {k: np.asarray(v) for k, v in constants().items()}

    def per_device(skip_input, w_encoder, w_bottom, w_middle, w_upper, cotangent):
        gx, gy = lax.axis_index("gx"), lax.axis_index("gy")
        ids = jnp.stack([gx, gy]).astype(jnp.int32)
        rows_all, cols_all = 4 * ngx, 16 * ngy
        sizes = (rows_all, cols_all)
        cells = rows_all * cols_all * 16
        scales = tuple(1.0 / math.sqrt(cells // k) for k in (1, 8, 64))
        c = {k: jnp.asarray(v, BF) for k, v in const.items()}

        blocks = jnp.broadcast_to(w_bottom[None], (ngx,) + w_bottom.shape)
        w_bot = lax.all_to_all(blocks, "gx", split_axis=0, concat_axis=0, tiled=True)
        w_bot = w_bot.reshape(ngx * w_bottom.shape[0], -1)

        skip = skip_input.transpose(1, 0, 2)
        cot = cotangent.transpose(1, 0, 2)
        to_left, to_right = call(
            pool_kernel, "pool", [((10, 32, 128), BF)] * 2, [], 0, skip, cot, c["pool_tile"]
        )
        right = shift(to_left, "gy", ngy, -1)
        left = shift(to_right, "gy", ngy, 1)
        (own,) = call(
            widen_kernel, "widen", [((28, 32, 128), BF)], [], 0, skip, cot, to_left, right, left
        )
        up = turn(own, "gx", ngx, 1)
        down = turn(own, "gx", ngx, -1)
        three = jnp.concatenate([up[24:28], own[24:28], down[24:28]], axis=0)
        far_up = turn(three, "gx", ngx, 3)
        far_down = turn(three, "gx", ngx, -3)

        outs = [
            ((4, 32, 256), BF),
            ((4, 32, 256), F32),
            ((192, 128), BF),
            ((4, 64, 128), F32),
            ((4, 288, 128), BF),
            ((96, 864), BF),
            ((192, 1728), BF),
            ((384, 576), BF),
        ]
        scratch = [
            ((16, 32, 256), BF),
            ((16, 288, 256), BF),
            ((16, 192, 256), F32),
            ((14, 64, 256), BF),
            ((8, 128), BF),
            ((7, 576, 128), BF),
            ((7, 384, 128), F32),
            ((5, 128, 128), BF),
            ((8, 1728, 128), BF),
            ((8, 192, 128), F32),
            ((6, 64, 384), BF),
            ((6, 64, 128), F32),
            ((12, 864, 384), BF),
            ((12, 96, 384), F32),
            ((10, 32, 384), BF),
            ((10, 288, 384), BF),
            ((10, 288, 384), F32),
            ((4, 64, 128), BF),
            ((4, 192, 128), BF),
            ((4, 576, 128), BF),
            ((4, 576, 128), F32),
        ]
        feat, dskip, packed, pre_one, taps_one, g_top, g_mid, g_bot = call(
            lambda *refs: main_kernel(sizes, scales, *refs),
            "main",
            outs,
            scratch,
            1,
            ids,
            own,
            up,
            down,
            far_up,
            far_down,
            forward_weight(w_encoder),
            forward_weight(w_bot),
            forward_weight(w_middle),
            forward_weight(w_upper),
            backward_weight(w_upper),
            backward_weight(w_middle),
            c["up_low"],
            c["sum_low"],
            c["up_mid"],
            c["sum_mid"],
            c["pool_low"],
        )

        from_left = shift(packed, "gy", ngy, 1)
        from_right = shift(packed, "gy", ngy, -1)
        line = jnp.stack([packed, from_left, from_right])
        line_up = shift(line, "gx", ngx, 1)
        line_down = shift(line, "gx", ngx, -1)
        low = line[:, 0:128]
        low_up = shift(low, "gx", ngx, 2)
        low_down = shift(low, "gx", ngx, -2)
        grad_skip, g_enc = call(
            lambda *refs: tail_kernel(sizes, scales[1], *refs),
            "tail",
            [((4, 32, 256), BF), ((192, 288), BF)],
            [
                ((5, 1152, 128), BF),
                ((5, 192, 128), F32),
                ((4, 64, 128), BF),
                ((4, 576, 128), BF),
                ((4, 96, 128), F32),
            ],
            1,
            ids,
            line,
            line_up,
            line_down,
            low_up,
            low_down,
            pre_one,
            taps_one,
            dskip,
            backward_weight(w_bot),
            backward_weight(w_encoder),
            c["up_low"],
            c["up_mid"],
        )

        grads = (g_top, g_mid, g_bot, g_enc)
        tiles = [tiles_of(g) for g in grads]
        count = sum(t.shape[0] for t in tiles)
        spare = -count % devices
        flat = jnp.concatenate(tiles + [jnp.zeros((spare, 8, 128), BF)], axis=0)
        parts = flat.reshape(devices, -1, 128)
        parts = lax.all_to_all(parts, ("gx", "gy"), split_axis=0, concat_axis=0, tiled=True)
        mine = parts.astype(F32).sum(axis=0).astype(BF)
        spread = jnp.broadcast_to(mine[None], (devices,) + mine.shape)
        spread = lax.all_to_all(spread, ("gx", "gy"), split_axis=0, concat_axis=0, tiled=True)
        spread = spread.reshape(-1, 8, 128)
        whole = []
        start = 0
        for g, t in zip(grads, tiles):
            whole.append(from_tiles(spread[start : start + t.shape[0]], *g.shape))
            start += t.shape[0]
        full_top, full_mid, full_bot, full_enc = whole
        block = w_bottom.shape[0]
        mine_bot = full_bot.reshape(3, ngx, block, -1)
        mine_bot = lax.dynamic_index_in_dim(mine_bot, gx, 1, keepdims=False)
        mine_bot = mine_bot.reshape(3 * block, -1)
        return (
            feat.transpose(1, 0, 2),
            grad_skip.transpose(1, 0, 2),
            full_gradient(full_enc),
            full_gradient(mine_bot),
            full_gradient(full_mid),
            full_gradient(full_top),
        )

    in_specs = (P(None, "gx", "gy"), P(), P("gx", None), P(), P(), P(None, "gx", "gy"))
    out_specs = (P(None, "gx", "gy"), P(None, "gx", "gy"), P(), P("gx", None), P(), P())
    return jax.shard_map(
        per_device, mesh=mesh, in_specs=in_specs, out_specs=out_specs, check_vma=False
    )
```

```python
import math

import jax
import jax.numpy as jnp
import numpy as np
from jax import lax
from jax.experimental import pallas as pl
from jax.experimental.pallas import tpu as pltpu
from jax.sharding import PartitionSpec as P


AXES = ("gx", "gy")
BF = jnp.bfloat16
F32 = jnp.float32


def columns(lanes, depth, split):
    col = np.arange(lanes) // depth
    return np.where(col >= split, col - lanes // depth, col), np.arange(lanes) % depth


def upsampling(coarse, fine):
    (col_c, z_c), (col_f, z_f) = (columns(*coarse), columns(*fine))
    hit = (col_c[:, None] == col_f[None, :] // 2) & (z_c[:, None] == z_f[None, :] // 2)
    return hit.astype(np.float32)


TOP = (384, 16, 20)
WIDE = (256, 8, 16)
MID = (128, 8, 12)
LOW = (128, 4, 16)


def constants():
    low_mid = upsampling(LOW, MID)
    mid_top = upsampling(MID, TOP)
    wide_low = upsampling(LOW, WIDE).T / 8.0
    tile_pool = mid_top[:64, :256].T / 8.0
    tile_pool = np.concatenate([tile_pool, tile_pool], axis=1)
    return {
        "up_low": low_mid,
        "sum_low": low_mid.T,
        "up_mid": mid_top,
        "sum_mid": mid_top.T,
        "pool_low": wide_low,
        "pool_tile": tile_pool,
    }


def dot(a, b):
    return jnp.dot(a, b, preferred_element_type=F32)


def dot_nt(a, b):
    return lax.dot_general(a, b, (((1,), (1,)), ((), ())), preferred_element_type=F32)


def dot_split(a, b):
    head = a.astype(BF)
    rest = (a - head.astype(F32)).astype(BF)
    return dot(head, b) + dot(rest, b)


def loop(count, body):
    def step(i, carry):
        body(i)
        return carry

    lax.fori_loop(0, count, step, 0)


def lane(length):
    return lax.broadcasted_iota(jnp.int32, (1, length), 1)


def inside(region, tile_cols, total_cols, index):
    lanes, depth, split = region
    col = lane(lanes) // depth
    col = jnp.where(col >= split, col - lanes // depth, col) + index * tile_cols
    return jnp.where((col >= 0) & (col < total_cols), 1.0, 0.0)


def row_ok(row, total):
    return jnp.where((row >= 0) & (row < total), 1.0, 0.0)


def depth_masks(shape, depth):
    z = lax.broadcasted_iota(jnp.int32, shape, 1) % depth
    below = jnp.where(z == depth - 1, 0.0, 1.0).astype(BF)
    above = jnp.where(z == 0, 0.0, 1.0).astype(BF)
    return below, above


def put_taps(dst, row, first, width, value, depth):
    chans, lanes = value.shape
    below, above = depth_masks(value.shape, depth)
    kinds = (value * below, value, value * above)
    for b in range(3):
        for e in range(3):
            shift = (b - 1) * depth + (e - 1)
            piece = kinds[e]
            if shift:
                piece = pltpu.roll(piece, (-shift) % lanes, 1)
            start = (3 * b + e) * width + first
            dst[row, start : start + chans, :] = piece


def sigmoid(v):
    return 1.0 / (1.0 + jnp.exp(-v))


def silu(v):
    return v * sigmoid(v)


def slope(v):
    s = sigmoid(v)
    return s * (1.0 + v * (1.0 - s))


def row_sum(ref, row, chans):
    return (
        ref[row, 0:chans, :]
        + ref[row + 1, chans : 2 * chans, :]
        + ref[row + 2, 2 * chans : 3 * chans, :]
    )


def put_padded(out, row, value):
    rows, width = value.shape
    out[row : row + rows, 0:width] = value.astype(BF)
    out[row : row + rows, width:] = jnp.zeros((rows, out.shape[1] - width), BF)


def pool_kernel(skip, cot, pool_tile, to_left, to_right):
    for r in range(4):
        to_left[r] = skip[r, :, 0:128]
        to_left[4 + r] = cot[r, :, 0:128]
        to_right[r] = skip[r, :, 128:256]
        to_right[4 + r] = cot[r, :, 128:256]
    for q in range(2):
        pooled = dot(skip[2 * q], pool_tile[...]) + dot(skip[2 * q + 1], pool_tile[...])
        pooled = pooled.astype(BF)
        to_left[8 + q] = pooled
        to_right[8 + q] = pooled


def widen_kernel(skip, cot, own, right, left, weight, out, spread):
    first = jnp.where(lax.broadcasted_iota(jnp.int32, (32, 128), 1) < 64, 1.0, 0.0)
    head = first.astype(BF)
    tail = (1.0 - first).astype(BF)
    for r in range(4):
        for k, tile in enumerate((skip, cot)):
            base = 12 * k + 3 * r
            out[base] = tile[r, :, 0:128]
            out[base + 1] = tile[r, :, 128:256]
            out[base + 2] = right[4 * k + r] * head + left[4 * k + r] * tail
    pieces = []
    for q in range(2):
        pieces.append(own[8 + q] * head + right[8 + q] * tail)
        pieces.append(left[8 + q] * tail)
    for p in range(spread.shape[0]):
        for q in range(4):
            spread[p, q] = pieces[q]
        for q in range(weight.shape[0]):
            spread[p, 4 + q] = weight[q]


def put_forward(w, out):
    rows = w.shape[0]
    width = out.shape[1]
    for a in range(3):
        out[rows * a : rows * a + rows, :] = w[:, a * width : (a + 1) * width]


def put_backward(w, out):
    chans = out.shape[0] // 3
    i = lax.broadcasted_iota(jnp.int32, (chans, chans), 0)
    j = lax.broadcasted_iota(jnp.int32, (chans, chans), 1)
    unit = jnp.where(i == j, 1.0, 0.0).astype(BF)
    for a in range(3):
        taps = [26 - 9 * a - k for k in range(9)]
        stacked = jnp.concatenate([w[:, t * chans : t * chans + chans] for t in taps], axis=0)
        out[chans * a : chans * a + chans, :] = dot_nt(unit, stacked).astype(BF)


def weight_kernel(forward, backward, *refs):
    sources, outs = refs[: len(forward)], refs[len(forward) :]
    k = 0
    for w, fwd, bwd in zip(sources, forward, backward):
        if fwd:
            put_forward(w, outs[k])
            k += 1
        if bwd:
            put_backward(w, outs[k])
            k += 1


def main_kernel(sizes, scales, *refs):
    (ids, own, up, down, pools) = refs[:5]
    (w_enc, w_bot, w_mid, w_top, t_top, t_mid) = refs[5:11]
    (up_low, sum_low, up_mid, sum_mid, pool_low) = refs[11:16]
    (feat, dskip, packed, pre_one, taps_out, g_top, g_mid, g_bot) = refs[16:24]
    (pool_s, taps_a, sum_a, act_a, taps_b, sum_b, act_b) = refs[24:31]
    (taps_c, sum_c, act_c, pre_c, taps_d, sum_d, err_d) = refs[31:38]
    (taps_e, sum_e, err_c, stack, taps_f, sum_f) = refs[38:44]
    (rows_all, cols_all) = sizes
    (scale_top, scale_mid, scale_low) = scales
    gx, gy = ids[0], ids[1]
    rows_mid, rows_low = rows_all // 2, rows_all // 4

    tiles = rows_all // 4
    for k in range(16):
        tile = gx + (k - 7) // 2
        keep = jnp.full((32, 128), row_ok(tile, tiles)).astype(BF)
        tile = jnp.clip(tile, 0, tiles - 1)
        slab = 2 * ((k - 7) % 2)
        pool_s[k, :, 0:128] = pools[tile, slab] * keep
        pool_s[k, :, 128:256] = pools[tile, slab + 1] * keep

    def enc_taps(k):
        put_taps(taps_a, k, 0, 32, pool_s[k], 8)
        sum_a[k] = dot(w_enc[...], taps_a[k])

    loop(16, enc_taps)
    wide_in = inside(WIDE, 8, cols_all // 2, gy)

    def enc_act(k):
        value = silu(row_sum(sum_a, k, 64)) * (wide_in * row_ok(gx * 2 + k - 6, rows_mid))
        act_a[k] = value.astype(BF)

    loop(14, enc_act)
    for m in range(4):
        pre = row_sum(sum_a, m + 5, 64)
        pre_one[m] = jnp.where(lane(128) < 96, pre[:, 0:128], pre[:, 128:256])
        taps_out[m] = taps_a[m + 6, :, 0:128]

    def low_taps(k):
        pooled = dot(act_a[2 * k], pool_low[...]) + dot(act_a[2 * k + 1], pool_low[...])
        put_taps(taps_b, k, 0, 64, pooled.astype(BF), 4)
        sum_b[k] = dot(w_bot[...], taps_b[k])

    loop(7, low_taps)
    low_in = inside(LOW, 4, cols_all // 4, gy)
    mid_in = inside(MID, 8, cols_all // 2, gy)
    pick = jnp.where(lax.broadcasted_iota(jnp.int32, (64, 128), 1) < 96, 1.0, 0.0)
    near = pick.astype(BF)
    away = (1.0 - pick).astype(BF)

    def low_act(k):
        value = silu(row_sum(sum_b, k, 128)) * (low_in * row_ok(gx + k - 2, rows_low))
        act_b[k] = dot(value.astype(BF), up_low[...]).astype(BF)

    loop(5, low_act)

    def mid_taps(k):
        put_taps(taps_c, k, 0, 192, act_b[(k + 1) // 2], 8)
        narrow = act_a[k + 3, :, 0:128] * near + act_a[k + 3, :, 128:256] * away
        put_taps(taps_c, k, 128, 192, narrow, 8)
        sum_c[k] = dot(w_mid[...], taps_c[k])

    loop(8, mid_taps)

    def mid_act(k):
        pre = row_sum(sum_c, k, 64)
        pre_c[k] = pre
        value = silu(pre) * (mid_in * row_ok(gx * 2 + k - 2, rows_mid))
        act_c[k] = dot(value.astype(BF), up_mid[...]).astype(BF)

    loop(6, mid_act)

    def skip_row(kind, k):
        part = (up, own, down)[k // 4]
        base = 12 * kind + 3 * (k % 4)
        return jnp.concatenate([part[base], part[base + 1], part[base + 2]], axis=1)

    for k in range(12):
        put_taps(taps_d, k, 64, 96, skip_row(0, k), 16)

    def top_taps(j):
        for half in range(2):
            put_taps(taps_d, 2 * j + half, 0, 96, act_c[j], 16)
            sum_d[2 * j + half] = dot(w_top[...], taps_d[2 * j + half])

    loop(6, top_taps)
    for k in range(10):
        pre = row_sum(sum_d, k, 32)
        s = sigmoid(pre)
        if 3 <= k < 7:
            feat[k - 3] = (pre * s)[:, 0:256].astype(BF)
        cot = skip_row(1, k + 1).astype(F32)
        err_d[k] = (cot * (s * (1.0 + pre * (1.0 - s)))).astype(BF)

    def top_back(k):
        put_taps(taps_e, k, 0, 32, err_d[k], 16)
        sum_e[k] = dot(t_top[...], taps_e[k])

    loop(10, top_back)

    total = None
    for k in range(6):
        parts = []
        for a in range(3):
            r = k - a
            own_row = 0 <= r < 4
            parts.append(err_d[r + 3, :, 0:256] if own_row else jnp.zeros((32, 256), BF))
        term = dot_nt(jnp.concatenate(parts, axis=0), taps_d[k + 3, :, 0:256])
        total = term if total is None else total + term
    put_padded(g_top, 0, total * scale_top)

    def mid_err(m):
        one = row_sum(sum_e, 2 * m, 96)
        two = row_sum(sum_e, 2 * m + 1, 96)
        whole = dot_split(one[0:64] + two[0:64], sum_mid[...])
        keep = mid_in * row_ok(gx * 2 + m - 1, rows_mid)
        err_c[m] = (whole * slope(pre_c[m + 1]) * keep).astype(BF)

    loop(4, mid_err)
    for r in range(4):
        dskip[r] = row_sum(sum_e, r + 2, 96)[64:96, 0:256]

    def mid_back(m):
        put_taps(taps_f, m, 0, 64, err_c[m], 8)
        sum_f[m] = dot(t_mid[...], taps_f[m])

    loop(4, mid_back)
    own_mid = jnp.where(lax.broadcasted_iota(jnp.int32, (64, 128), 1) < 64, 1.0, 0.0).astype(BF)
    for k in range(4):
        for a in range(3):
            r = k - a
            piece = err_c[r + 1] * own_mid if 0 <= r < 2 else jnp.zeros((64, 128), BF)
            stack[k, 64 * a : 64 * a + 64, :] = piece
    total = None
    for k in range(4):
        term = dot_nt(stack[k], taps_c[k + 2])
        total = term if total is None else total + term
    put_padded(g_mid, 0, total * scale_mid)

    one = row_sum(sum_f, 0, 192)
    two = row_sum(sum_f, 1, 192)
    whole = dot_split(one[0:128] + two[0:128], sum_low[...])
    keep = jnp.where(lane(128) < 16, 1.0, 0.0)
    err_low = (whole * slope(row_sum(sum_b, 2, 128)) * keep).astype(BF)
    packed[0:128, :] = err_low
    both = jnp.where(lane(128) < 64, one[128:192], pltpu.roll(two[128:192], 64, 1))
    packed[128:192, :] = both.astype(BF)
    for a in range(3):
        put_padded(g_bot, 128 * a, dot_nt(err_low, taps_b[a + 2]) * scale_low)


def tail_kernel(sizes, scale_mid, *refs):
    (ids, own, up, down, up_two, down_two, pre_one, taps_in, dskip) = refs[:9]
    (t_bot, t_enc, up_low, up_mid) = refs[9:13]
    (grad_skip, g_enc) = refs[13:15]
    (taps_a, sum_a, err_s, taps_b, sum_b) = refs[15:20]
    (rows_all, cols_all) = sizes
    gx, gy = ids[0], ids[1]
    rows_mid = rows_all // 2
    mid_in = inside(MID, 8, cols_all // 2, gy)

    for k, ref in enumerate((up_two, up, own, down, down_two)):
        value = (
            ref[0, 0:128, :].astype(F32)
            + pltpu.roll(ref[2, 0:128, :].astype(F32), 16, 1)
            + pltpu.roll(ref[1, 0:128, :].astype(F32), 112, 1)
        )
        put_taps(taps_a, k, 0, 128, value.astype(BF), 4)
        sum_a[k] = dot(t_bot[...], taps_a[k])
    ups = [dot_split(row_sum(sum_a, k, 64), up_low[...]) * 0.125 for k in range(3)]
    for m in range(4):
        ref = (up, own, own, down)[m]
        odd = m % 2 == 0
        tiles = [ref[k, 128:192, :].astype(F32) for k in range(3)]
        mine, left, right = tiles
        if odd:
            mine = pltpu.roll(mine, 64, 1)
        else:
            left, right = pltpu.roll(left, 64, 1), pltpu.roll(right, 64, 1)
        at = lane(128)
        part = jnp.where(at < 64, mine, jnp.where(at < 96, right, left))
        keep = mid_in * row_ok(gx * 2 + m - 1, rows_mid)
        err = (part + ups[(m + 1) // 2]) * slope(pre_one[m]) * keep
        err = err.astype(BF)
        err_s[m] = err
        put_taps(taps_b, m, 0, 64, err, 8)
        sum_b[m] = dot(t_enc[...], taps_b[m])
    own_mid = jnp.where(lax.broadcasted_iota(jnp.int32, (64, 128), 1) < 64, 1.0, 0.0).astype(BF)
    total = None
    for k in range(4):
        parts = []
        for a in range(3):
            r = k - a
            parts.append(err_s[r + 1] * own_mid if 0 <= r < 2 else jnp.zeros((64, 128), BF))
        term = dot_nt(jnp.concatenate(parts, axis=0), taps_in[k])
        total = term if total is None else total + term
    total = (total * scale_mid).astype(BF)
    g_enc[0:192, :] = total[:, 0:128]
    g_enc[192:384, :] = total[:, 128:256]
    rest = [total[48 * q : 48 * q + 48, 256:288] for q in range(4)]
    g_enc[384:432, :] = jnp.concatenate(rest, axis=1)
    if g_enc.shape[0] > 432:
        g_enc[432:, :] = jnp.zeros((g_enc.shape[0] - 432, 128), BF)
    for q in range(2):
        fine = dot_split(row_sum(sum_b, q, 32), up_mid[:, 0:256]) * 0.125
        for half in range(2):
            r = 2 * q + half
            grad_skip[r] = (dskip[r] + fine).astype(BF)


def finish_kernel(g, out):
    rest = jnp.concatenate([g[384:432, 32 * q : 32 * q + 32] for q in range(4)], axis=0)
    pieces = []
    for a in range(3):
        at = 64 * a
        pieces += [g[at : at + 64, :], g[192 + at : 256 + at, :], rest[at : at + 64, :]]
    out[...] = jnp.concatenate(pieces, axis=1).astype(F32)


VMEM = pl.BlockSpec(memory_space=pltpu.VMEM)
SMEM = pl.BlockSpec(memory_space=pltpu.SMEM)


def call(kernel, outs, scratch, scalars, *args, cost=1):
    return pl.pallas_call(
        kernel,
        out_shape=[jax.ShapeDtypeStruct(s, d) for s, d in outs],
        in_specs=[SMEM] * scalars + [VMEM] * (len(args) - scalars),
        out_specs=[VMEM] * len(outs),
        scratch_shapes=[pltpu.VMEM(s, d) for s, d in scratch],
        compiler_params=pltpu.CompilerParams(vmem_limit_bytes=56 * 1024 * 1024),
        cost_estimate=pl.CostEstimate(
            flops=cost * 500_000_000, bytes_accessed=cost * 1_000_000, transcendentals=0
        ),
    )(*args)


def shift(value, axis, count, step):
    return lax.ppermute(value, axis, [(i, i + step) for i in range(count) if 0 <= i + step < count])


def tiles_of(g):
    rows, width = g.shape
    return g.reshape(rows // 8, 8, width // 128, 128).transpose(0, 2, 1, 3).reshape(-1, 8, 128)


def from_tiles(tiles, rows, width):
    wide = -(-width // 128)
    g = tiles.reshape(rows // 8, wide, 8, 128).transpose(0, 2, 1, 3).reshape(rows, wide * 128)
    return g[:, :width]


def full_gradient(g):
    rows, _ = g.shape
    out = rows // 3
    return jnp.concatenate([g[out * a : out * a + out] for a in range(3)], axis=1).astype(F32)


def solution(mesh):
    ngx, ngy = mesh.shape["gx"], mesh.shape["gy"]
    devices = ngx * ngy
    const = {k: np.asarray(v) for k, v in constants().items()}

    def step(skip_input, w_encoder, w_bottom, w_middle, w_upper, cotangent):
        gx, gy = lax.axis_index("gx"), lax.axis_index("gy")
        ids = jnp.stack([gx, gy]).astype(jnp.int32)
        rows_all, cols_all = 4 * ngx, 16 * ngy
        sizes = (rows_all, cols_all)
        cells = rows_all * cols_all * 16
        scales = tuple(1.0 / math.sqrt(cells // k) for k in (1, 8, 64))
        c = {k: jnp.asarray(v, BF) for k, v in const.items()}

        block, width = w_bottom.shape
        slabs = block * 2048 // 4096
        weight = jnp.pad(w_bottom, ((0, 0), (0, 2048 - width)))
        lanes = weight.shape[1] // 128
        weight = weight.reshape(block, lanes, 128).transpose(1, 0, 2).reshape(slabs, 32, 128)

        skip = skip_input.transpose(1, 0, 2)
        cot = cotangent.transpose(1, 0, 2)
        to_left, to_right = call(
            pool_kernel, [((10, 32, 128), BF)] * 2, [], 0, skip, cot, c["pool_tile"]
        )
        right = shift(to_left, "gy", ngy, -1)
        left = shift(to_right, "gy", ngy, 1)
        own, spread = call(
            widen_kernel,
            [((24, 32, 128), BF), ((ngx, 4 + slabs, 32, 128), BF)],
            [],
            0,
            skip,
            cot,
            to_left,
            right,
            left,
            weight,
        )
        up = shift(own, "gx", ngx, 1)
        down = shift(own, "gx", ngx, -1)
        pools = lax.all_to_all(spread, "gx", split_axis=0, concat_axis=0, tiled=True)
        w_all = pools[:, 4:].reshape(ngx, lanes, block, 128).transpose(0, 2, 1, 3)
        w_all = w_all.reshape(ngx * block, lanes * 128)[:, :width]
        w_enc, t_enc, w_mid, t_mid, w_top, t_top = call(
            lambda *refs: weight_kernel((1, 1, 1), (1, 1, 1), *refs),
            [
                ((192, 288), BF),
                ((96, 576), BF),
                ((192, 1728), BF),
                ((576, 576), BF),
                ((96, 864), BF),
                ((288, 288), BF),
            ],
            [],
            0,
            w_encoder,
            w_middle,
            w_upper,
            cost=4,
        )
        w_bot, t_bot = call(
            lambda *refs: weight_kernel((1,), (1,), *refs),
            [((384, 576), BF), ((192, 1152), BF)],
            [],
            0,
            w_all,
            cost=2,
        )

        outs = [
            ((4, 32, 256), BF),
            ((4, 32, 256), F32),
            ((192, 128), BF),
            ((4, 64, 128), F32),
            ((4, 288, 128), BF),
            ((96, 896), BF),
            ((192, 1792), BF),
            ((384, 640), BF),
        ]
        scratch = [
            ((16, 32, 256), BF),
            ((16, 288, 256), BF),
            ((16, 192, 256), F32),
            ((14, 64, 256), BF),
            ((7, 576, 128), BF),
            ((7, 384, 128), F32),
            ((5, 128, 128), BF),
            ((8, 1728, 128), BF),
            ((8, 192, 128), F32),
            ((6, 64, 384), BF),
            ((6, 64, 128), F32),
            ((12, 864, 384), BF),
            ((12, 96, 384), F32),
            ((10, 32, 384), BF),
            ((10, 288, 384), BF),
            ((10, 288, 384), F32),
            ((4, 64, 128), BF),
            ((4, 192, 128), BF),
            ((4, 576, 128), BF),
            ((4, 576, 128), F32),
        ]
        feat, dskip, packed, pre_one, taps_one, g_top, g_mid, g_bot = call(
            lambda *refs: main_kernel(sizes, scales, *refs),
            outs,
            scratch,
            1,
            ids,
            own,
            up,
            down,
            pools,
            w_enc,
            w_bot,
            w_mid,
            w_top,
            t_top,
            t_mid,
            c["up_low"],
            c["sum_low"],
            c["up_mid"],
            c["sum_mid"],
            c["pool_low"],
            cost=20,
        )

        def scatter(pairs):
            pairs = lax.all_to_all(pairs, AXES, split_axis=0, concat_axis=0, tiled=True)
            pairs = pairs.reshape(devices, -1, 2, 128)
            return pairs.astype(F32).sum(axis=0).astype(BF)

        grads = ((g_top, 864), (g_mid, 1728), (g_bot, 576))
        tiles = [tiles_of(g) for g, _ in grads]
        used = 4 * sum(t.shape[0] for t in tiles)
        flat = [t.reshape(-1, 2, 128) for t in tiles]
        flat = jnp.concatenate(flat + [jnp.zeros((-used % devices, 2, 128), BF)], axis=0)
        mine_main = scatter(flat)

        from_left = shift(packed, "gy", ngy, 1)
        from_right = shift(packed, "gy", ngy, -1)
        line = jnp.stack([packed, from_left, from_right])
        line_up = shift(line, "gx", ngx, 1)
        line_down = shift(line, "gx", ngx, -1)
        low = line[:, 0:128]
        low_up = shift(low, "gx", ngx, 2)
        low_down = shift(low, "gx", ngx, -2)
        grad_skip, g_enc = call(
            lambda *refs: tail_kernel(sizes, scales[1], *refs),
            [((4, 32, 256), BF), ((432 + 2 * (-216 % devices), 128), BF)],
            [
                ((5, 1152, 128), BF),
                ((5, 192, 128), F32),
                ((4, 64, 128), BF),
                ((4, 576, 128), BF),
                ((4, 96, 128), F32),
            ],
            1,
            ids,
            line,
            line_up,
            line_down,
            low_up,
            low_down,
            pre_one,
            taps_one,
            dskip,
            t_bot,
            t_enc,
            c["up_low"],
            c["up_mid"],
            cost=4,
        )

        mine_enc = scatter(g_enc.reshape(-1, 2, 128))
        share = mine_main.shape[0]
        mine = jnp.concatenate([mine_main, mine_enc], axis=0)
        spread = jnp.broadcast_to(mine[None], (devices,) + mine.shape).reshape(-1, 2, 128)
        spread = lax.all_to_all(spread, AXES, split_axis=0, concat_axis=0, tiled=True)
        spread = spread.reshape(devices, -1, 2, 128)
        full_enc = spread[:, share:].reshape(-1, 128)
        whole = spread[:, :share].reshape(-1, 2, 128)[:used].reshape(-1, 8, 128)
        (full_enc,) = call(finish_kernel, [((64, 864), F32)], [], 0, full_enc)

        full = []
        start = 0
        for (g, width), t in zip(grads, tiles):
            full.append(from_tiles(whole[start : start + t.shape[0]], g.shape[0], width))
            start += t.shape[0]
        full_top, full_mid, full_bot = full
        mine_bot = full_bot.reshape(3, ngx, block, -1)
        mine_bot = lax.dynamic_index_in_dim(mine_bot, gx, 1, keepdims=False)
        mine_bot = mine_bot.reshape(3 * block, -1)
        return (
            feat.transpose(1, 0, 2),
            grad_skip.transpose(1, 0, 2),
            full_enc,
            full_gradient(mine_bot),
            full_gradient(full_mid),
            full_gradient(full_top),
        )

    in_specs = (P(None, "gx", "gy"), P(), P("gx", None), P(), P(), P(None, "gx", "gy"))
    out_specs = (P(None, "gx", "gy"), P(None, "gx", "gy"), P(), P("gx", None), P(), P())
    return jax.shard_map(step, mesh=mesh, in_specs=in_specs, out_specs=out_specs, check_vma=False)
```

```python
import math

import jax
import jax.numpy as jnp
import numpy as np
from jax import lax
from jax.experimental import pallas as pl
from jax.experimental.pallas import tpu as pltpu
from jax.sharding import PartitionSpec as P

AXES = ("gx", "gy")
BF = jnp.bfloat16
F32 = jnp.float32


def columns(lanes, depth, split):
    col = np.arange(lanes) // depth
    return np.where(col >= split, col - lanes // depth, col), np.arange(lanes) % depth


def upsampling(coarse, fine):
    (col_c, z_c), (col_f, z_f) = (columns(*coarse), columns(*fine))
    hit = (col_c[:, None] == col_f[None, :] // 2) & (z_c[:, None] == z_f[None, :] // 2)
    return hit.astype(np.float32)


TOP = (384, 16, 20)
WIDE = (256, 8, 16)
MID = (128, 8, 12)
LOW = (128, 4, 16)


def constants():
    low_mid = upsampling(LOW, MID)
    mid_top = upsampling(MID, TOP)
    wide_low = upsampling(LOW, WIDE).T / 8.0
    tile_pool = mid_top[:64, :256].T / 8.0
    tile_pool = np.concatenate([tile_pool, tile_pool], axis=1)
    return {
        "up_low": low_mid,
        "sum_low": low_mid.T,
        "up_mid": mid_top,
        "sum_mid": mid_top.T,
        "pool_low": wide_low,
        "pool_tile": tile_pool,
    }


def dot(a, b):
    return jnp.dot(a, b, preferred_element_type=F32)


def dot_nt(a, b):
    return lax.dot_general(a, b, (((1,), (1,)), ((), ())), preferred_element_type=F32)


def dot_split(a, b):
    head = a.astype(BF)
    rest = (a - head.astype(F32)).astype(BF)
    return dot(head, b) + dot(rest, b)


def loop(count, body):
    def step(i, carry):
        body(i)
        return carry

    lax.fori_loop(0, count, step, 0)


def lane(length):
    return lax.broadcasted_iota(jnp.int32, (1, length), 1)


def inside(region, tile_cols, total_cols, index):
    lanes, depth, split = region
    col = lane(lanes) // depth
    col = jnp.where(col >= split, col - lanes // depth, col) + index * tile_cols
    return jnp.where((col >= 0) & (col < total_cols), 1.0, 0.0)


def row_ok(row, total):
    return jnp.where((row >= 0) & (row < total), 1.0, 0.0)


def depth_masks(shape, depth):
    z = lax.broadcasted_iota(jnp.int32, shape, 1) % depth
    below = jnp.where(z == depth - 1, 0.0, 1.0).astype(BF)
    above = jnp.where(z == 0, 0.0, 1.0).astype(BF)
    return below, above


def put_taps(dst, row, first, width, value, depth):
    chans, lanes = value.shape
    below, above = depth_masks(value.shape, depth)
    kinds = (value * below, value, value * above)
    for b in range(3):
        for e in range(3):
            shift = (b - 1) * depth + (e - 1)
            piece = kinds[e]
            if shift:
                piece = pltpu.roll(piece, (-shift) % lanes, 1)
            start = (3 * b + e) * width + first
            dst[row, start : start + chans, :] = piece


def sigmoid(v):
    return 1.0 / (1.0 + jnp.exp(-v))


def silu(v):
    return v * sigmoid(v)


def slope(v):
    s = sigmoid(v)
    return s * (1.0 + v * (1.0 - s))


def row_sum(ref, row, chans):
    return (
        ref[row, 0:chans, :]
        + ref[row + 1, chans : 2 * chans, :]
        + ref[row + 2, 2 * chans : 3 * chans, :]
    )


def put_padded(out, row, value):
    rows, width = value.shape
    out[row : row + rows, 0:width] = value.astype(BF)
    out[row : row + rows, width:] = jnp.zeros((rows, out.shape[1] - width), BF)


def pool_kernel(skip, cot, pool_tile, to_left, to_right):
    for r in range(4):
        to_left[r] = skip[r, :, 0:128]
        to_left[4 + r] = cot[r, :, 0:128]
        to_right[r] = skip[r, :, 128:256]
        to_right[4 + r] = cot[r, :, 128:256]
    for q in range(2):
        pooled = dot(skip[2 * q], pool_tile[...]) + dot(skip[2 * q + 1], pool_tile[...])
        pooled = pooled.astype(BF)
        to_left[8 + q] = pooled
        to_right[8 + q] = pooled


def widen_kernel(skip, cot, own, right, left, weight, out, spread):
    first = jnp.where(lax.broadcasted_iota(jnp.int32, (32, 128), 1) < 64, 1.0, 0.0)
    head = first.astype(BF)
    tail = (1.0 - first).astype(BF)
    for r in range(4):
        for k, tile in enumerate((skip, cot)):
            base = 12 * k + 3 * r
            out[base] = tile[r, :, 0:128]
            out[base + 1] = tile[r, :, 128:256]
            out[base + 2] = right[4 * k + r] * head + left[4 * k + r] * tail
    pieces = []
    for q in range(2):
        pieces.append(own[8 + q] * head + right[8 + q] * tail)
        pieces.append(left[8 + q] * tail)
    for p in range(spread.shape[0]):
        for q in range(4):
            spread[p, q] = pieces[q]
        for q in range(weight.shape[0]):
            spread[p, 4 + q] = weight[q]


def put_forward(w, out):
    rows = w.shape[0]
    width = out.shape[1]
    for a in range(3):
        out[rows * a : rows * a + rows, :] = w[:, a * width : (a + 1) * width]


def put_backward(w, out):
    chans = out.shape[0] // 3
    i = lax.broadcasted_iota(jnp.int32, (chans, chans), 0)
    j = lax.broadcasted_iota(jnp.int32, (chans, chans), 1)
    unit = jnp.where(i == j, 1.0, 0.0).astype(BF)
    for a in range(3):
        taps = [26 - 9 * a - k for k in range(9)]
        stacked = jnp.concatenate([w[:, t * chans : t * chans + chans] for t in taps], axis=0)
        out[chans * a : chans * a + chans, :] = dot_nt(unit, stacked).astype(BF)


def weight_kernel(forward, backward, *refs):
    sources, outs = refs[: len(forward)], refs[len(forward) :]
    k = 0
    for w, fwd, bwd in zip(sources, forward, backward):
        if fwd:
            put_forward(w, outs[k])
            k += 1
        if bwd:
            put_backward(w, outs[k])
            k += 1


def main_kernel(sizes, scales, *refs):
    (ids, own, up, down, pools) = refs[:5]
    (w_enc, w_bot, w_mid, w_top, t_top, t_mid) = refs[5:11]
    (up_low, sum_low, up_mid, sum_mid, pool_low) = refs[11:16]
    (feat, dskip, packed, pre_one, taps_out, g_top, g_mid, g_bot) = refs[16:24]
    (pool_s, taps_a, sum_a, act_a, taps_b, sum_b, act_b) = refs[24:31]
    (taps_c, sum_c, act_c, pre_c, taps_d, sum_d, err_d) = refs[31:38]
    (taps_e, sum_e, err_c, stack, taps_f, sum_f) = refs[38:44]
    (rows_all, cols_all) = sizes
    (scale_top, scale_mid, scale_low) = scales
    gx, gy = ids[0], ids[1]
    rows_mid, rows_low = rows_all // 2, rows_all // 4

    tiles = rows_all // 4
    for k in range(16):
        tile = gx + (k - 7) // 2
        keep = jnp.full((32, 128), row_ok(tile, tiles)).astype(BF)
        tile = jnp.clip(tile, 0, tiles - 1)
        slab = 2 * ((k - 7) % 2)
        pool_s[k, :, 0:128] = pools[tile, slab] * keep
        pool_s[k, :, 128:256] = pools[tile, slab + 1] * keep

    def enc_taps(k):
        put_taps(taps_a, k, 0, 32, pool_s[k], 8)
        sum_a[k] = dot(w_enc[...], taps_a[k])

    loop(16, enc_taps)
    wide_in = inside(WIDE, 8, cols_all // 2, gy)

    def enc_act(k):
        value = silu(row_sum(sum_a, k, 64)) * (wide_in * row_ok(gx * 2 + k - 6, rows_mid))
        act_a[k] = value.astype(BF)

    loop(14, enc_act)
    for m in range(4):
        pre = row_sum(sum_a, m + 5, 64)
        pre_one[m] = jnp.where(lane(128) < 96, pre[:, 0:128], pre[:, 128:256])
        taps_out[m] = taps_a[m + 6, :, 0:128]

    def low_taps(k):
        pooled = dot(act_a[2 * k], pool_low[...]) + dot(act_a[2 * k + 1], pool_low[...])
        put_taps(taps_b, k, 0, 64, pooled.astype(BF), 4)
        sum_b[k] = dot(w_bot[...], taps_b[k])

    loop(7, low_taps)
    low_in = inside(LOW, 4, cols_all // 4, gy)
    mid_in = inside(MID, 8, cols_all // 2, gy)
    pick = jnp.where(lax.broadcasted_iota(jnp.int32, (64, 128), 1) < 96, 1.0, 0.0)
    near = pick.astype(BF)
    away = (1.0 - pick).astype(BF)

    def low_act(k):
        value = silu(row_sum(sum_b, k, 128)) * (low_in * row_ok(gx + k - 2, rows_low))
        act_b[k] = dot(value.astype(BF), up_low[...]).astype(BF)

    loop(5, low_act)

    def mid_taps(k):
        put_taps(taps_c, k, 0, 192, act_b[(k + 1) // 2], 8)
        narrow = act_a[k + 3, :, 0:128] * near + act_a[k + 3, :, 128:256] * away
        put_taps(taps_c, k, 128, 192, narrow, 8)
        sum_c[k] = dot(w_mid[...], taps_c[k])

    loop(8, mid_taps)

    def mid_act(k):
        pre = row_sum(sum_c, k, 64)
        pre_c[k] = pre
        value = silu(pre) * (mid_in * row_ok(gx * 2 + k - 2, rows_mid))
        act_c[k] = dot(value.astype(BF), up_mid[...]).astype(BF)

    loop(6, mid_act)

    def skip_row(kind, k):
        part = (up, own, down)[k // 4]
        base = 12 * kind + 3 * (k % 4)
        return jnp.concatenate([part[base], part[base + 1], part[base + 2]], axis=1)

    for k in range(12):
        put_taps(taps_d, k, 64, 96, skip_row(0, k), 16)

    def top_taps(j):
        for half in range(2):
            put_taps(taps_d, 2 * j + half, 0, 96, act_c[j], 16)
            sum_d[2 * j + half] = dot(w_top[...], taps_d[2 * j + half])

    loop(6, top_taps)
    for k in range(10):
        pre = row_sum(sum_d, k, 32)
        s = sigmoid(pre)
        if 3 <= k < 7:
            feat[k - 3] = (pre * s)[:, 0:256].astype(BF)
        cot = skip_row(1, k + 1).astype(F32)
        err_d[k] = (cot * (s * (1.0 + pre * (1.0 - s)))).astype(BF)

    def top_back(k):
        put_taps(taps_e, k, 0, 32, err_d[k], 16)
        sum_e[k] = dot(t_top[...], taps_e[k])

    loop(10, top_back)

    total = None
    for k in range(6):
        parts = []
        for a in range(3):
            r = k - a
            own_row = 0 <= r < 4
            parts.append(err_d[r + 3, :, 0:256] if own_row else jnp.zeros((32, 256), BF))
        term = dot_nt(jnp.concatenate(parts, axis=0), taps_d[k + 3, :, 0:256])
        total = term if total is None else total + term
    put_padded(g_top, 0, total * scale_top)

    def mid_err(m):
        one = row_sum(sum_e, 2 * m, 96)
        two = row_sum(sum_e, 2 * m + 1, 96)
        whole = dot_split(one[0:64] + two[0:64], sum_mid[...])
        keep = mid_in * row_ok(gx * 2 + m - 1, rows_mid)
        err_c[m] = (whole * slope(pre_c[m + 1]) * keep).astype(BF)

    loop(4, mid_err)
    for r in range(4):
        dskip[r] = row_sum(sum_e, r + 2, 96)[64:96, 0:256]

    def mid_back(m):
        put_taps(taps_f, m, 0, 64, err_c[m], 8)
        sum_f[m] = dot(t_mid[...], taps_f[m])

    loop(4, mid_back)
    own_mid = jnp.where(lax.broadcasted_iota(jnp.int32, (64, 128), 1) < 64, 1.0, 0.0).astype(BF)
    for k in range(4):
        for a in range(3):
            r = k - a
            piece = err_c[r + 1] * own_mid if 0 <= r < 2 else jnp.zeros((64, 128), BF)
            stack[k, 64 * a : 64 * a + 64, :] = piece
    total = None
    for k in range(4):
        term = dot_nt(stack[k], taps_c[k + 2])
        total = term if total is None else total + term
    put_padded(g_mid, 0, total * scale_mid)

    one = row_sum(sum_f, 0, 192)
    two = row_sum(sum_f, 1, 192)
    whole = dot_split(one[0:128] + two[0:128], sum_low[...])
    keep = jnp.where(lane(128) < 16, 1.0, 0.0)
    err_low = (whole * slope(row_sum(sum_b, 2, 128)) * keep).astype(BF)
    packed[0:128, :] = err_low
    both = jnp.where(lane(128) < 64, one[128:192], pltpu.roll(two[128:192], 64, 1))
    packed[128:192, :] = both.astype(BF)
    for a in range(3):
        put_padded(g_bot, 128 * a, dot_nt(err_low, taps_b[a + 2]) * scale_low)


def tail_kernel(sizes, scale_mid, *refs):
    (ids, own, up, down, up_two, down_two, pre_one, taps_in, dskip) = refs[:9]
    (t_bot, t_enc, up_low, up_mid) = refs[9:13]
    (grad_skip, g_enc) = refs[13:15]
    (taps_a, sum_a, err_s, taps_b, sum_b) = refs[15:20]
    (rows_all, cols_all) = sizes
    gx, gy = ids[0], ids[1]
    rows_mid = rows_all // 2
    mid_in = inside(MID, 8, cols_all // 2, gy)

    for k, ref in enumerate((up_two, up, own, down, down_two)):
        value = (
            ref[0, 0:128, :].astype(F32)
            + pltpu.roll(ref[2, 0:128, :].astype(F32), 16, 1)
            + pltpu.roll(ref[1, 0:128, :].astype(F32), 112, 1)
        )
        put_taps(taps_a, k, 0, 128, value.astype(BF), 4)
        sum_a[k] = dot(t_bot[...], taps_a[k])
    ups = [dot_split(row_sum(sum_a, k, 64), up_low[...]) * 0.125 for k in range(3)]
    for m in range(4):
        ref = (up, own, own, down)[m]
        odd = m % 2 == 0
        tiles = [ref[k, 128:192, :].astype(F32) for k in range(3)]
        mine, left, right = tiles
        if odd:
            mine = pltpu.roll(mine, 64, 1)
        else:
            left, right = pltpu.roll(left, 64, 1), pltpu.roll(right, 64, 1)
        at = lane(128)
        part = jnp.where(at < 64, mine, jnp.where(at < 96, right, left))
        keep = mid_in * row_ok(gx * 2 + m - 1, rows_mid)
        err = (part + ups[(m + 1) // 2]) * slope(pre_one[m]) * keep
        err = err.astype(BF)
        err_s[m] = err
        put_taps(taps_b, m, 0, 64, err, 8)
        sum_b[m] = dot(t_enc[...], taps_b[m])
    own_mid = jnp.where(lax.broadcasted_iota(jnp.int32, (64, 128), 1) < 64, 1.0, 0.0).astype(BF)
    total = None
    for k in range(4):
        parts = []
        for a in range(3):
            r = k - a
            parts.append(err_s[r + 1] * own_mid if 0 <= r < 2 else jnp.zeros((64, 128), BF))
        term = dot_nt(jnp.concatenate(parts, axis=0), taps_in[k])
        total = term if total is None else total + term
    total = (total * scale_mid).astype(BF)
    g_enc[0:192, :] = total[:, 0:128]
    g_enc[192:384, :] = total[:, 128:256]
    rest = [total[48 * q : 48 * q + 48, 256:288] for q in range(4)]
    g_enc[384:432, :] = jnp.concatenate(rest, axis=1)
    for q in range(2):
        fine = dot_split(row_sum(sum_b, q, 32), up_mid[:, 0:256]) * 0.125
        for half in range(2):
            r = 2 * q + half
            grad_skip[r] = (dskip[r] + fine).astype(BF)


def finish_kernel(g, out):
    rest = jnp.concatenate([g[384:432, 32 * q : 32 * q + 32] for q in range(4)], axis=0)
    pieces = []
    for a in range(3):
        at = 64 * a
        pieces += [g[at : at + 64, :], g[192 + at : 256 + at, :], rest[at : at + 64, :]]
    out[...] = jnp.concatenate(pieces, axis=1).astype(F32)


VMEM = pl.BlockSpec(memory_space=pltpu.VMEM)
SMEM = pl.BlockSpec(memory_space=pltpu.SMEM)


def call(kernel, outs, scratch, scalars, *args, cost=1):
    return pl.pallas_call(
        kernel,
        out_shape=[jax.ShapeDtypeStruct(s, d) for s, d in outs],
        in_specs=[SMEM] * scalars + [VMEM] * (len(args) - scalars),
        out_specs=[VMEM] * len(outs),
        scratch_shapes=[pltpu.VMEM(s, d) for s, d in scratch],
        compiler_params=pltpu.CompilerParams(vmem_limit_bytes=56 * 1024 * 1024),
        cost_estimate=pl.CostEstimate(
            flops=cost * 500_000_000, bytes_accessed=cost * 1_000_000, transcendentals=0
        ),
    )(*args)


def shift(value, axis, count, step):
    return lax.ppermute(value, axis, [(i, i + step) for i in range(count) if 0 <= i + step < count])


def tiles_of(g):
    rows, width = g.shape
    return g.reshape(rows // 8, 8, width // 128, 128).transpose(0, 2, 1, 3).reshape(-1, 8, 128)


def from_tiles(tiles, rows, width):
    wide = -(-width // 128)
    g = tiles.reshape(rows // 8, wide, 8, 128).transpose(0, 2, 1, 3).reshape(rows, wide * 128)
    return g[:, :width]


def full_gradient(g):
    rows, _ = g.shape
    out = rows // 3
    return jnp.concatenate([g[out * a : out * a + out] for a in range(3)], axis=1).astype(F32)


def solution(mesh):
    ngx, ngy = mesh.shape["gx"], mesh.shape["gy"]
    devices = ngx * ngy
    const = {k: np.asarray(v) for k, v in constants().items()}

    def step(skip_input, w_encoder, w_bottom, w_middle, w_upper, cotangent):
        gx, gy = lax.axis_index("gx"), lax.axis_index("gy")
        ids = jnp.stack([gx, gy]).astype(jnp.int32)
        rows_all, cols_all = 4 * ngx, 16 * ngy
        sizes = (rows_all, cols_all)
        cells = rows_all * cols_all * 16
        scales = tuple(1.0 / math.sqrt(cells // k) for k in (1, 8, 64))
        c = {k: jnp.asarray(v, BF) for k, v in const.items()}

        block, width = w_bottom.shape
        slabs = block * 2048 // 4096
        weight = jnp.pad(w_bottom, ((0, 0), (0, 2048 - width)))
        lanes = weight.shape[1] // 128
        weight = weight.reshape(block, lanes, 128).transpose(1, 0, 2).reshape(slabs, 32, 128)

        skip = skip_input.transpose(1, 0, 2)
        cot = cotangent.transpose(1, 0, 2)
        to_left, to_right = call(
            pool_kernel, [((10, 32, 128), BF)] * 2, [], 0, skip, cot, c["pool_tile"]
        )
        right = shift(to_left, "gy", ngy, -1)
        left = shift(to_right, "gy", ngy, 1)
        own, spread = call(
            widen_kernel,
            [((24, 32, 128), BF), ((ngx, 4 + slabs, 32, 128), BF)],
            [],
            0,
            skip,
            cot,
            to_left,
            right,
            left,
            weight,
        )
        up = shift(own, "gx", ngx, 1)
        down = shift(own, "gx", ngx, -1)
        pools = lax.all_to_all(spread, "gx", split_axis=0, concat_axis=0, tiled=True)
        w_all = pools[:, 4:].reshape(ngx, lanes, block, 128).transpose(0, 2, 1, 3)
        w_all = w_all.reshape(ngx * block, lanes * 128)[:, :width]
        w_enc, t_enc, w_mid, t_mid, w_top, t_top = call(
            lambda *refs: weight_kernel((1, 1, 1), (1, 1, 1), *refs),
            [
                ((192, 288), BF),
                ((96, 576), BF),
                ((192, 1728), BF),
                ((576, 576), BF),
                ((96, 864), BF),
                ((288, 288), BF),
            ],
            [],
            0,
            w_encoder,
            w_middle,
            w_upper,
            cost=4,
        )
        w_bot, t_bot = call(
            lambda *refs: weight_kernel((1,), (1,), *refs),
            [((384, 576), BF), ((192, 1152), BF)],
            [],
            0,
            w_all,
            cost=2,
        )

        outs = [
            ((4, 32, 256), BF),
            ((4, 32, 256), F32),
            ((192, 128), BF),
            ((4, 64, 128), F32),
            ((4, 288, 128), BF),
            ((96, 896), BF),
            ((192, 1792), BF),
            ((384, 640), BF),
        ]
        scratch = [
            ((16, 32, 256), BF),
            ((16, 288, 256), BF),
            ((16, 192, 256), F32),
            ((14, 64, 256), BF),
            ((7, 576, 128), BF),
            ((7, 384, 128), F32),
            ((5, 128, 128), BF),
            ((8, 1728, 128), BF),
            ((8, 192, 128), F32),
            ((6, 64, 384), BF),
            ((6, 64, 128), F32),
            ((12, 864, 384), BF),
            ((12, 96, 384), F32),
            ((10, 32, 384), BF),
            ((10, 288, 384), BF),
            ((10, 288, 384), F32),
            ((4, 64, 128), BF),
            ((4, 192, 128), BF),
            ((4, 576, 128), BF),
            ((4, 576, 128), F32),
        ]
        feat, dskip, packed, pre_one, taps_one, g_top, g_mid, g_bot = call(
            lambda *refs: main_kernel(sizes, scales, *refs),
            outs,
            scratch,
            1,
            ids,
            own,
            up,
            down,
            pools,
            w_enc,
            w_bot,
            w_mid,
            w_top,
            t_top,
            t_mid,
            c["up_low"],
            c["sum_low"],
            c["up_mid"],
            c["sum_mid"],
            c["pool_low"],
            cost=20,
        )

        from_left = shift(packed, "gy", ngy, 1)
        from_right = shift(packed, "gy", ngy, -1)
        line = jnp.stack([packed, from_left, from_right])
        line_up = shift(line, "gx", ngx, 1)
        line_down = shift(line, "gx", ngx, -1)
        low = line[:, 0:128]
        low_up = shift(low, "gx", ngx, 2)
        low_down = shift(low, "gx", ngx, -2)
        grad_skip, g_enc = call(
            lambda *refs: tail_kernel(sizes, scales[1], *refs),
            [((4, 32, 256), BF), ((432, 128), BF)],
            [
                ((5, 1152, 128), BF),
                ((5, 192, 128), F32),
                ((4, 64, 128), BF),
                ((4, 576, 128), BF),
                ((4, 96, 128), F32),
            ],
            1,
            ids,
            line,
            line_up,
            line_down,
            low_up,
            low_down,
            pre_one,
            taps_one,
            dskip,
            t_bot,
            t_enc,
            c["up_low"],
            c["up_mid"],
            cost=4,
        )

        grads = ((g_top, 864), (g_mid, 1728), (g_bot, 576), (g_enc, 128))
        tiles = [tiles_of(g) for g, _ in grads]
        spare = -sum(t.shape[0] for t in tiles) % devices
        flat = jnp.concatenate(tiles + [jnp.zeros((spare, 8, 128), BF)], axis=0)
        half = flat.shape[0] // 2
        core = gx % 2
        swap = [(i, i ^ 1) for i in range(ngx)]
        keep = lax.dynamic_slice_in_dim(flat, core * half, half, 0)
        other = lax.dynamic_slice_in_dim(flat, (1 - core) * half, half, 0)
        other = lax.ppermute(other, "gx", swap)
        mine = (keep.astype(F32) + other.astype(F32)).astype(BF)
        parts = mine.reshape(devices // 2, -1, 128)
        groups = [[i for i in range(devices) if i // ngy % 2 == k] for k in range(2)]
        parts = lax.all_to_all(
            parts, AXES, split_axis=0, concat_axis=0, axis_index_groups=groups, tiled=True
        )
        total = parts.astype(F32).sum(axis=0).astype(BF)
        spread = jnp.broadcast_to(total[None], parts.shape)
        spread = lax.all_to_all(
            spread, AXES, split_axis=0, concat_axis=0, axis_index_groups=groups, tiled=True
        )
        mine = spread.reshape(half, 8, 128)
        other = lax.ppermute(mine, "gx", swap)
        first = jnp.where(core == 0, mine, other)
        second = jnp.where(core == 0, other, mine)
        whole = jnp.concatenate([first, second], axis=0)

        full = []
        start = 0
        for (g, width), t in zip(grads, tiles):
            full.append(from_tiles(whole[start : start + t.shape[0]], g.shape[0], width))
            start += t.shape[0]
        full_top, full_mid, full_bot, full_enc = full
        (full_enc,) = call(finish_kernel, [((64, 864), F32)], [], 0, full_enc)
        mine_bot = full_bot.reshape(3, ngx, block, -1)
        mine_bot = lax.dynamic_index_in_dim(mine_bot, gx, 1, keepdims=False)
        mine_bot = mine_bot.reshape(3 * block, -1)
        return (
            feat.transpose(1, 0, 2),
            grad_skip.transpose(1, 0, 2),
            full_enc,
            full_gradient(mine_bot),
            full_gradient(full_mid),
            full_gradient(full_top),
        )

    in_specs = (P(None, "gx", "gy"), P(), P("gx", None), P(), P(), P(None, "gx", "gy"))
    out_specs = (P(None, "gx", "gy"), P(None, "gx", "gy"), P(), P("gx", None), P(), P())
    return jax.shard_map(step, mesh=mesh, in_specs=in_specs, out_specs=out_specs, check_vma=False)
```

```python
import math

import jax
import jax.numpy as jnp
import numpy as np
from jax import lax
from jax.experimental import pallas as pl
from jax.experimental.pallas import tpu as pltpu
from jax.sharding import PartitionSpec as P

AXES = ("gx", "gy")
BF = jnp.bfloat16
F32 = jnp.float32


def columns(lanes, depth, split):
    col = np.arange(lanes) // depth
    return np.where(col >= split, col - lanes // depth, col), np.arange(lanes) % depth


def upsampling(coarse, fine):
    (col_c, z_c), (col_f, z_f) = (columns(*coarse), columns(*fine))
    hit = (col_c[:, None] == col_f[None, :] // 2) & (z_c[:, None] == z_f[None, :] // 2)
    return hit.astype(np.float32)


TOP = (384, 16, 20)
WIDE = (256, 8, 16)
MID = (128, 8, 12)
LOW = (128, 4, 16)


def constants():
    low_mid = upsampling(LOW, MID)
    mid_top = upsampling(MID, TOP)
    wide_low = upsampling(LOW, WIDE).T / 8.0
    tile_pool = mid_top[:64, :256].T / 8.0
    tile_pool = np.concatenate([tile_pool, tile_pool], axis=1)
    return {
        "up_low": low_mid,
        "sum_low": low_mid.T,
        "up_mid": mid_top,
        "sum_mid": mid_top.T,
        "pool_low": wide_low,
        "pool_tile": tile_pool,
    }


def dot(a, b):
    return jnp.dot(a, b, preferred_element_type=F32)


def dot_nt(a, b):
    return lax.dot_general(a, b, (((1,), (1,)), ((), ())), preferred_element_type=F32)


def dot_split(a, b):
    head = a.astype(BF)
    rest = (a - head.astype(F32)).astype(BF)
    return dot(head, b) + dot(rest, b)


def loop(count, body, unroll=1):
    def step(i, carry):
        for u in range(unroll):
            body(i * unroll + u)
        return carry

    if unroll == count:
        step(0, 0)
    else:
        lax.fori_loop(0, count // unroll, step, 0)


def lane(length):
    return lax.broadcasted_iota(jnp.int32, (1, length), 1)


def inside(region, tile_cols, total_cols, index):
    lanes, depth, split = region
    col = lane(lanes) // depth
    col = jnp.where(col >= split, col - lanes // depth, col) + index * tile_cols
    return jnp.where((col >= 0) & (col < total_cols), 1.0, 0.0)


def row_ok(row, total):
    return jnp.where((row >= 0) & (row < total), 1.0, 0.0)


def depth_masks(shape, depth):
    z = lax.broadcasted_iota(jnp.int32, shape, 1) % depth
    below = jnp.where(z == depth - 1, 0.0, 1.0).astype(BF)
    above = jnp.where(z == 0, 0.0, 1.0).astype(BF)
    return below, above


def put_taps(dst, row, first, width, value, depth):
    chans, lanes = value.shape
    below, above = depth_masks(value.shape, depth)
    kinds = (value * below, value, value * above)
    for b in range(3):
        for e in range(3):
            shift = (b - 1) * depth + (e - 1)
            piece = kinds[e]
            if shift:
                piece = pltpu.roll(piece, (-shift) % lanes, 1)
            start = (3 * b + e) * width + first
            dst[row, start : start + chans, :] = piece


def sigmoid(v):
    return 1.0 / (1.0 + jnp.exp(-v))


def silu(v):
    return v * sigmoid(v)


def slope(v):
    s = sigmoid(v)
    return s * (1.0 + v * (1.0 - s))


def row_sum(ref, row, chans):
    return (
        ref[row, 0:chans, :]
        + ref[row + 1, chans : 2 * chans, :]
        + ref[row + 2, 2 * chans : 3 * chans, :]
    )


def put_padded(out, row, value):
    rows, width = value.shape
    out[row : row + rows, 0:width] = value.astype(BF)
    out[row : row + rows, width:] = jnp.zeros((rows, out.shape[1] - width), BF)


def pool_kernel(skip, cot, pool_tile, to_left, to_right):
    for r in range(4):
        to_left[r] = skip[r, :, 0:128]
        to_left[4 + r] = cot[r, :, 0:128]
        to_right[r] = skip[r, :, 128:256]
        to_right[4 + r] = cot[r, :, 128:256]
    for q in range(2):
        pooled = dot(skip[2 * q], pool_tile[...]) + dot(skip[2 * q + 1], pool_tile[...])
        pooled = pooled.astype(BF)
        to_left[8 + q] = pooled
        to_right[8 + q] = pooled


def widen_kernel(skip, cot, own, right, left, weight, out, spread):
    first = jnp.where(lax.broadcasted_iota(jnp.int32, (32, 128), 1) < 64, 1.0, 0.0)
    head = first.astype(BF)
    tail = (1.0 - first).astype(BF)
    for r in range(4):
        for k, tile in enumerate((skip, cot)):
            base = 12 * k + 3 * r
            out[base] = tile[r, :, 0:128]
            out[base + 1] = tile[r, :, 128:256]
            out[base + 2] = right[4 * k + r] * head + left[4 * k + r] * tail
    pieces = []
    for q in range(2):
        pieces.append(own[8 + q] * head + right[8 + q] * tail)
        pieces.append(left[8 + q] * tail)
    for p in range(spread.shape[0]):
        for q in range(4):
            spread[p, q] = pieces[q]
        for q in range(weight.shape[0]):
            spread[p, 4 + q] = weight[q]


def put_forward(w, out):
    rows = w.shape[0]
    width = out.shape[1]
    for a in range(3):
        out[rows * a : rows * a + rows, :] = w[:, a * width : (a + 1) * width]


def put_backward(w, out):
    chans = out.shape[0] // 3
    i = lax.broadcasted_iota(jnp.int32, (chans, chans), 0)
    j = lax.broadcasted_iota(jnp.int32, (chans, chans), 1)
    unit = jnp.where(i == j, 1.0, 0.0).astype(BF)
    for a in range(3):
        taps = [26 - 9 * a - k for k in range(9)]
        stacked = jnp.concatenate([w[:, t * chans : t * chans + chans] for t in taps], axis=0)
        out[chans * a : chans * a + chans, :] = dot_nt(unit, stacked).astype(BF)


def weight_kernel(forward, backward, *refs):
    sources, outs = refs[: len(forward)], refs[len(forward) :]
    k = 0
    for w, fwd, bwd in zip(sources, forward, backward):
        if fwd:
            put_forward(w, outs[k])
            k += 1
        if bwd:
            put_backward(w, outs[k])
            k += 1


def main_kernel(sizes, scales, *refs):
    (ids, own, up, down, pools) = refs[:5]
    (w_enc, w_bot, w_mid, w_top, t_top, t_mid) = refs[5:11]
    (up_low, sum_low, up_mid, sum_mid, pool_low) = refs[11:16]
    (feat, dskip, packed, pre_one, taps_out, g_top, g_mid, g_bot) = refs[16:24]
    (pool_s, taps_a, sum_a, act_a, taps_b, sum_b, act_b) = refs[24:31]
    (taps_c, sum_c, act_c, pre_c, taps_d, sum_d, err_d) = refs[31:38]
    (taps_e, sum_e, err_c, stack, taps_f, sum_f) = refs[38:44]
    (rows_all, cols_all) = sizes
    (scale_top, scale_mid, scale_low) = scales
    gx, gy = ids[0], ids[1]
    rows_mid, rows_low = rows_all // 2, rows_all // 4

    tiles = rows_all // 4
    for k in range(16):
        tile = gx + (k - 7) // 2
        keep = jnp.full((32, 128), row_ok(tile, tiles)).astype(BF)
        tile = jnp.clip(tile, 0, tiles - 1)
        slab = 2 * ((k - 7) % 2)
        pool_s[k, :, 0:128] = pools[tile, slab] * keep
        pool_s[k, :, 128:256] = pools[tile, slab + 1] * keep

    def enc_taps(k):
        put_taps(taps_a, k, 0, 32, pool_s[k], 8)
        sum_a[k] = dot(w_enc[...], taps_a[k])

    loop(16, enc_taps, 4)
    wide_in = inside(WIDE, 8, cols_all // 2, gy)

    def enc_act(k):
        value = silu(row_sum(sum_a, k, 64)) * (wide_in * row_ok(gx * 2 + k - 6, rows_mid))
        act_a[k] = value.astype(BF)

    loop(14, enc_act, 2)
    for m in range(4):
        pre = row_sum(sum_a, m + 5, 64)
        pre_one[m] = jnp.where(lane(128) < 96, pre[:, 0:128], pre[:, 128:256])
        taps_out[m] = taps_a[m + 6, :, 0:128]

    def low_taps(k):
        pooled = dot(act_a[2 * k], pool_low[...]) + dot(act_a[2 * k + 1], pool_low[...])
        put_taps(taps_b, k, 0, 64, pooled.astype(BF), 4)
        sum_b[k] = dot(w_bot[...], taps_b[k])

    loop(7, low_taps, 7)
    low_in = inside(LOW, 4, cols_all // 4, gy)
    mid_in = inside(MID, 8, cols_all // 2, gy)
    pick = jnp.where(lax.broadcasted_iota(jnp.int32, (64, 128), 1) < 96, 1.0, 0.0)
    near = pick.astype(BF)
    away = (1.0 - pick).astype(BF)

    def low_act(k):
        value = silu(row_sum(sum_b, k, 128)) * (low_in * row_ok(gx + k - 2, rows_low))
        act_b[k] = dot(value.astype(BF), up_low[...]).astype(BF)

    loop(5, low_act, 5)

    def mid_taps(k):
        put_taps(taps_c, k, 0, 192, act_b[(k + 1) // 2], 8)
        narrow = act_a[k + 3, :, 0:128] * near + act_a[k + 3, :, 128:256] * away
        put_taps(taps_c, k, 128, 192, narrow, 8)
        sum_c[k] = dot(w_mid[...], taps_c[k])

    loop(8, mid_taps, 2)

    def mid_act(k):
        pre = row_sum(sum_c, k, 64)
        pre_c[k] = pre
        value = silu(pre) * (mid_in * row_ok(gx * 2 + k - 2, rows_mid))
        act_c[k] = dot(value.astype(BF), up_mid[...]).astype(BF)

    loop(6, mid_act, 6)

    def skip_row(kind, k):
        part = (up, own, down)[k // 4]
        base = 12 * kind + 3 * (k % 4)
        return jnp.concatenate([part[base], part[base + 1], part[base + 2]], axis=1)

    for k in range(12):
        put_taps(taps_d, k, 64, 96, skip_row(0, k), 16)

    def top_taps(j):
        for half in range(2):
            put_taps(taps_d, 2 * j + half, 0, 96, act_c[j], 16)
            sum_d[2 * j + half] = dot(w_top[...], taps_d[2 * j + half])

    loop(6, top_taps, 2)
    for k in range(10):
        pre = row_sum(sum_d, k, 32)
        s = sigmoid(pre)
        if 3 <= k < 7:
            feat[k - 3] = (pre * s)[:, 0:256].astype(BF)
        cot = skip_row(1, k + 1).astype(F32)
        err_d[k] = (cot * (s * (1.0 + pre * (1.0 - s)))).astype(BF)

    def top_back(k):
        put_taps(taps_e, k, 0, 32, err_d[k], 16)
        sum_e[k] = dot(t_top[...], taps_e[k])

    loop(10, top_back, 2)

    total = None
    for k in range(6):
        parts = []
        for a in range(3):
            r = k - a
            own_row = 0 <= r < 4
            parts.append(err_d[r + 3, :, 0:256] if own_row else jnp.zeros((32, 256), BF))
        term = dot_nt(jnp.concatenate(parts, axis=0), taps_d[k + 3, :, 0:256])
        total = term if total is None else total + term
    put_padded(g_top, 0, total * scale_top)

    def mid_err(m):
        one = row_sum(sum_e, 2 * m, 96)
        two = row_sum(sum_e, 2 * m + 1, 96)
        whole = dot_split(one[0:64] + two[0:64], sum_mid[...])
        keep = mid_in * row_ok(gx * 2 + m - 1, rows_mid)
        err_c[m] = (whole * slope(pre_c[m + 1]) * keep).astype(BF)

    loop(4, mid_err, 4)
    for r in range(4):
        dskip[r] = row_sum(sum_e, r + 2, 96)[64:96, 0:256]

    def mid_back(m):
        put_taps(taps_f, m, 0, 64, err_c[m], 8)
        sum_f[m] = dot(t_mid[...], taps_f[m])

    loop(4, mid_back, 2)
    own_mid = jnp.where(lax.broadcasted_iota(jnp.int32, (64, 128), 1) < 64, 1.0, 0.0).astype(BF)
    for k in range(4):
        for a in range(3):
            r = k - a
            piece = err_c[r + 1] * own_mid if 0 <= r < 2 else jnp.zeros((64, 128), BF)
            stack[k, 64 * a : 64 * a + 64, :] = piece
    total = None
    for k in range(4):
        term = dot_nt(stack[k], taps_c[k + 2])
        total = term if total is None else total + term
    put_padded(g_mid, 0, total * scale_mid)

    one = row_sum(sum_f, 0, 192)
    two = row_sum(sum_f, 1, 192)
    whole = dot_split(one[0:128] + two[0:128], sum_low[...])
    keep = jnp.where(lane(128) < 16, 1.0, 0.0)
    err_low = (whole * slope(row_sum(sum_b, 2, 128)) * keep).astype(BF)
    packed[0:128, :] = err_low
    both = jnp.where(lane(128) < 64, one[128:192], pltpu.roll(two[128:192], 64, 1))
    packed[128:192, :] = both.astype(BF)
    for a in range(3):
        put_padded(g_bot, 128 * a, dot_nt(err_low, taps_b[a + 2]) * scale_low)


def tail_kernel(sizes, scale_mid, *refs):
    (ids, own, up_two, down_two, mate, beyond, pre_one, taps_in, dskip) = refs[:9]
    (t_bot, t_enc, up_low, up_mid) = refs[9:13]
    (grad_skip, g_enc) = refs[13:15]
    (taps_a, sum_a, err_s, taps_b, sum_b, near) = refs[15:21]
    (rows_all, cols_all) = sizes
    gx, gy = ids[0], ids[1]
    rows_mid = rows_all // 2
    mid_in = inside(MID, 8, cols_all // 2, gy)

    below = jnp.full((3, 192, 128), jnp.where(gx % 2 == 0, 1.0, 0.0)).astype(BF)
    above = (1.0 - below.astype(F32)).astype(BF)
    near[0] = beyond[...] * below + mate[...] * above
    near[1] = mate[...] * below + beyond[...] * above
    up, down = near.at[0], near.at[1]

    for k, ref in enumerate((up_two, up, own, down, down_two)):
        value = (
            ref[0, 0:128, :].astype(F32)
            + pltpu.roll(ref[2, 0:128, :].astype(F32), 16, 1)
            + pltpu.roll(ref[1, 0:128, :].astype(F32), 112, 1)
        )
        put_taps(taps_a, k, 0, 128, value.astype(BF), 4)
        sum_a[k] = dot(t_bot[...], taps_a[k])
    ups = [dot_split(row_sum(sum_a, k, 64), up_low[...]) * 0.125 for k in range(3)]
    for m in range(4):
        ref = (up, own, own, down)[m]
        odd = m % 2 == 0
        tiles = [ref[k, 128:192, :].astype(F32) for k in range(3)]
        mine, left, right = tiles
        if odd:
            mine = pltpu.roll(mine, 64, 1)
        else:
            left, right = pltpu.roll(left, 64, 1), pltpu.roll(right, 64, 1)
        at = lane(128)
        part = jnp.where(at < 64, mine, jnp.where(at < 96, right, left))
        keep = mid_in * row_ok(gx * 2 + m - 1, rows_mid)
        err = (part + ups[(m + 1) // 2]) * slope(pre_one[m]) * keep
        err = err.astype(BF)
        err_s[m] = err
        put_taps(taps_b, m, 0, 64, err, 8)
        sum_b[m] = dot(t_enc[...], taps_b[m])
    own_mid = jnp.where(lax.broadcasted_iota(jnp.int32, (64, 128), 1) < 64, 1.0, 0.0).astype(BF)
    total = None
    for k in range(4):
        parts = []
        for a in range(3):
            r = k - a
            parts.append(err_s[r + 1] * own_mid if 0 <= r < 2 else jnp.zeros((64, 128), BF))
        term = dot_nt(jnp.concatenate(parts, axis=0), taps_in[k])
        total = term if total is None else total + term
    total = (total * scale_mid).astype(BF)
    g_enc[0:192, :] = total[:, 0:128]
    g_enc[192:384, :] = total[:, 128:256]
    rest = [total[48 * q : 48 * q + 48, 256:288] for q in range(4)]
    g_enc[384:432, :] = jnp.concatenate(rest, axis=1)
    for q in range(2):
        fine = dot_split(row_sum(sum_b, q, 32), up_mid[:, 0:256]) * 0.125
        for half in range(2):
            r = 2 * q + half
            grad_skip[r] = (dskip[r] + fine).astype(BF)


def finish_kernel(g, out):
    rest = jnp.concatenate([g[384:432, 32 * q : 32 * q + 32] for q in range(4)], axis=0)
    pieces = []
    for a in range(3):
        at = 64 * a
        pieces += [g[at : at + 64, :], g[192 + at : 256 + at, :], rest[at : at + 64, :]]
    out[...] = jnp.concatenate(pieces, axis=1).astype(F32)


VMEM = pl.BlockSpec(memory_space=pltpu.VMEM)
SMEM = pl.BlockSpec(memory_space=pltpu.SMEM)


def call(kernel, outs, scratch, scalars, *args, cost=1, grant=8):
    return pl.pallas_call(
        kernel,
        out_shape=[jax.ShapeDtypeStruct(s, d) for s, d in outs],
        in_specs=[SMEM] * scalars + [VMEM] * (len(args) - scalars),
        out_specs=[VMEM] * len(outs),
        scratch_shapes=[pltpu.VMEM(s, d) for s, d in scratch],
        compiler_params=pltpu.CompilerParams(vmem_limit_bytes=grant * 1024 * 1024),
        cost_estimate=pl.CostEstimate(
            flops=cost * 500_000_000, bytes_accessed=cost * 1_000_000, transcendentals=0
        ),
    )(*args)


def shift(value, axis, count, step):
    return lax.ppermute(value, axis, [(i, i + step) for i in range(count) if 0 <= i + step < count])


def tiles_of(g):
    rows, width = g.shape
    return g.reshape(rows // 8, 8, width // 128, 128).transpose(0, 2, 1, 3).reshape(-1, 8, 128)


def from_tiles(tiles, rows, width):
    wide = -(-width // 128)
    g = tiles.reshape(rows // 8, wide, 8, 128).transpose(0, 2, 1, 3).reshape(rows, wide * 128)
    return g[:, :width]


def full_gradient(g):
    rows, _ = g.shape
    out = rows // 3
    return jnp.concatenate([g[out * a : out * a + out] for a in range(3)], axis=1).astype(F32)


def solution(mesh):
    ngx, ngy = mesh.shape["gx"], mesh.shape["gy"]
    devices = ngx * ngy
    const = {k: np.asarray(v) for k, v in constants().items()}

    def step(skip_input, w_encoder, w_bottom, w_middle, w_upper, cotangent):
        gx, gy = lax.axis_index("gx"), lax.axis_index("gy")
        ids = jnp.stack([gx, gy]).astype(jnp.int32)
        rows_all, cols_all = 4 * ngx, 16 * ngy
        sizes = (rows_all, cols_all)
        cells = rows_all * cols_all * 16
        scales = tuple(1.0 / math.sqrt(cells // k) for k in (1, 8, 64))
        c = {k: jnp.asarray(v, BF) for k, v in const.items()}

        block, width = w_bottom.shape
        slabs = block * 2048 // 4096
        weight = jnp.pad(w_bottom, ((0, 0), (0, 2048 - width)))
        lanes = weight.shape[1] // 128
        weight = weight.reshape(block, lanes, 128).transpose(1, 0, 2).reshape(slabs, 32, 128)

        skip = skip_input.transpose(1, 0, 2)
        cot = cotangent.transpose(1, 0, 2)
        to_left, to_right = call(
            pool_kernel, [((10, 32, 128), BF)] * 2, [], 0, skip, cot, c["pool_tile"]
        )
        right = shift(to_left, "gy", ngy, -1)
        left = shift(to_right, "gy", ngy, 1)
        own, spread = call(
            widen_kernel,
            [((24, 32, 128), BF), ((ngx, 4 + slabs, 32, 128), BF)],
            [],
            0,
            skip,
            cot,
            to_left,
            right,
            left,
            weight,
        )
        up = shift(own, "gx", ngx, 1)
        down = shift(own, "gx", ngx, -1)
        pools = lax.all_to_all(spread, "gx", split_axis=0, concat_axis=0, tiled=True)
        w_all = pools[:, 4:].reshape(ngx, lanes, block, 128).transpose(0, 2, 1, 3)
        w_all = w_all.reshape(ngx * block, lanes * 128)[:, :width]
        w_enc, t_enc, w_mid, t_mid, w_top, t_top = call(
            lambda *refs: weight_kernel((1, 1, 1), (1, 1, 1), *refs),
            [
                ((192, 288), BF),
                ((96, 576), BF),
                ((192, 1728), BF),
                ((576, 576), BF),
                ((96, 864), BF),
                ((288, 288), BF),
            ],
            [],
            0,
            w_encoder,
            w_middle,
            w_upper,
            cost=4,
        )
        (w_bot,) = call(
            lambda *refs: weight_kernel((1,), (0,), *refs), [((384, 576), BF)], [], 0, w_all
        )
        (t_bot,) = call(
            lambda *refs: weight_kernel((0,), (1,), *refs),
            [((192, 1152), BF)],
            [],
            0,
            w_all,
            cost=2,
        )

        outs = [
            ((4, 32, 256), BF),
            ((4, 32, 256), F32),
            ((192, 128), BF),
            ((4, 64, 128), F32),
            ((4, 288, 128), BF),
            ((96, 896), BF),
            ((192, 1792), BF),
            ((384, 640), BF),
        ]
        scratch = [
            ((16, 32, 256), BF),
            ((16, 288, 256), BF),
            ((16, 192, 256), F32),
            ((14, 64, 256), BF),
            ((7, 576, 128), BF),
            ((7, 384, 128), F32),
            ((5, 128, 128), BF),
            ((8, 1728, 128), BF),
            ((8, 192, 128), F32),
            ((6, 64, 384), BF),
            ((6, 64, 128), F32),
            ((12, 864, 384), BF),
            ((12, 96, 384), F32),
            ((10, 32, 384), BF),
            ((10, 288, 384), BF),
            ((10, 288, 384), F32),
            ((4, 64, 128), BF),
            ((4, 192, 128), BF),
            ((4, 576, 128), BF),
            ((4, 576, 128), F32),
        ]
        feat, dskip, packed, pre_one, taps_one, g_top, g_mid, g_bot = call(
            lambda *refs: main_kernel(sizes, scales, *refs),
            outs,
            scratch,
            1,
            ids,
            own,
            up,
            down,
            pools,
            w_enc,
            w_bot,
            w_mid,
            w_top,
            t_top,
            t_mid,
            c["up_low"],
            c["sum_low"],
            c["up_mid"],
            c["sum_mid"],
            c["pool_low"],
            cost=20,
            grant=40,
        )

        from_left = shift(packed, "gy", ngy, 1)
        from_right = shift(packed, "gy", ngy, -1)
        line = jnp.stack([packed, from_left, from_right])
        core = gx % 2
        swap = [(i, i ^ 1) for i in range(ngx)]
        mate = lax.ppermute(line, "gx", swap)
        line_up = shift(line, "gx", ngx, 2)
        line_down = shift(line, "gx", ngx, -2)
        beyond = lax.ppermute(jnp.where(core == 0, line_down, line_up), "gx", swap)
        grad_skip, g_enc = call(
            lambda *refs: tail_kernel(sizes, scales[1], *refs),
            [((4, 32, 256), BF), ((432, 128), BF)],
            [
                ((5, 1152, 128), BF),
                ((5, 192, 128), F32),
                ((4, 64, 128), BF),
                ((4, 576, 128), BF),
                ((4, 96, 128), F32),
                ((2, 3, 192, 128), BF),
            ],
            1,
            ids,
            line,
            line_up,
            line_down,
            mate,
            beyond,
            pre_one,
            taps_one,
            dskip,
            t_bot,
            t_enc,
            c["up_low"],
            c["up_mid"],
            cost=4,
        )

        grads = ((g_top, 864), (g_mid, 1728), (g_bot, 576), (g_enc, 128))
        tiles = [tiles_of(g) for g, _ in grads]
        spare = -sum(t.shape[0] for t in tiles) % devices
        flat = jnp.concatenate(tiles + [jnp.zeros((spare, 8, 128), BF)], axis=0)
        half = flat.shape[0] // 2
        keep = lax.dynamic_slice_in_dim(flat, core * half, half, 0)
        other = lax.dynamic_slice_in_dim(flat, (1 - core) * half, half, 0)
        other = lax.ppermute(other, "gx", swap)
        mine = (keep.astype(F32) + other.astype(F32)).astype(BF)
        parts = mine.reshape(devices // 2, -1, 128)
        groups = [[i for i in range(devices) if i // ngy % 2 == k] for k in range(2)]
        parts = lax.all_to_all(
            parts, AXES, split_axis=0, concat_axis=0, axis_index_groups=groups, tiled=True
        )
        total = parts.astype(F32).sum(axis=0).astype(BF)
        spread = jnp.broadcast_to(total[None], parts.shape)
        spread = lax.all_to_all(
            spread, AXES, split_axis=0, concat_axis=0, axis_index_groups=groups, tiled=True
        )
        mine = spread.reshape(half, 8, 128)
        other = lax.ppermute(mine, "gx", swap)
        first = jnp.where(core == 0, mine, other)
        second = jnp.where(core == 0, other, mine)
        whole = jnp.concatenate([first, second], axis=0)

        full = []
        start = 0
        for (g, width), t in zip(grads, tiles):
            full.append(from_tiles(whole[start : start + t.shape[0]], g.shape[0], width))
            start += t.shape[0]
        full_top, full_mid, full_bot, full_enc = full
        (full_enc,) = call(finish_kernel, [((64, 864), F32)], [], 0, full_enc)
        mine_bot = full_bot.reshape(3, ngx, block, -1)
        mine_bot = lax.dynamic_index_in_dim(mine_bot, gx, 1, keepdims=False)
        mine_bot = mine_bot.reshape(3 * block, -1)
        return (
            feat.transpose(1, 0, 2),
            grad_skip.transpose(1, 0, 2),
            full_enc,
            full_gradient(mine_bot),
            full_gradient(full_mid),
            full_gradient(full_top),
        )

    in_specs = (P(None, "gx", "gy"), P(), P("gx", None), P(), P(), P(None, "gx", "gy"))
    out_specs = (P(None, "gx", "gy"), P(None, "gx", "gy"), P(), P("gx", None), P(), P())
    return jax.shard_map(step, mesh=mesh, in_specs=in_specs, out_specs=out_specs, check_vma=False)
```

```python
import math

import jax
import jax.numpy as jnp
import numpy as np
from jax import lax
from jax.experimental import pallas as pl
from jax.experimental.pallas import tpu as pltpu
from jax.sharding import PartitionSpec as P

AXES = ("gx", "gy")
BF = jnp.bfloat16
F32 = jnp.float32


def columns(lanes, depth, split):
    col = np.arange(lanes) // depth
    return np.where(col >= split, col - lanes // depth, col), np.arange(lanes) % depth


def upsampling(coarse, fine):
    (col_c, z_c), (col_f, z_f) = (columns(*coarse), columns(*fine))
    hit = (col_c[:, None] == col_f[None, :] // 2) & (z_c[:, None] == z_f[None, :] // 2)
    return hit.astype(np.float32)


TOP = (384, 16, 20)
WIDE = (256, 8, 16)
MID = (128, 8, 12)
LOW = (128, 4, 16)


def constants():
    low_mid = upsampling(LOW, MID)
    mid_top = upsampling(MID, TOP)
    wide_low = upsampling(LOW, WIDE).T / 8.0
    tile_pool = mid_top[:64, :256].T / 8.0
    tile_pool = np.concatenate([tile_pool, tile_pool], axis=1)
    return {
        "up_low": low_mid,
        "sum_low": low_mid.T,
        "up_mid": mid_top,
        "sum_mid": mid_top.T,
        "pool_low": wide_low,
        "pool_tile": tile_pool,
    }


def dot(a, b):
    return jnp.dot(a, b, preferred_element_type=F32)


def dot_nt(a, b):
    return lax.dot_general(a, b, (((1,), (1,)), ((), ())), preferred_element_type=F32)


def dot_split(a, b):
    head = a.astype(BF)
    rest = (a - head.astype(F32)).astype(BF)
    return dot(head, b) + dot(rest, b)


def loop(count, body, unroll=1):
    def step(i, carry):
        for u in range(unroll):
            body(i * unroll + u)
        return carry

    if unroll == count:
        step(0, 0)
    else:
        lax.fori_loop(0, count // unroll, step, 0)


def lane(length):
    return lax.broadcasted_iota(jnp.int32, (1, length), 1)


def inside(region, tile_cols, total_cols, index):
    lanes, depth, split = region
    col = lane(lanes) // depth
    col = jnp.where(col >= split, col - lanes // depth, col) + index * tile_cols
    return jnp.where((col >= 0) & (col < total_cols), 1.0, 0.0)


def row_ok(row, total):
    return jnp.where((row >= 0) & (row < total), 1.0, 0.0)


def depth_masks(shape, depth):
    z = lax.broadcasted_iota(jnp.int32, shape, 1) % depth
    below = jnp.where(z == depth - 1, 0.0, 1.0).astype(BF)
    above = jnp.where(z == 0, 0.0, 1.0).astype(BF)
    return below, above


def put_taps(dst, row, first, width, value, depth):
    chans, lanes = value.shape
    below, above = depth_masks(value.shape, depth)
    kinds = (value * below, value, value * above)
    for b in range(3):
        for e in range(3):
            shift = (b - 1) * depth + (e - 1)
            piece = kinds[e]
            if shift:
                piece = pltpu.roll(piece, (-shift) % lanes, 1)
            start = (3 * b + e) * width + first
            dst[row, start : start + chans, :] = piece


def sigmoid(v):
    return 1.0 / (1.0 + jnp.exp(-v))


def silu(v):
    return v * sigmoid(v)


def slope(v):
    s = sigmoid(v)
    return s * (1.0 + v * (1.0 - s))


def row_sum(ref, row, chans):
    return (
        ref[row, 0:chans, :]
        + ref[row + 1, chans : 2 * chans, :]
        + ref[row + 2, 2 * chans : 3 * chans, :]
    )


def put_padded(out, row, value):
    rows, width = value.shape
    out[row : row + rows, 0:width] = value.astype(BF)
    out[row : row + rows, width:] = jnp.zeros((rows, out.shape[1] - width), BF)


def pool_kernel(skip, cot, pool_tile, to_left, to_right):
    for r in range(4):
        to_left[r] = skip[r, :, 0:128]
        to_left[4 + r] = cot[r, :, 0:128]
        to_right[r] = skip[r, :, 128:256]
        to_right[4 + r] = cot[r, :, 128:256]
    for q in range(2):
        pooled = dot(skip[2 * q], pool_tile[...]) + dot(skip[2 * q + 1], pool_tile[...])
        pooled = pooled.astype(BF)
        to_left[8 + q] = pooled
        to_right[8 + q] = pooled


def widen_kernel(skip, cot, own, right, left, weight, out):
    first = jnp.where(lax.broadcasted_iota(jnp.int32, (32, 128), 1) < 64, 1.0, 0.0)
    head = first.astype(BF)
    tail = (1.0 - first).astype(BF)
    for r in range(4):
        for k, tile in enumerate((skip, cot)):
            base = 12 * k + 3 * r
            out[base] = tile[r, :, 0:128]
            out[base + 1] = tile[r, :, 128:256]
            out[base + 2] = right[4 * k + r] * head + left[4 * k + r] * tail
    for q in range(2):
        out[24 + 2 * q] = own[8 + q] * head + right[8 + q] * tail
        out[25 + 2 * q] = left[8 + q] * tail
    for q in range(weight.shape[0]):
        out[28 + q] = weight[q]


def gather_kernel(tiles, block, *refs):
    (ids, own, up, down, mate, beyond, far_up, far_down, three_m, far_up_m, far_down_m) = refs[:11]
    (fine, pools, w_out, w_all, w_flat) = refs[11:16]
    gx = ids[0]
    core = gx % 2
    wide = own.shape[0] - 24
    low = jnp.where(core == 0, 1.0, 0.0)
    below = jnp.full((24, 32, 128), low).astype(BF)
    above = jnp.full((24, 32, 128), 1.0 - low).astype(BF)
    first = beyond[...] * below + mate[0:24] * above
    last = mate[0:24] * below + beyond[...] * above
    top = jnp.full((12, 32, 128), row_ok(gx - 1, tiles)).astype(BF)
    bottom = jnp.full((12, 32, 128), row_ok(gx + 1, tiles)).astype(BF)
    for k in range(2):
        fine[0, 12 * k : 12 * k + 12] = first[12 * k : 12 * k + 12] * top
        fine[1, 12 * k : 12 * k + 12] = last[12 * k : 12 * k + 12] * bottom

    def chips(own_at, down_at, up_at, far_down_ref, far_up_ref):
        return [
            own_at,
            down_at,
            (far_down_ref, 0),
            (far_down_ref, wide),
            (far_down_ref, 2 * wide),
            (far_up_ref, wide),
            (far_up_ref, 2 * wide),
            up_at,
        ]

    mine = chips((own, 24), (down, 24), (up, 24), far_down, far_up)
    other = chips((three_m, wide), (three_m, 2 * wide), (three_m, 0), far_down_m, far_up_m)
    for parity, entries in ((gx, mine), (gx + 1 - 2 * core, other)):
        for j, (ref, at) in enumerate(entries):
            w_all[(parity + 2 * j) % tiles] = ref[at + 4 : at + wide]
        for j, step in ((0, 0), (1, 2), (2, 4), (6, -4), (7, -2)):
            tile = parity + step
            ref, at = entries[j]
            place = tile - gx + 5
            keep = jnp.full((4, 32, 128), row_ok(tile, tiles)).astype(BF)
            pools[place] = ref[at : at + 4] * keep
    lanes = w_flat.shape[1] // 128
    for b in range(tiles):
        rows = w_all[b].reshape(lanes * block, 128)
        for l in range(lanes):
            w_flat[b * block : b * block + block, 128 * l : 128 * l + 128] = rows[
                l * block : l * block + block
            ]
    put_forward(w_flat, w_out)


def put_forward(w, out):
    rows = w.shape[0]
    width = out.shape[1]
    for a in range(3):
        out[rows * a : rows * a + rows, :] = w[:, a * width : (a + 1) * width]


def put_backward(w, out):
    chans = out.shape[0] // 3
    i = lax.broadcasted_iota(jnp.int32, (chans, chans), 0)
    j = lax.broadcasted_iota(jnp.int32, (chans, chans), 1)
    unit = jnp.where(i == j, 1.0, 0.0).astype(BF)
    for a in range(3):
        taps = [26 - 9 * a - k for k in range(9)]
        stacked = jnp.concatenate([w[:, t * chans : t * chans + chans] for t in taps], axis=0)
        out[chans * a : chans * a + chans, :] = dot_nt(unit, stacked).astype(BF)


def weight_kernel(forward, backward, *refs):
    sources, outs = refs[: len(forward)], refs[len(forward) :]
    k = 0
    for w, fwd, bwd in zip(sources, forward, backward):
        if fwd:
            put_forward(w, outs[k])
            k += 1
        if bwd:
            put_backward(w, outs[k])
            k += 1


def main_kernel(sizes, scales, *refs):
    (ids, own, fine, pools) = refs[:4]
    up, down = fine.at[0], fine.at[1]
    (w_enc, w_bot, w_mid, w_top, t_top, t_mid) = refs[4:10]
    (up_low, sum_low, up_mid, sum_mid, pool_low) = refs[10:15]
    (feat, dskip, packed, pre_one, taps_out, g_top, g_mid, g_bot) = refs[15:23]
    (pool_s, taps_a, sum_a, act_a, taps_b, sum_b, act_b) = refs[23:30]
    (taps_c, sum_c, act_c, pre_c, taps_d, sum_d, err_d) = refs[30:37]
    (taps_e, sum_e, err_c, stack, taps_f, sum_f) = refs[37:43]
    (rows_all, cols_all) = sizes
    (scale_top, scale_mid, scale_low) = scales
    gx, gy = ids[0], ids[1]
    rows_mid, rows_low = rows_all // 2, rows_all // 4

    for k in range(16):
        tile, slab = 5 + (k - 7) // 2, 2 * ((k - 7) % 2)
        pool_s[k, :, 0:128] = pools[tile, slab]
        pool_s[k, :, 128:256] = pools[tile, slab + 1]

    def enc_taps(k):
        put_taps(taps_a, k, 0, 32, pool_s[k], 8)
        sum_a[k] = dot(w_enc[...], taps_a[k])

    loop(16, enc_taps, 4)
    wide_in = inside(WIDE, 8, cols_all // 2, gy)

    def enc_act(k):
        value = silu(row_sum(sum_a, k, 64)) * (wide_in * row_ok(gx * 2 + k - 6, rows_mid))
        act_a[k] = value.astype(BF)

    loop(14, enc_act, 2)
    for m in range(4):
        pre = row_sum(sum_a, m + 5, 64)
        pre_one[m] = jnp.where(lane(128) < 96, pre[:, 0:128], pre[:, 128:256])
        taps_out[m] = taps_a[m + 6, :, 0:128]

    def low_taps(k):
        pooled = dot(act_a[2 * k], pool_low[...]) + dot(act_a[2 * k + 1], pool_low[...])
        put_taps(taps_b, k, 0, 64, pooled.astype(BF), 4)
        sum_b[k] = dot(w_bot[...], taps_b[k])

    loop(7, low_taps, 7)
    low_in = inside(LOW, 4, cols_all // 4, gy)
    mid_in = inside(MID, 8, cols_all // 2, gy)
    pick = jnp.where(lax.broadcasted_iota(jnp.int32, (64, 128), 1) < 96, 1.0, 0.0)
    near = pick.astype(BF)
    away = (1.0 - pick).astype(BF)

    def low_act(k):
        value = silu(row_sum(sum_b, k, 128)) * (low_in * row_ok(gx + k - 2, rows_low))
        act_b[k] = dot(value.astype(BF), up_low[...]).astype(BF)

    loop(5, low_act, 5)

    def mid_taps(k):
        put_taps(taps_c, k, 0, 192, act_b[(k + 1) // 2], 8)
        narrow = act_a[k + 3, :, 0:128] * near + act_a[k + 3, :, 128:256] * away
        put_taps(taps_c, k, 128, 192, narrow, 8)
        sum_c[k] = dot(w_mid[...], taps_c[k])

    loop(8, mid_taps, 2)

    def mid_act(k):
        pre = row_sum(sum_c, k, 64)
        pre_c[k] = pre
        value = silu(pre) * (mid_in * row_ok(gx * 2 + k - 2, rows_mid))
        act_c[k] = dot(value.astype(BF), up_mid[...]).astype(BF)

    loop(6, mid_act, 6)

    def skip_row(kind, k):
        part = (up, own, down)[k // 4]
        base = 12 * kind + 3 * (k % 4)
        return jnp.concatenate([part[base], part[base + 1], part[base + 2]], axis=1)

    for k in range(12):
        put_taps(taps_d, k, 64, 96, skip_row(0, k), 16)

    def top_taps(j):
        for half in range(2):
            put_taps(taps_d, 2 * j + half, 0, 96, act_c[j], 16)
            sum_d[2 * j + half] = dot(w_top[...], taps_d[2 * j + half])

    loop(6, top_taps, 2)
    for k in range(10):
        pre = row_sum(sum_d, k, 32)
        s = sigmoid(pre)
        if 3 <= k < 7:
            feat[k - 3] = (pre * s)[:, 0:256].astype(BF)
        cot = skip_row(1, k + 1).astype(F32)
        err_d[k] = (cot * (s * (1.0 + pre * (1.0 - s)))).astype(BF)

    def top_back(k):
        put_taps(taps_e, k, 0, 32, err_d[k], 16)
        sum_e[k] = dot(t_top[...], taps_e[k])

    loop(10, top_back, 2)

    total = None
    for k in range(6):
        parts = []
        for a in range(3):
            r = k - a
            own_row = 0 <= r < 4
            parts.append(err_d[r + 3, :, 0:256] if own_row else jnp.zeros((32, 256), BF))
        term = dot_nt(jnp.concatenate(parts, axis=0), taps_d[k + 3, :, 0:256])
        total = term if total is None else total + term
    put_padded(g_top, 0, total * scale_top)

    def mid_err(m):
        one = row_sum(sum_e, 2 * m, 96)
        two = row_sum(sum_e, 2 * m + 1, 96)
        whole = dot_split(one[0:64] + two[0:64], sum_mid[...])
        keep = mid_in * row_ok(gx * 2 + m - 1, rows_mid)
        err_c[m] = (whole * slope(pre_c[m + 1]) * keep).astype(BF)

    loop(4, mid_err, 4)
    for r in range(4):
        dskip[r] = row_sum(sum_e, r + 2, 96)[64:96, 0:256]

    def mid_back(m):
        put_taps(taps_f, m, 0, 64, err_c[m], 8)
        sum_f[m] = dot(t_mid[...], taps_f[m])

    loop(4, mid_back, 2)
    own_mid = jnp.where(lax.broadcasted_iota(jnp.int32, (64, 128), 1) < 64, 1.0, 0.0).astype(BF)
    for k in range(4):
        for a in range(3):
            r = k - a
            piece = err_c[r + 1] * own_mid if 0 <= r < 2 else jnp.zeros((64, 128), BF)
            stack[k, 64 * a : 64 * a + 64, :] = piece
    total = None
    for k in range(4):
        term = dot_nt(stack[k], taps_c[k + 2])
        total = term if total is None else total + term
    put_padded(g_mid, 0, total * scale_mid)

    one = row_sum(sum_f, 0, 192)
    two = row_sum(sum_f, 1, 192)
    whole = dot_split(one[0:128] + two[0:128], sum_low[...])
    keep = jnp.where(lane(128) < 16, 1.0, 0.0)
    err_low = (whole * slope(row_sum(sum_b, 2, 128)) * keep).astype(BF)
    packed[0:128, :] = err_low
    both = jnp.where(lane(128) < 64, one[128:192], pltpu.roll(two[128:192], 64, 1))
    packed[128:192, :] = both.astype(BF)
    for a in range(3):
        put_padded(g_bot, 128 * a, dot_nt(err_low, taps_b[a + 2]) * scale_low)


def tail_kernel(sizes, scale_mid, *refs):
    (ids, own, up_two, down_two, mate, beyond, pre_one, taps_in, dskip) = refs[:9]
    (t_bot, t_enc, up_low, up_mid) = refs[9:13]
    (grad_skip, g_enc) = refs[13:15]
    (taps_a, sum_a, err_s, taps_b, sum_b, near) = refs[15:21]
    (rows_all, cols_all) = sizes
    gx, gy = ids[0], ids[1]
    rows_mid = rows_all // 2
    mid_in = inside(MID, 8, cols_all // 2, gy)

    below = jnp.full((3, 192, 128), jnp.where(gx % 2 == 0, 1.0, 0.0)).astype(BF)
    above = (1.0 - below.astype(F32)).astype(BF)
    near[0] = beyond[...] * below + mate[...] * above
    near[1] = mate[...] * below + beyond[...] * above
    up, down = near.at[0], near.at[1]

    for k, ref in enumerate((up_two, up, own, down, down_two)):
        value = (
            ref[0, 0:128, :].astype(F32)
            + pltpu.roll(ref[2, 0:128, :].astype(F32), 16, 1)
            + pltpu.roll(ref[1, 0:128, :].astype(F32), 112, 1)
        )
        put_taps(taps_a, k, 0, 128, value.astype(BF), 4)
        sum_a[k] = dot(t_bot[...], taps_a[k])
    ups = [dot_split(row_sum(sum_a, k, 64), up_low[...]) * 0.125 for k in range(3)]
    for m in range(4):
        ref = (up, own, own, down)[m]
        odd = m % 2 == 0
        tiles = [ref[k, 128:192, :].astype(F32) for k in range(3)]
        mine, left, right = tiles
        if odd:
            mine = pltpu.roll(mine, 64, 1)
        else:
            left, right = pltpu.roll(left, 64, 1), pltpu.roll(right, 64, 1)
        at = lane(128)
        part = jnp.where(at < 64, mine, jnp.where(at < 96, right, left))
        keep = mid_in * row_ok(gx * 2 + m - 1, rows_mid)
        err = (part + ups[(m + 1) // 2]) * slope(pre_one[m]) * keep
        err = err.astype(BF)
        err_s[m] = err
        put_taps(taps_b, m, 0, 64, err, 8)
        sum_b[m] = dot(t_enc[...], taps_b[m])
    own_mid = jnp.where(lax.broadcasted_iota(jnp.int32, (64, 128), 1) < 64, 1.0, 0.0).astype(BF)
    total = None
    for k in range(4):
        parts = []
        for a in range(3):
            r = k - a
            parts.append(err_s[r + 1] * own_mid if 0 <= r < 2 else jnp.zeros((64, 128), BF))
        term = dot_nt(jnp.concatenate(parts, axis=0), taps_in[k])
        total = term if total is None else total + term
    total = (total * scale_mid).astype(BF)
    g_enc[0:192, :] = total[:, 0:128]
    g_enc[192:384, :] = total[:, 128:256]
    rest = [total[48 * q : 48 * q + 48, 256:288] for q in range(4)]
    g_enc[384:432, :] = jnp.concatenate(rest, axis=1)
    for q in range(2):
        fine = dot_split(row_sum(sum_b, q, 32), up_mid[:, 0:256]) * 0.125
        for half in range(2):
            r = 2 * q + half
            grad_skip[r] = (dskip[r] + fine).astype(BF)


def finish_kernel(g, out):
    rest = jnp.concatenate([g[384:432, 32 * q : 32 * q + 32] for q in range(4)], axis=0)
    pieces = []
    for a in range(3):
        at = 64 * a
        pieces += [g[at : at + 64, :], g[192 + at : 256 + at, :], rest[at : at + 64, :]]
    out[...] = jnp.concatenate(pieces, axis=1).astype(F32)


VMEM = pl.BlockSpec(memory_space=pltpu.VMEM)
SMEM = pl.BlockSpec(memory_space=pltpu.SMEM)


def call(kernel, outs, scratch, scalars, *args, cost=1, grant=8):
    return pl.pallas_call(
        kernel,
        out_shape=[jax.ShapeDtypeStruct(s, d) for s, d in outs],
        in_specs=[SMEM] * scalars + [VMEM] * (len(args) - scalars),
        out_specs=[VMEM] * len(outs),
        scratch_shapes=[pltpu.VMEM(s, d) for s, d in scratch],
        compiler_params=pltpu.CompilerParams(vmem_limit_bytes=grant * 1024 * 1024),
        cost_estimate=pl.CostEstimate(
            flops=cost * 500_000_000, bytes_accessed=cost * 1_000_000, transcendentals=0
        ),
    )(*args)


def shift(value, axis, count, step):
    return lax.ppermute(value, axis, [(i, i + step) for i in range(count) if 0 <= i + step < count])


def turn(value, axis, count, step):
    return lax.ppermute(value, axis, [(i, (i + step) % count) for i in range(count)])


def tiles_of(g):
    rows, width = g.shape
    return g.reshape(rows // 8, 8, width // 128, 128).transpose(0, 2, 1, 3).reshape(-1, 8, 128)


def from_tiles(tiles, rows, width):
    wide = -(-width // 128)
    g = tiles.reshape(rows // 8, wide, 8, 128).transpose(0, 2, 1, 3).reshape(rows, wide * 128)
    return g[:, :width]


def full_gradient(g):
    rows, _ = g.shape
    out = rows // 3
    return jnp.concatenate([g[out * a : out * a + out] for a in range(3)], axis=1).astype(F32)


def solution(mesh):
    ngx, ngy = mesh.shape["gx"], mesh.shape["gy"]
    devices = ngx * ngy
    const = {k: np.asarray(v) for k, v in constants().items()}

    def step(skip_input, w_encoder, w_bottom, w_middle, w_upper, cotangent):
        gx, gy = lax.axis_index("gx"), lax.axis_index("gy")
        ids = jnp.stack([gx, gy]).astype(jnp.int32)
        rows_all, cols_all = 4 * ngx, 16 * ngy
        sizes = (rows_all, cols_all)
        cells = rows_all * cols_all * 16
        scales = tuple(1.0 / math.sqrt(cells // k) for k in (1, 8, 64))
        c = {k: jnp.asarray(v, BF) for k, v in const.items()}

        block, width = w_bottom.shape
        slabs = block * 2048 // 4096
        weight = jnp.pad(w_bottom, ((0, 0), (0, 2048 - width)))
        lanes = weight.shape[1] // 128
        weight = weight.reshape(block, lanes, 128).transpose(1, 0, 2).reshape(slabs, 32, 128)

        skip = skip_input.transpose(1, 0, 2)
        cot = cotangent.transpose(1, 0, 2)
        to_left, to_right = call(
            pool_kernel, [((10, 32, 128), BF)] * 2, [], 0, skip, cot, c["pool_tile"]
        )
        right = shift(to_left, "gy", ngy, -1)
        left = shift(to_right, "gy", ngy, 1)
        (own,) = call(
            widen_kernel,
            [((28 + slabs, 32, 128), BF)],
            [],
            0,
            skip,
            cot,
            to_left,
            right,
            left,
            weight,
        )
        core = gx % 2
        swap = [(i, i ^ 1) for i in range(ngx)]
        up = turn(own, "gx", ngx, 2)
        down = turn(own, "gx", ngx, -2)
        mate = lax.ppermute(own[0:24], "gx", swap)
        three = jnp.concatenate([up[24:], own[24:], down[24:]], axis=0)
        far_up = turn(three, "gx", ngx, 6)
        far_down = turn(three, "gx", ngx, -6)
        three_m = lax.ppermute(three, "gx", swap)
        beyond = lax.ppermute(jnp.where(core == 0, down[0:24], up[0:24]), "gx", swap)
        far_up_m = lax.ppermute(far_up, "gx", swap)
        far_down_m = lax.ppermute(far_down, "gx", swap)
        fine, pools, w_bot, _, w_flat = call(
            lambda *refs: gather_kernel(ngx, block, *refs),
            [
                ((2, 24, 32, 128), BF),
                ((11, 4, 32, 128), BF),
                ((384, 576), BF),
                ((ngx, slabs, 32, 128), BF),
                ((ngx * block, lanes * 128), BF),
            ],
            [],
            1,
            ids,
            own,
            up,
            down,
            mate,
            beyond,
            far_up,
            far_down,
            three_m,
            far_up_m,
            far_down_m,
        )
        w_enc, t_enc, w_mid, t_mid, w_top, t_top = call(
            lambda *refs: weight_kernel((1, 1, 1), (1, 1, 1), *refs),
            [
                ((192, 288), BF),
                ((96, 576), BF),
                ((192, 1728), BF),
                ((576, 576), BF),
                ((96, 864), BF),
                ((288, 288), BF),
            ],
            [],
            0,
            w_encoder,
            w_middle,
            w_upper,
            cost=4,
        )
        (t_bot,) = call(
            lambda *refs: weight_kernel((0,), (1,), *refs),
            [((192, 1152), BF)],
            [],
            0,
            w_flat,
            cost=2,
        )

        outs = [
            ((4, 32, 256), BF),
            ((4, 32, 256), F32),
            ((192, 128), BF),
            ((4, 64, 128), F32),
            ((4, 288, 128), BF),
            ((96, 896), BF),
            ((192, 1792), BF),
            ((384, 640), BF),
        ]
        scratch = [
            ((16, 32, 256), BF),
            ((16, 288, 256), BF),
            ((16, 192, 256), F32),
            ((14, 64, 256), BF),
            ((7, 576, 128), BF),
            ((7, 384, 128), F32),
            ((5, 128, 128), BF),
            ((8, 1728, 128), BF),
            ((8, 192, 128), F32),
            ((6, 64, 384), BF),
            ((6, 64, 128), F32),
            ((12, 864, 384), BF),
            ((12, 96, 384), F32),
            ((10, 32, 384), BF),
            ((10, 288, 384), BF),
            ((10, 288, 384), F32),
            ((4, 64, 128), BF),
            ((4, 192, 128), BF),
            ((4, 576, 128), BF),
            ((4, 576, 128), F32),
        ]
        feat, dskip, packed, pre_one, taps_one, g_top, g_mid, g_bot = call(
            lambda *refs: main_kernel(sizes, scales, *refs),
            outs,
            scratch,
            1,
            ids,
            own,
            fine,
            pools,
            w_enc,
            w_bot,
            w_mid,
            w_top,
            t_top,
            t_mid,
            c["up_low"],
            c["sum_low"],
            c["up_mid"],
            c["sum_mid"],
            c["pool_low"],
            cost=20,
            grant=33,
        )

        from_left = shift(packed, "gy", ngy, 1)
        from_right = shift(packed, "gy", ngy, -1)
        line = jnp.stack([packed, from_left, from_right])
        mate = lax.ppermute(line, "gx", swap)
        line_up = shift(line, "gx", ngx, 2)
        line_down = shift(line, "gx", ngx, -2)
        beyond = lax.ppermute(jnp.where(core == 0, line_down, line_up), "gx", swap)
        grad_skip, g_enc = call(
            lambda *refs: tail_kernel(sizes, scales[1], *refs),
            [((4, 32, 256), BF), ((432, 128), BF)],
            [
                ((5, 1152, 128), BF),
                ((5, 192, 128), F32),
                ((4, 64, 128), BF),
                ((4, 576, 128), BF),
                ((4, 96, 128), F32),
                ((2, 3, 192, 128), BF),
            ],
            1,
            ids,
            line,
            line_up,
            line_down,
            mate,
            beyond,
            pre_one,
            taps_one,
            dskip,
            t_bot,
            t_enc,
            c["up_low"],
            c["up_mid"],
            cost=4,
        )

        grads = ((g_top, 864), (g_mid, 1728), (g_bot, 576), (g_enc, 128))
        tiles = [tiles_of(g) for g, _ in grads]
        spare = -sum(t.shape[0] for t in tiles) % devices
        flat = jnp.concatenate(tiles + [jnp.zeros((spare, 8, 128), BF)], axis=0)
        half = flat.shape[0] // 2
        keep = lax.dynamic_slice_in_dim(flat, core * half, half, 0)
        other = lax.dynamic_slice_in_dim(flat, (1 - core) * half, half, 0)
        other = lax.ppermute(other, "gx", swap)
        mine = (keep.astype(F32) + other.astype(F32)).astype(BF)
        parts = mine.reshape(devices // 2, -1, 128)
        groups = [[i for i in range(devices) if i // ngy % 2 == k] for k in range(2)]
        parts = lax.all_to_all(
            parts, AXES, split_axis=0, concat_axis=0, axis_index_groups=groups, tiled=True
        )
        total = parts.astype(F32).sum(axis=0).astype(BF)
        spread = jnp.broadcast_to(total[None], parts.shape)
        spread = lax.all_to_all(
            spread, AXES, split_axis=0, concat_axis=0, axis_index_groups=groups, tiled=True
        )
        mine = spread.reshape(half, 8, 128)
        other = lax.ppermute(mine, "gx", swap)
        first = jnp.where(core == 0, mine, other)
        second = jnp.where(core == 0, other, mine)
        whole = jnp.concatenate([first, second], axis=0)

        full = []
        start = 0
        for (g, width), t in zip(grads, tiles):
            full.append(from_tiles(whole[start : start + t.shape[0]], g.shape[0], width))
            start += t.shape[0]
        full_top, full_mid, full_bot, full_enc = full
        (full_enc,) = call(finish_kernel, [((64, 864), F32)], [], 0, full_enc)
        mine_bot = full_bot.reshape(3, ngx, block, -1)
        mine_bot = lax.dynamic_index_in_dim(mine_bot, gx, 1, keepdims=False)
        mine_bot = mine_bot.reshape(3 * block, -1)
        return (
            feat.transpose(1, 0, 2),
            grad_skip.transpose(1, 0, 2),
            full_enc,
            full_gradient(mine_bot),
            full_gradient(full_mid),
            full_gradient(full_top),
        )

    in_specs = (P(None, "gx", "gy"), P(), P("gx", None), P(), P(), P(None, "gx", "gy"))
    out_specs = (P(None, "gx", "gy"), P(None, "gx", "gy"), P(), P("gx", None), P(), P())
    return jax.shard_map(step, mesh=mesh, in_specs=in_specs, out_specs=out_specs, check_vma=False)
```

```python
import math

import jax
import jax.numpy as jnp
import numpy as np
from jax import lax
from jax.experimental import pallas as pl
from jax.experimental.pallas import tpu as pltpu
from jax.sharding import PartitionSpec as P

AXES = ("gx", "gy")
BF = jnp.bfloat16
F32 = jnp.float32


def columns(lanes, depth, split):
    col = np.arange(lanes) // depth
    return np.where(col >= split, col - lanes // depth, col), np.arange(lanes) % depth


def upsampling(coarse, fine):
    (col_c, z_c), (col_f, z_f) = (columns(*coarse), columns(*fine))
    hit = (col_c[:, None] == col_f[None, :] // 2) & (z_c[:, None] == z_f[None, :] // 2)
    return hit.astype(np.float32)


TOP = (384, 16, 20)
WIDE = (256, 8, 16)
MID = (128, 8, 12)
LOW = (128, 4, 16)


def constants():
    low_mid = upsampling(LOW, MID)
    mid_top = upsampling(MID, TOP)
    wide_low = upsampling(LOW, WIDE).T / 8.0
    tile_pool = mid_top[:64, :256].T / 8.0
    tile_pool = np.concatenate([tile_pool, tile_pool], axis=1)
    return {
        "up_low": low_mid,
        "sum_low": low_mid.T,
        "up_mid": mid_top,
        "sum_mid": mid_top.T,
        "pool_low": wide_low,
        "pool_tile": tile_pool,
    }


def dot(a, b):
    return jnp.dot(a, b, preferred_element_type=F32)


def dot_nt(a, b):
    return lax.dot_general(a, b, (((1,), (1,)), ((), ())), preferred_element_type=F32)


def dot_split(a, b):
    head = a.astype(BF)
    rest = (a - head.astype(F32)).astype(BF)
    return dot(head, b) + dot(rest, b)


def loop(count, body, unroll=1):
    def step(i, carry):
        for u in range(unroll):
            body(i * unroll + u)
        return carry

    if unroll == count:
        step(0, 0)
    else:
        lax.fori_loop(0, count // unroll, step, 0)


def lane(length):
    return lax.broadcasted_iota(jnp.int32, (1, length), 1)


def inside(region, tile_cols, total_cols, index):
    lanes, depth, split = region
    col = lane(lanes) // depth
    col = jnp.where(col >= split, col - lanes // depth, col) + index * tile_cols
    return jnp.where((col >= 0) & (col < total_cols), 1.0, 0.0)


def row_ok(row, total):
    return jnp.where((row >= 0) & (row < total), 1.0, 0.0)


def depth_masks(shape, depth):
    z = lax.broadcasted_iota(jnp.int32, shape, 1) % depth
    below = jnp.where(z == depth - 1, 0.0, 1.0).astype(BF)
    above = jnp.where(z == 0, 0.0, 1.0).astype(BF)
    return below, above


def put_taps(dst, row, first, width, value, depth):
    chans, lanes = value.shape
    below, above = depth_masks(value.shape, depth)
    kinds = (value * below, value, value * above)
    for b in range(3):
        for e in range(3):
            shift = (b - 1) * depth + (e - 1)
            piece = kinds[e]
            if shift:
                piece = pltpu.roll(piece, (-shift) % lanes, 1)
            start = (3 * b + e) * width + first
            dst[row, start : start + chans, :] = piece


def sigmoid(v):
    return 1.0 / (1.0 + jnp.exp(-v))


def silu(v):
    return v * sigmoid(v)


def slope(v):
    s = sigmoid(v)
    return s * (1.0 + v * (1.0 - s))


def row_sum(ref, row, chans):
    return (
        ref[row, 0:chans, :]
        + ref[row + 1, chans : 2 * chans, :]
        + ref[row + 2, 2 * chans : 3 * chans, :]
    )


def put_padded(out, row, value):
    rows, width = value.shape
    out[row : row + rows, 0:width] = value.astype(BF)
    out[row : row + rows, width:] = jnp.zeros((rows, out.shape[1] - width), BF)


def pool_kernel(skip, cot, pool_tile, to_left, to_right):
    for r in range(4):
        to_left[r] = skip[r, :, 0:128]
        to_left[4 + r] = cot[r, :, 0:128]
        to_right[r] = skip[r, :, 128:256]
        to_right[4 + r] = cot[r, :, 128:256]
    for q in range(2):
        pooled = dot(skip[2 * q], pool_tile[...]) + dot(skip[2 * q + 1], pool_tile[...])
        pooled = pooled.astype(BF)
        to_left[8 + q] = pooled
        to_right[8 + q] = pooled


def widen_kernel(skip, cot, own, right, left, out):
    first = jnp.where(lax.broadcasted_iota(jnp.int32, (32, 128), 1) < 64, 1.0, 0.0)
    head = first.astype(BF)
    tail = (1.0 - first).astype(BF)
    for r in range(4):
        for k, tile in enumerate((skip, cot)):
            base = 12 * k + 3 * r
            out[base] = tile[r, :, 0:128]
            out[base + 1] = tile[r, :, 128:256]
            out[base + 2] = right[4 * k + r] * head + left[4 * k + r] * tail
    for q in range(2):
        out[24 + 2 * q] = own[8 + q] * head + right[8 + q] * tail
        out[25 + 2 * q] = left[8 + q] * tail


def gather_kernel(tiles, block, *refs):
    (ids, own, up, down, far_up, far_down, mate, beyond, w_mine, w_mate) = refs[:10]
    (fine, pools, w_out, w_all, w_flat) = refs[10:15]
    gx = ids[0]
    core = gx % 2
    low = jnp.where(core == 0, 1.0, 0.0)
    below = jnp.full((24, 32, 128), low).astype(BF)
    above = jnp.full((24, 32, 128), 1.0 - low).astype(BF)
    first = beyond[0:24] * below + mate[0:24] * above
    last = mate[0:24] * below + beyond[0:24] * above
    fine[0] = first
    fine[1] = last

    for place, (ref, at) in (
        (1, (far_up, 0)),
        (3, (up, 24)),
        (5, (own, 24)),
        (7, (down, 24)),
        (9, (far_down, 0)),
    ):
        pools[place] = ref[at : at + 4]
    centre = 6 - 2 * core
    pools[centre - 2] = beyond[24:28]
    pools[centre] = mate[24:28]
    pools[centre + 2] = beyond[28:32]
    pools[centre - 4 + 8 * core] = beyond[32:36]

    slabs = w_all.shape[1]
    around = tiles // 4
    y = (gx // 2) % around
    side = gx // (2 * around)
    for lane_core, ref in ((core, w_mine), (1 - core, w_mate)):
        for far in range(2):
            for k in range(around):
                z_part = (side + far) % 2
                y_part = (y + around - k) % around
                at = (far * around + k) * slabs
                w_all[(z_part * around + y_part) * 2 + lane_core] = ref[at : at + slabs]
    lanes = w_flat.shape[1] // 128
    for b in range(tiles):
        rows = w_all[b].reshape(lanes * block, 128)
        for l in range(lanes):
            w_flat[b * block : b * block + block, 128 * l : 128 * l + 128] = rows[
                l * block : l * block + block
            ]
    put_forward(w_flat, w_out)


def put_forward(w, out):
    rows = w.shape[0]
    width = out.shape[1]
    for a in range(3):
        out[rows * a : rows * a + rows, :] = w[:, a * width : (a + 1) * width]


def put_backward(w, out):
    chans = out.shape[0] // 3
    i = lax.broadcasted_iota(jnp.int32, (chans, chans), 0)
    j = lax.broadcasted_iota(jnp.int32, (chans, chans), 1)
    unit = jnp.where(i == j, 1.0, 0.0).astype(BF)
    for a in range(3):
        taps = [26 - 9 * a - k for k in range(9)]
        stacked = jnp.concatenate([w[:, t * chans : t * chans + chans] for t in taps], axis=0)
        out[chans * a : chans * a + chans, :] = dot_nt(unit, stacked).astype(BF)


def weight_kernel(forward, backward, *refs):
    sources, outs = refs[: len(forward)], refs[len(forward) :]
    k = 0
    for w, fwd, bwd in zip(sources, forward, backward):
        if fwd:
            put_forward(w, outs[k])
            k += 1
        if bwd:
            put_backward(w, outs[k])
            k += 1


def main_kernel(sizes, scales, *refs):
    (ids, own, fine, pools) = refs[:4]
    up, down = fine.at[0], fine.at[1]
    (w_enc, w_bot, w_mid, w_top, t_top, t_mid) = refs[4:10]
    (up_low, sum_low, up_mid, sum_mid, pool_low) = refs[10:15]
    (feat, dskip, packed, pre_one, taps_out, g_top, g_mid, g_bot) = refs[15:23]
    (pool_s, taps_a, sum_a, act_a, taps_b, sum_b, act_b) = refs[23:30]
    (taps_c, sum_c, act_c, pre_c, taps_d, sum_d, err_d) = refs[30:37]
    (taps_e, sum_e, err_c, stack, taps_f, sum_f) = refs[37:43]
    (rows_all, cols_all) = sizes
    (scale_top, scale_mid, scale_low) = scales
    gx, gy = ids[0], ids[1]
    rows_mid, rows_low = rows_all // 2, rows_all // 4

    for k in range(16):
        tile, slab = 5 + (k - 7) // 2, 2 * ((k - 7) % 2)
        pool_s[k, :, 0:128] = pools[tile, slab]
        pool_s[k, :, 128:256] = pools[tile, slab + 1]

    def enc_taps(k):
        put_taps(taps_a, k, 0, 32, pool_s[k], 8)
        sum_a[k] = dot(w_enc[...], taps_a[k])

    loop(16, enc_taps, 4)
    wide_in = inside(WIDE, 8, cols_all // 2, gy)

    def enc_act(k):
        value = silu(row_sum(sum_a, k, 64)) * (wide_in * row_ok(gx * 2 + k - 6, rows_mid))
        act_a[k] = value.astype(BF)

    loop(14, enc_act, 2)
    for m in range(4):
        pre = row_sum(sum_a, m + 5, 64)
        pre_one[m] = jnp.where(lane(128) < 96, pre[:, 0:128], pre[:, 128:256])
        taps_out[m] = taps_a[m + 6, :, 0:128]

    def low_taps(k):
        pooled = dot(act_a[2 * k], pool_low[...]) + dot(act_a[2 * k + 1], pool_low[...])
        put_taps(taps_b, k, 0, 64, pooled.astype(BF), 4)
        sum_b[k] = dot(w_bot[...], taps_b[k])

    loop(7, low_taps, 7)
    low_in = inside(LOW, 4, cols_all // 4, gy)
    mid_in = inside(MID, 8, cols_all // 2, gy)
    pick = jnp.where(lax.broadcasted_iota(jnp.int32, (64, 128), 1) < 96, 1.0, 0.0)
    near = pick.astype(BF)
    away = (1.0 - pick).astype(BF)

    def low_act(k):
        value = silu(row_sum(sum_b, k, 128)) * (low_in * row_ok(gx + k - 2, rows_low))
        act_b[k] = dot(value.astype(BF), up_low[...]).astype(BF)

    loop(5, low_act, 5)

    def mid_taps(k):
        put_taps(taps_c, k, 0, 192, act_b[(k + 1) // 2], 8)
        narrow = act_a[k + 3, :, 0:128] * near + act_a[k + 3, :, 128:256] * away
        put_taps(taps_c, k, 128, 192, narrow, 8)
        sum_c[k] = dot(w_mid[...], taps_c[k])

    loop(8, mid_taps, 2)

    def mid_act(k):
        pre = row_sum(sum_c, k, 64)
        pre_c[k] = pre
        value = silu(pre) * (mid_in * row_ok(gx * 2 + k - 2, rows_mid))
        act_c[k] = dot(value.astype(BF), up_mid[...]).astype(BF)

    loop(6, mid_act, 6)

    def skip_row(kind, k):
        part = (up, own, down)[k // 4]
        base = 12 * kind + 3 * (k % 4)
        return jnp.concatenate([part[base], part[base + 1], part[base + 2]], axis=1)

    for k in range(12):
        put_taps(taps_d, k, 64, 96, skip_row(0, k), 16)

    def top_taps(j):
        for half in range(2):
            put_taps(taps_d, 2 * j + half, 0, 96, act_c[j], 16)
            sum_d[2 * j + half] = dot(w_top[...], taps_d[2 * j + half])

    loop(6, top_taps, 2)
    for k in range(10):
        pre = row_sum(sum_d, k, 32)
        s = sigmoid(pre)
        if 3 <= k < 7:
            feat[k - 3] = (pre * s)[:, 0:256].astype(BF)
        cot = skip_row(1, k + 1).astype(F32)
        err_d[k] = (cot * (s * (1.0 + pre * (1.0 - s)))).astype(BF)

    def top_back(k):
        put_taps(taps_e, k, 0, 32, err_d[k], 16)
        sum_e[k] = dot(t_top[...], taps_e[k])

    loop(10, top_back, 2)

    total = None
    for k in range(6):
        parts = []
        for a in range(3):
            r = k - a
            own_row = 0 <= r < 4
            parts.append(err_d[r + 3, :, 0:256] if own_row else jnp.zeros((32, 256), BF))
        term = dot_nt(jnp.concatenate(parts, axis=0), taps_d[k + 3, :, 0:256])
        total = term if total is None else total + term
    put_padded(g_top, 0, total * scale_top)

    def mid_err(m):
        one = row_sum(sum_e, 2 * m, 96)
        two = row_sum(sum_e, 2 * m + 1, 96)
        whole = dot_split(one[0:64] + two[0:64], sum_mid[...])
        keep = mid_in * row_ok(gx * 2 + m - 1, rows_mid)
        err_c[m] = (whole * slope(pre_c[m + 1]) * keep).astype(BF)

    loop(4, mid_err, 4)
    for r in range(4):
        dskip[r] = row_sum(sum_e, r + 2, 96)[64:96, 0:256]

    def mid_back(m):
        put_taps(taps_f, m, 0, 64, err_c[m], 8)
        sum_f[m] = dot(t_mid[...], taps_f[m])

    loop(4, mid_back, 2)
    own_mid = jnp.where(lax.broadcasted_iota(jnp.int32, (64, 128), 1) < 64, 1.0, 0.0).astype(BF)
    for k in range(4):
        for a in range(3):
            r = k - a
            piece = err_c[r + 1] * own_mid if 0 <= r < 2 else jnp.zeros((64, 128), BF)
            stack[k, 64 * a : 64 * a + 64, :] = piece
    total = None
    for k in range(4):
        term = dot_nt(stack[k], taps_c[k + 2])
        total = term if total is None else total + term
    put_padded(g_mid, 0, total * scale_mid)

    one = row_sum(sum_f, 0, 192)
    two = row_sum(sum_f, 1, 192)
    whole = dot_split(one[0:128] + two[0:128], sum_low[...])
    keep = jnp.where(lane(128) < 16, 1.0, 0.0)
    err_low = (whole * slope(row_sum(sum_b, 2, 128)) * keep).astype(BF)
    packed[0:128, :] = err_low
    both = jnp.where(lane(128) < 64, one[128:192], pltpu.roll(two[128:192], 64, 1))
    packed[128:192, :] = both.astype(BF)
    for a in range(3):
        put_padded(g_bot, 128 * a, dot_nt(err_low, taps_b[a + 2]) * scale_low)


def tail_kernel(sizes, scale_mid, *refs):
    (ids, own, up_two, down_two, mate, beyond, pre_one, taps_in, dskip) = refs[:9]
    (t_bot, t_enc, up_low, up_mid) = refs[9:13]
    (grad_skip, g_enc) = refs[13:15]
    (taps_a, sum_a, err_s, taps_b, sum_b, near) = refs[15:21]
    (rows_all, cols_all) = sizes
    gx, gy = ids[0], ids[1]
    rows_mid = rows_all // 2
    mid_in = inside(MID, 8, cols_all // 2, gy)

    below = jnp.full((3, 192, 128), jnp.where(gx % 2 == 0, 1.0, 0.0)).astype(BF)
    above = (1.0 - below.astype(F32)).astype(BF)
    near[0] = beyond[...] * below + mate[...] * above
    near[1] = mate[...] * below + beyond[...] * above
    up, down = near.at[0], near.at[1]

    for k, ref in enumerate((up_two, up, own, down, down_two)):
        value = (
            ref[0, 0:128, :].astype(F32)
            + pltpu.roll(ref[2, 0:128, :].astype(F32), 16, 1)
            + pltpu.roll(ref[1, 0:128, :].astype(F32), 112, 1)
        )
        put_taps(taps_a, k, 0, 128, value.astype(BF), 4)
        sum_a[k] = dot(t_bot[...], taps_a[k])
    ups = [dot_split(row_sum(sum_a, k, 64), up_low[...]) * 0.125 for k in range(3)]
    for m in range(4):
        ref = (up, own, own, down)[m]
        odd = m % 2 == 0
        tiles = [ref[k, 128:192, :].astype(F32) for k in range(3)]
        mine, left, right = tiles
        if odd:
            mine = pltpu.roll(mine, 64, 1)
        else:
            left, right = pltpu.roll(left, 64, 1), pltpu.roll(right, 64, 1)
        at = lane(128)
        part = jnp.where(at < 64, mine, jnp.where(at < 96, right, left))
        keep = mid_in * row_ok(gx * 2 + m - 1, rows_mid)
        err = (part + ups[(m + 1) // 2]) * slope(pre_one[m]) * keep
        err = err.astype(BF)
        err_s[m] = err
        put_taps(taps_b, m, 0, 64, err, 8)
        sum_b[m] = dot(t_enc[...], taps_b[m])
    own_mid = jnp.where(lax.broadcasted_iota(jnp.int32, (64, 128), 1) < 64, 1.0, 0.0).astype(BF)
    total = None
    for k in range(4):
        parts = []
        for a in range(3):
            r = k - a
            parts.append(err_s[r + 1] * own_mid if 0 <= r < 2 else jnp.zeros((64, 128), BF))
        term = dot_nt(jnp.concatenate(parts, axis=0), taps_in[k])
        total = term if total is None else total + term
    total = (total * scale_mid).astype(BF)
    g_enc[0:192, :] = total[:, 0:128]
    g_enc[192:384, :] = total[:, 128:256]
    rest = [total[48 * q : 48 * q + 48, 256:288] for q in range(4)]
    g_enc[384:432, :] = jnp.concatenate(rest, axis=1)
    for q in range(2):
        fine = dot_split(row_sum(sum_b, q, 32), up_mid[:, 0:256]) * 0.125
        for half in range(2):
            r = 2 * q + half
            grad_skip[r] = (dskip[r] + fine).astype(BF)


def finish_kernel(g, out):
    rest = jnp.concatenate([g[384:432, 32 * q : 32 * q + 32] for q in range(4)], axis=0)
    pieces = []
    for a in range(3):
        at = 64 * a
        pieces += [g[at : at + 64, :], g[192 + at : 256 + at, :], rest[at : at + 64, :]]
    out[...] = jnp.concatenate(pieces, axis=1).astype(F32)


VMEM = pl.BlockSpec(memory_space=pltpu.VMEM)
SMEM = pl.BlockSpec(memory_space=pltpu.SMEM)


def call(kernel, outs, scratch, scalars, *args, cost=1, grant=8):
    return pl.pallas_call(
        kernel,
        out_shape=[jax.ShapeDtypeStruct(s, d) for s, d in outs],
        in_specs=[SMEM] * scalars + [VMEM] * (len(args) - scalars),
        out_specs=[VMEM] * len(outs),
        scratch_shapes=[pltpu.VMEM(s, d) for s, d in scratch],
        compiler_params=pltpu.CompilerParams(vmem_limit_bytes=grant * 1024 * 1024),
        cost_estimate=pl.CostEstimate(
            flops=cost * 500_000_000, bytes_accessed=cost * 1_000_000, transcendentals=0
        ),
    )(*args)


def shift(value, axis, count, step):
    return lax.ppermute(value, axis, [(i, i + step) for i in range(count) if 0 <= i + step < count])


def tiles_of(g):
    rows, width = g.shape
    return g.reshape(rows // 8, 8, width // 128, 128).transpose(0, 2, 1, 3).reshape(-1, 8, 128)


def from_tiles(tiles, rows, width):
    wide = -(-width // 128)
    g = tiles.reshape(rows // 8, wide, 8, 128).transpose(0, 2, 1, 3).reshape(rows, wide * 128)
    return g[:, :width]


def full_gradient(g):
    rows, _ = g.shape
    out = rows // 3
    return jnp.concatenate([g[out * a : out * a + out] for a in range(3)], axis=1).astype(F32)


def solution(mesh):
    ngx, ngy = mesh.shape["gx"], mesh.shape["gy"]
    devices = ngx * ngy
    const = {k: np.asarray(v) for k, v in constants().items()}

    def step(skip_input, w_encoder, w_bottom, w_middle, w_upper, cotangent):
        gx, gy = lax.axis_index("gx"), lax.axis_index("gy")
        ids = jnp.stack([gx, gy]).astype(jnp.int32)
        rows_all, cols_all = 4 * ngx, 16 * ngy
        sizes = (rows_all, cols_all)
        cells = rows_all * cols_all * 16
        scales = tuple(1.0 / math.sqrt(cells // k) for k in (1, 8, 64))
        c = {k: jnp.asarray(v, BF) for k, v in const.items()}

        block, width = w_bottom.shape
        slabs = block * 2048 // 4096
        weight = jnp.pad(w_bottom, ((0, 0), (0, 2048 - width)))
        lanes = weight.shape[1] // 128
        weight = weight.reshape(block, lanes, 128).transpose(1, 0, 2).reshape(slabs, 32, 128)

        swap = [(i, i ^ 1) for i in range(ngx)]
        around = ngx // 4

        def along_y(i, k):
            side, y, core = i // (2 * around), i // 2 % around, i % 2
            return (side * around + (y + k) % around) * 2 + core

        part = ngy // 4 if ngy % 4 == 0 else ngy

        def mirrored(i):
            x, y = i // ngy, i % ngy
            y = (ngy // part - 1 - y // part) * part + y % part
            return (x + ngx // 2) % ngx * ngy + y

        w_line = [weight]
        for k in range(1, around):
            w_line.append(lax.ppermute(weight, "gx", [(i, along_y(i, k)) for i in range(ngx)]))
        w_line = jnp.concatenate(w_line, axis=0)
        w_far = lax.ppermute(w_line, AXES, [(i, mirrored(i)) for i in range(devices)])
        w_mine = jnp.concatenate([w_line, w_far], axis=0)
        w_mate = lax.ppermute(w_mine, "gx", swap)

        skip = skip_input.transpose(1, 0, 2)
        cot = cotangent.transpose(1, 0, 2)
        to_left, to_right = call(
            pool_kernel, [((10, 32, 128), BF)] * 2, [], 0, skip, cot, c["pool_tile"]
        )
        right = shift(to_left, "gy", ngy, -1)
        left = shift(to_right, "gy", ngy, 1)
        (own,) = call(widen_kernel, [((28, 32, 128), BF)], [], 0, skip, cot, to_left, right, left)
        core = gx % 2
        up = shift(own, "gx", ngx, 2)
        down = shift(own, "gx", ngx, -2)
        far_up = shift(own[24:28], "gx", ngx, 4)
        far_down = shift(own[24:28], "gx", ngx, -4)
        mate = lax.ppermute(own, "gx", swap)
        beyond = [
            jnp.where(core == 0, down[0:24], up[0:24]),
            up[24:28],
            down[24:28],
            jnp.where(core == 0, far_down, far_up),
        ]
        beyond = lax.ppermute(jnp.concatenate(beyond, axis=0), "gx", swap)
        fine, pools, w_bot, _, w_flat = call(
            lambda *refs: gather_kernel(ngx, block, *refs),
            [
                ((2, 24, 32, 128), BF),
                ((11, 4, 32, 128), BF),
                ((384, 576), BF),
                ((ngx, slabs, 32, 128), BF),
                ((ngx * block, lanes * 128), BF),
            ],
            [],
            1,
            ids,
            own,
            up,
            down,
            far_up,
            far_down,
            mate,
            beyond,
            w_mine,
            w_mate,
        )
        w_enc, t_enc, w_mid, t_mid, w_top, t_top = call(
            lambda *refs: weight_kernel((1, 1, 1), (1, 1, 1), *refs),
            [
                ((192, 288), BF),
                ((96, 576), BF),
                ((192, 1728), BF),
                ((576, 576), BF),
                ((96, 864), BF),
                ((288, 288), BF),
            ],
            [],
            0,
            w_encoder,
            w_middle,
            w_upper,
            cost=4,
        )
        (t_bot,) = call(
            lambda *refs: weight_kernel((0,), (1,), *refs),
            [((192, 1152), BF)],
            [],
            0,
            w_flat,
            cost=2,
        )

        outs = [
            ((4, 32, 256), BF),
            ((4, 32, 256), F32),
            ((192, 128), BF),
            ((4, 64, 128), F32),
            ((4, 288, 128), BF),
            ((96, 896), BF),
            ((192, 1792), BF),
            ((384, 640), BF),
        ]
        scratch = [
            ((16, 32, 256), BF),
            ((16, 288, 256), BF),
            ((16, 192, 256), F32),
            ((14, 64, 256), BF),
            ((7, 576, 128), BF),
            ((7, 384, 128), F32),
            ((5, 128, 128), BF),
            ((8, 1728, 128), BF),
            ((8, 192, 128), F32),
            ((6, 64, 384), BF),
            ((6, 64, 128), F32),
            ((12, 864, 384), BF),
            ((12, 96, 384), F32),
            ((10, 32, 384), BF),
            ((10, 288, 384), BF),
            ((10, 288, 384), F32),
            ((4, 64, 128), BF),
            ((4, 192, 128), BF),
            ((4, 576, 128), BF),
            ((4, 576, 128), F32),
        ]
        feat, dskip, packed, pre_one, taps_one, g_top, g_mid, g_bot = call(
            lambda *refs: main_kernel(sizes, scales, *refs),
            outs,
            scratch,
            1,
            ids,
            own,
            fine,
            pools,
            w_enc,
            w_bot,
            w_mid,
            w_top,
            t_top,
            t_mid,
            c["up_low"],
            c["sum_low"],
            c["up_mid"],
            c["sum_mid"],
            c["pool_low"],
            cost=20,
            grant=33,
        )

        from_left = shift(packed, "gy", ngy, 1)
        from_right = shift(packed, "gy", ngy, -1)
        line = jnp.stack([packed, from_left, from_right])
        mate = lax.ppermute(line, "gx", swap)
        line_up = shift(line, "gx", ngx, 2)
        line_down = shift(line, "gx", ngx, -2)
        beyond = lax.ppermute(jnp.where(core == 0, line_down, line_up), "gx", swap)
        grad_skip, g_enc = call(
            lambda *refs: tail_kernel(sizes, scales[1], *refs),
            [((4, 32, 256), BF), ((432, 128), BF)],
            [
                ((5, 1152, 128), BF),
                ((5, 192, 128), F32),
                ((4, 64, 128), BF),
                ((4, 576, 128), BF),
                ((4, 96, 128), F32),
                ((2, 3, 192, 128), BF),
            ],
            1,
            ids,
            line,
            line_up,
            line_down,
            mate,
            beyond,
            pre_one,
            taps_one,
            dskip,
            t_bot,
            t_enc,
            c["up_low"],
            c["up_mid"],
            cost=4,
        )

        grads = ((g_top, 864), (g_mid, 1728), (g_bot, 576), (g_enc, 128))
        tiles = [tiles_of(g) for g, _ in grads]
        spare = -sum(t.shape[0] for t in tiles) % devices
        flat = jnp.concatenate(tiles + [jnp.zeros((spare, 8, 128), BF)], axis=0)
        half = flat.shape[0] // 2
        keep = lax.dynamic_slice_in_dim(flat, core * half, half, 0)
        other = lax.dynamic_slice_in_dim(flat, (1 - core) * half, half, 0)
        other = lax.ppermute(other, "gx", swap)
        mine = (keep.astype(F32) + other.astype(F32)).astype(BF)
        parts = mine.reshape(devices // 2, -1, 128)
        groups = [[i for i in range(devices) if i // ngy % 2 == k] for k in range(2)]
        parts = lax.all_to_all(
            parts, AXES, split_axis=0, concat_axis=0, axis_index_groups=groups, tiled=True
        )
        total = parts.astype(F32).sum(axis=0).astype(BF)
        spread = jnp.broadcast_to(total[None], parts.shape)
        spread = lax.all_to_all(
            spread, AXES, split_axis=0, concat_axis=0, axis_index_groups=groups, tiled=True
        )
        mine = spread.reshape(half, 8, 128)
        other = lax.ppermute(mine, "gx", swap)
        first = jnp.where(core == 0, mine, other)
        second = jnp.where(core == 0, other, mine)
        whole = jnp.concatenate([first, second], axis=0)

        full = []
        start = 0
        for (g, width), t in zip(grads, tiles):
            full.append(from_tiles(whole[start : start + t.shape[0]], g.shape[0], width))
            start += t.shape[0]
        full_top, full_mid, full_bot, full_enc = full
        (full_enc,) = call(finish_kernel, [((64, 864), F32)], [], 0, full_enc)
        mine_bot = full_bot.reshape(3, ngx, block, -1)
        mine_bot = lax.dynamic_index_in_dim(mine_bot, gx, 1, keepdims=False)
        mine_bot = mine_bot.reshape(3 * block, -1)
        return (
            feat.transpose(1, 0, 2),
            grad_skip.transpose(1, 0, 2),
            full_enc,
            full_gradient(mine_bot),
            full_gradient(full_mid),
            full_gradient(full_top),
        )

    in_specs = (P(None, "gx", "gy"), P(), P("gx", None), P(), P(), P(None, "gx", "gy"))
    out_specs = (P(None, "gx", "gy"), P(None, "gx", "gy"), P(), P("gx", None), P(), P())
    return jax.shard_map(step, mesh=mesh, in_specs=in_specs, out_specs=out_specs, check_vma=False)
```

```python
import math

import jax
import jax.numpy as jnp
import numpy as np
from jax import lax
from jax.experimental import pallas as pl
from jax.experimental.pallas import tpu as pltpu
from jax.sharding import PartitionSpec as P

AXES = ("gx", "gy")
BF = jnp.bfloat16
F32 = jnp.float32


def columns(lanes, depth, split):
    col = np.arange(lanes) // depth
    return np.where(col >= split, col - lanes // depth, col), np.arange(lanes) % depth


def upsampling(coarse, fine):
    (col_c, z_c), (col_f, z_f) = (columns(*coarse), columns(*fine))
    hit = (col_c[:, None] == col_f[None, :] // 2) & (z_c[:, None] == z_f[None, :] // 2)
    return hit.astype(np.float32)


TOP = (384, 16, 20)
WIDE = (256, 8, 16)
MID = (128, 8, 12)
LOW = (128, 4, 16)


def constants():
    low_mid = upsampling(LOW, MID)
    mid_top = upsampling(MID, TOP)
    wide_low = upsampling(LOW, WIDE).T / 8.0
    tile_pool = mid_top[:64, :256].T / 8.0
    tile_pool = np.concatenate([tile_pool, tile_pool], axis=1)
    return {
        "up_low": low_mid,
        "sum_low": low_mid.T,
        "up_mid": mid_top,
        "sum_mid": mid_top.T,
        "pool_low": wide_low,
        "pool_tile": tile_pool,
    }


def dot(a, b):
    return jnp.dot(a, b, preferred_element_type=F32)


def dot_nt(a, b):
    return lax.dot_general(a, b, (((1,), (1,)), ((), ())), preferred_element_type=F32)


def dot_split(a, b):
    head = a.astype(BF)
    rest = (a - head.astype(F32)).astype(BF)
    return dot(head, b) + dot(rest, b)


def loop(count, body, unroll=1):
    def step(i, carry):
        for u in range(unroll):
            body(i * unroll + u)
        return carry

    if unroll == count:
        step(0, 0)
    else:
        lax.fori_loop(0, count // unroll, step, 0)


def lane(length):
    return lax.broadcasted_iota(jnp.int32, (1, length), 1)


def inside(region, tile_cols, total_cols, index):
    lanes, depth, split = region
    col = lane(lanes) // depth
    col = jnp.where(col >= split, col - lanes // depth, col) + index * tile_cols
    return jnp.where((col >= 0) & (col < total_cols), 1.0, 0.0)


def row_ok(row, total):
    return jnp.where((row >= 0) & (row < total), 1.0, 0.0)


def depth_masks(shape, depth):
    z = lax.broadcasted_iota(jnp.int32, shape, 1) % depth
    below = jnp.where(z == depth - 1, 0.0, 1.0).astype(BF)
    above = jnp.where(z == 0, 0.0, 1.0).astype(BF)
    return below, above


def put_taps(dst, row, first, width, value, depth):
    chans, lanes = value.shape
    below, above = depth_masks(value.shape, depth)
    kinds = (value * below, value, value * above)
    for b in range(3):
        for e in range(3):
            shift = (b - 1) * depth + (e - 1)
            piece = kinds[e]
            if shift:
                piece = pltpu.roll(piece, (-shift) % lanes, 1)
            start = (3 * b + e) * width + first
            dst[row, start : start + chans, :] = piece


def sigmoid(v):
    return 1.0 / (1.0 + jnp.exp(-v))


def silu(v):
    return v * sigmoid(v)


def slope(v):
    s = sigmoid(v)
    return s * (1.0 + v * (1.0 - s))


def row_sum(ref, row, chans):
    return (
        ref[row, 0:chans, :]
        + ref[row + 1, chans : 2 * chans, :]
        + ref[row + 2, 2 * chans : 3 * chans, :]
    )


def put_padded(out, row, value):
    rows, width = value.shape
    out[row : row + rows, 0:width] = value.astype(BF)
    out[row : row + rows, width:] = jnp.zeros((rows, out.shape[1] - width), BF)


def pool_kernel(skip, cot, pool_tile, to_left, to_right):
    for r in range(4):
        to_left[r] = skip[r, :, 0:128]
        to_left[4 + r] = cot[r, :, 0:128]
        to_right[r] = skip[r, :, 128:256]
        to_right[4 + r] = cot[r, :, 128:256]
    for q in range(2):
        pooled = dot(skip[2 * q], pool_tile[...]) + dot(skip[2 * q + 1], pool_tile[...])
        pooled = pooled.astype(BF)
        to_left[8 + q] = pooled
        to_right[8 + q] = pooled


def widen_kernel(skip, cot, own, right, left, out):
    first = jnp.where(lax.broadcasted_iota(jnp.int32, (32, 128), 1) < 64, 1.0, 0.0)
    head = first.astype(BF)
    tail = (1.0 - first).astype(BF)
    for r in range(4):
        for k, tile in enumerate((skip, cot)):
            base = 12 * k + 3 * r
            out[base] = tile[r, :, 0:128]
            out[base + 1] = tile[r, :, 128:256]
            out[base + 2] = right[4 * k + r] * head + left[4 * k + r] * tail
    for q in range(2):
        out[24 + 2 * q] = own[8 + q] * head + right[8 + q] * tail
        out[25 + 2 * q] = left[8 + q] * tail


def gather_kernel(tiles, block, *refs):
    (ids, own, up, down, far_up, far_down, mate, beyond, w_mine, w_mate) = refs[:10]
    (fine, pools, w_out, w_all, w_flat) = refs[10:15]
    gx = ids[0]
    core = gx % 2
    low = jnp.where(core == 0, 1.0, 0.0)
    below = jnp.full((12, 32, 128), low).astype(BF)
    above = jnp.full((12, 32, 128), 1.0 - low).astype(BF)
    fine[0, 0:12] = up[0:12] * below + mate[0:12] * above
    fine[0, 12:24] = beyond[0:12] * below + mate[12:24] * above
    fine[1, 0:12] = mate[0:12] * below + beyond[0:12] * above
    fine[1, 12:24] = mate[12:24] * below + down[0:12] * above

    for place, (ref, at) in (
        (1, (far_up, 0)),
        (3, (up, 12)),
        (5, (own, 24)),
        (7, (down, 12)),
        (9, (far_down, 0)),
    ):
        pools[place] = ref[at : at + 4]
    centre = 6 - 2 * core
    pools[centre - 2] = beyond[12:16]
    pools[centre] = mate[24:28]
    pools[centre + 2] = beyond[16:20]
    pools[centre - 4 + 8 * core] = beyond[20:24]

    slabs = w_all.shape[1]
    around = tiles // 4
    y = (gx // 2) % around
    side = gx // (2 * around)
    for lane_core, ref in ((core, w_mine), (1 - core, w_mate)):
        for far in range(2):
            for k in range(around):
                z_part = (side + far) % 2
                y_part = (y + around - k) % around
                at = (far * around + k) * slabs
                w_all[(z_part * around + y_part) * 2 + lane_core] = ref[at : at + slabs]
    lanes = w_flat.shape[1] // 128
    for b in range(tiles):
        rows = w_all[b].reshape(lanes * block, 128)
        for l in range(lanes):
            w_flat[b * block : b * block + block, 128 * l : 128 * l + 128] = rows[
                l * block : l * block + block
            ]
    put_forward(w_flat, w_out)


def put_forward(w, out):
    rows = w.shape[0]
    width = out.shape[1]
    for a in range(3):
        out[rows * a : rows * a + rows, :] = w[:, a * width : (a + 1) * width]


def put_backward(w, out):
    chans = out.shape[0] // 3
    i = lax.broadcasted_iota(jnp.int32, (chans, chans), 0)
    j = lax.broadcasted_iota(jnp.int32, (chans, chans), 1)
    unit = jnp.where(i == j, 1.0, 0.0).astype(BF)
    for a in range(3):
        taps = [26 - 9 * a - k for k in range(9)]
        stacked = jnp.concatenate([w[:, t * chans : t * chans + chans] for t in taps], axis=0)
        out[chans * a : chans * a + chans, :] = dot_nt(unit, stacked).astype(BF)


def weight_kernel(forward, backward, *refs):
    sources, outs = refs[: len(forward)], refs[len(forward) :]
    k = 0
    for w, fwd, bwd in zip(sources, forward, backward):
        if fwd:
            put_forward(w, outs[k])
            k += 1
        if bwd:
            put_backward(w, outs[k])
            k += 1


def main_kernel(sizes, scales, *refs):
    (ids, own, fine, pools) = refs[:4]
    up, down = fine.at[0], fine.at[1]
    (w_enc, w_bot, w_mid, w_top, t_top, t_mid) = refs[4:10]
    (up_low, sum_low, up_mid, sum_mid, pool_low) = refs[10:15]
    (feat, dskip, packed, pre_one, taps_out, g_top, g_mid, g_bot) = refs[15:23]
    (pool_s, taps_a, sum_a, act_a, taps_b, sum_b, act_b) = refs[23:30]
    (taps_c, sum_c, act_c, pre_c, taps_d, sum_d, err_d) = refs[30:37]
    (taps_e, sum_e, err_c, stack, taps_f, sum_f) = refs[37:43]
    (rows_all, cols_all) = sizes
    (scale_top, scale_mid, scale_low) = scales
    gx, gy = ids[0], ids[1]
    rows_mid, rows_low = rows_all // 2, rows_all // 4

    for k in range(16):
        tile, slab = 5 + (k - 7) // 2, 2 * ((k - 7) % 2)
        pool_s[k, :, 0:128] = pools[tile, slab]
        pool_s[k, :, 128:256] = pools[tile, slab + 1]

    def enc_taps(k):
        put_taps(taps_a, k, 0, 32, pool_s[k], 8)
        sum_a[k] = dot(w_enc[...], taps_a[k])

    loop(16, enc_taps, 4)
    wide_in = inside(WIDE, 8, cols_all // 2, gy)

    def enc_act(k):
        value = silu(row_sum(sum_a, k, 64)) * (wide_in * row_ok(gx * 2 + k - 6, rows_mid))
        act_a[k] = value.astype(BF)

    loop(14, enc_act, 2)
    for m in range(4):
        pre = row_sum(sum_a, m + 5, 64)
        pre_one[m] = jnp.where(lane(128) < 96, pre[:, 0:128], pre[:, 128:256])
        taps_out[m] = taps_a[m + 6, :, 0:128]

    def low_taps(k):
        pooled = dot(act_a[2 * k], pool_low[...]) + dot(act_a[2 * k + 1], pool_low[...])
        put_taps(taps_b, k, 0, 64, pooled.astype(BF), 4)
        sum_b[k] = dot(w_bot[...], taps_b[k])

    loop(7, low_taps, 7)
    low_in = inside(LOW, 4, cols_all // 4, gy)
    mid_in = inside(MID, 8, cols_all // 2, gy)
    pick = jnp.where(lax.broadcasted_iota(jnp.int32, (64, 128), 1) < 96, 1.0, 0.0)
    near = pick.astype(BF)
    away = (1.0 - pick).astype(BF)

    def low_act(k):
        value = silu(row_sum(sum_b, k, 128)) * (low_in * row_ok(gx + k - 2, rows_low))
        act_b[k] = dot(value.astype(BF), up_low[...]).astype(BF)

    loop(5, low_act, 5)

    def mid_taps(k):
        put_taps(taps_c, k, 0, 192, act_b[(k + 1) // 2], 8)
        narrow = act_a[k + 3, :, 0:128] * near + act_a[k + 3, :, 128:256] * away
        put_taps(taps_c, k, 128, 192, narrow, 8)
        sum_c[k] = dot(w_mid[...], taps_c[k])

    loop(8, mid_taps, 2)

    def mid_act(k):
        pre = row_sum(sum_c, k, 64)
        pre_c[k] = pre
        value = silu(pre) * (mid_in * row_ok(gx * 2 + k - 2, rows_mid))
        act_c[k] = dot(value.astype(BF), up_mid[...]).astype(BF)

    loop(6, mid_act, 6)

    def skip_row(kind, k):
        part = (up, own, down)[k // 4]
        base = 12 * kind + 3 * (k % 4)
        return jnp.concatenate([part[base], part[base + 1], part[base + 2]], axis=1)

    for k in range(12):
        put_taps(taps_d, k, 64, 96, skip_row(0, k), 16)

    def top_taps(j):
        for half in range(2):
            put_taps(taps_d, 2 * j + half, 0, 96, act_c[j], 16)
            sum_d[2 * j + half] = dot(w_top[...], taps_d[2 * j + half])

    loop(6, top_taps, 2)
    for k in range(10):
        pre = row_sum(sum_d, k, 32)
        s = sigmoid(pre)
        if 3 <= k < 7:
            feat[k - 3] = (pre * s)[:, 0:256].astype(BF)
        cot = skip_row(1, k + 1).astype(F32)
        err_d[k] = (cot * (s * (1.0 + pre * (1.0 - s)))).astype(BF)

    def top_back(k):
        put_taps(taps_e, k, 0, 32, err_d[k], 16)
        sum_e[k] = dot(t_top[...], taps_e[k])

    loop(10, top_back, 2)

    total = None
    for k in range(6):
        parts = []
        for a in range(3):
            r = k - a
            own_row = 0 <= r < 4
            parts.append(err_d[r + 3, :, 0:256] if own_row else jnp.zeros((32, 256), BF))
        term = dot_nt(jnp.concatenate(parts, axis=0), taps_d[k + 3, :, 0:256])
        total = term if total is None else total + term
    put_padded(g_top, 0, total * scale_top)

    def mid_err(m):
        one = row_sum(sum_e, 2 * m, 96)
        two = row_sum(sum_e, 2 * m + 1, 96)
        whole = dot_split(one[0:64] + two[0:64], sum_mid[...])
        keep = mid_in * row_ok(gx * 2 + m - 1, rows_mid)
        err_c[m] = (whole * slope(pre_c[m + 1]) * keep).astype(BF)

    loop(4, mid_err, 4)
    for r in range(4):
        dskip[r] = row_sum(sum_e, r + 2, 96)[64:96, 0:256]

    def mid_back(m):
        put_taps(taps_f, m, 0, 64, err_c[m], 8)
        sum_f[m] = dot(t_mid[...], taps_f[m])

    loop(4, mid_back, 2)
    own_mid = jnp.where(lax.broadcasted_iota(jnp.int32, (64, 128), 1) < 64, 1.0, 0.0).astype(BF)
    for k in range(4):
        for a in range(3):
            r = k - a
            piece = err_c[r + 1] * own_mid if 0 <= r < 2 else jnp.zeros((64, 128), BF)
            stack[k, 64 * a : 64 * a + 64, :] = piece
    total = None
    for k in range(4):
        term = dot_nt(stack[k], taps_c[k + 2])
        total = term if total is None else total + term
    put_padded(g_mid, 0, total * scale_mid)

    one = row_sum(sum_f, 0, 192)
    two = row_sum(sum_f, 1, 192)
    whole = dot_split(one[0:128] + two[0:128], sum_low[...])
    keep = jnp.where(lane(128) < 16, 1.0, 0.0)
    err_low = (whole * slope(row_sum(sum_b, 2, 128)) * keep).astype(BF)
    packed[0:128, :] = err_low
    both = jnp.where(lane(128) < 64, one[128:192], pltpu.roll(two[128:192], 64, 1))
    packed[128:192, :] = both.astype(BF)
    for a in range(3):
        put_padded(g_bot, 128 * a, dot_nt(err_low, taps_b[a + 2]) * scale_low)


def join_kernel(own, left, right, out):
    wide = [ref[0:128, :].astype(F32) for ref in (own, right, left)]
    err = wide[0] + pltpu.roll(wide[1], 16, 1) + pltpu.roll(wide[2], 112, 1)
    out[0:128, :] = err.astype(BF)
    at = lane(128)
    mine, right, left = [ref[128:192, :].astype(F32) for ref in (own, right, left)]
    turned = [pltpu.roll(v, 64, 1) for v in (mine, right, left)]
    for row, (a, b, c) in enumerate(((mine, turned[1], turned[2]), (turned[0], right, left))):
        value = jnp.where(at < 64, a, jnp.where(at < 96, b, c))
        out[128 + 64 * row : 192 + 64 * row, :] = value.astype(BF)


def tail_kernel(sizes, scale_mid, *refs):
    (ids, own, up_two, down_two, mate, beyond, pre_one, taps_in, dskip) = refs[:9]
    (t_bot, t_enc, up_low, up_mid) = refs[9:13]
    (grad_skip, g_enc) = refs[13:15]
    (taps_a, sum_a, err_s, taps_b, sum_b) = refs[15:20]
    (rows_all, cols_all) = sizes
    gx, gy = ids[0], ids[1]
    rows_mid = rows_all // 2
    mid_in = inside(MID, 8, cols_all // 2, gy)

    low = jnp.where(gx % 2 == 0, 1.0, 0.0)
    high = 1.0 - low
    below = jnp.full((128, 128), low).astype(BF)
    above = jnp.full((128, 128), high).astype(BF)
    rows = (
        up_two[0:128, :],
        beyond[0:128, :] * below + mate[0:128, :] * above,
        own[0:128, :],
        mate[0:128, :] * below + beyond[0:128, :] * above,
        down_two[0:128, :],
    )
    for k, value in enumerate(rows):
        put_taps(taps_a, k, 0, 128, value, 4)
        sum_a[k] = dot(t_bot[...], taps_a[k])
    ups = [dot_split(row_sum(sum_a, k, 64), up_low[...]) * 0.125 for k in range(3)]
    next_row = beyond[128:192, :].astype(F32)
    parts = (
        next_row * low + mate[192:256, :].astype(F32) * high,
        own[128:192, :].astype(F32),
        own[192:256, :].astype(F32),
        mate[128:192, :].astype(F32) * low + next_row * high,
    )
    for m in range(4):
        part = parts[m]
        keep = mid_in * row_ok(gx * 2 + m - 1, rows_mid)
        err = (part + ups[(m + 1) // 2]) * slope(pre_one[m]) * keep
        err = err.astype(BF)
        err_s[m] = err
        put_taps(taps_b, m, 0, 64, err, 8)
        sum_b[m] = dot(t_enc[...], taps_b[m])
    own_mid = jnp.where(lax.broadcasted_iota(jnp.int32, (64, 128), 1) < 64, 1.0, 0.0).astype(BF)
    total = None
    for k in range(4):
        parts = []
        for a in range(3):
            r = k - a
            parts.append(err_s[r + 1] * own_mid if 0 <= r < 2 else jnp.zeros((64, 128), BF))
        term = dot_nt(jnp.concatenate(parts, axis=0), taps_in[k])
        total = term if total is None else total + term
    total = (total * scale_mid).astype(BF)
    g_enc[0:192, :] = total[:, 0:128]
    g_enc[192:384, :] = total[:, 128:256]
    rest = [total[48 * q : 48 * q + 48, 256:288] for q in range(4)]
    g_enc[384:432, :] = jnp.concatenate(rest, axis=1)
    for q in range(2):
        fine = dot_split(row_sum(sum_b, q, 32), up_mid[:, 0:256]) * 0.125
        for half in range(2):
            r = 2 * q + half
            grad_skip[r] = (dskip[r] + fine).astype(BF)


def finish_kernel(g, out):
    rest = jnp.concatenate([g[384:432, 32 * q : 32 * q + 32] for q in range(4)], axis=0)
    pieces = []
    for a in range(3):
        at = 64 * a
        pieces += [g[at : at + 64, :], g[192 + at : 256 + at, :], rest[at : at + 64, :]]
    out[...] = jnp.concatenate(pieces, axis=1).astype(F32)


VMEM = pl.BlockSpec(memory_space=pltpu.VMEM)
SMEM = pl.BlockSpec(memory_space=pltpu.SMEM)


def call(kernel, outs, scratch, scalars, *args, cost=1, grant=8):
    return pl.pallas_call(
        kernel,
        out_shape=[jax.ShapeDtypeStruct(s, d) for s, d in outs],
        in_specs=[SMEM] * scalars + [VMEM] * (len(args) - scalars),
        out_specs=[VMEM] * len(outs),
        scratch_shapes=[pltpu.VMEM(s, d) for s, d in scratch],
        compiler_params=pltpu.CompilerParams(vmem_limit_bytes=grant * 1024 * 1024),
        cost_estimate=pl.CostEstimate(
            flops=cost * 500_000_000, bytes_accessed=cost * 1_000_000, transcendentals=0
        ),
    )(*args)


def shift(value, axis, count, step):
    return lax.ppermute(value, axis, [(i, i + step) for i in range(count) if 0 <= i + step < count])


def tiles_of(g):
    rows, width = g.shape
    return g.reshape(rows // 8, 8, width // 128, 128).transpose(0, 2, 1, 3).reshape(-1, 8, 128)


def from_tiles(tiles, rows, width):
    wide = -(-width // 128)
    g = tiles.reshape(rows // 8, wide, 8, 128).transpose(0, 2, 1, 3).reshape(rows, wide * 128)
    return g[:, :width]


def full_gradient(g):
    rows, _ = g.shape
    out = rows // 3
    return jnp.concatenate([g[out * a : out * a + out] for a in range(3)], axis=1).astype(F32)


def solution(mesh):
    ngx, ngy = mesh.shape["gx"], mesh.shape["gy"]
    devices = ngx * ngy
    const = {k: np.asarray(v) for k, v in constants().items()}

    def step(skip_input, w_encoder, w_bottom, w_middle, w_upper, cotangent):
        gx, gy = lax.axis_index("gx"), lax.axis_index("gy")
        ids = jnp.stack([gx, gy]).astype(jnp.int32)
        rows_all, cols_all = 4 * ngx, 16 * ngy
        sizes = (rows_all, cols_all)
        cells = rows_all * cols_all * 16
        scales = tuple(1.0 / math.sqrt(cells // k) for k in (1, 8, 64))
        c = {k: jnp.asarray(v, BF) for k, v in const.items()}

        block, width = w_bottom.shape
        slabs = block * 2048 // 4096
        weight = jnp.pad(w_bottom, ((0, 0), (0, 2048 - width)))
        lanes = weight.shape[1] // 128
        weight = weight.reshape(block, lanes, 128).transpose(1, 0, 2).reshape(slabs, 32, 128)

        swap = [(i, i ^ 1) for i in range(ngx)]
        around = ngx // 4

        def along_y(i, k):
            side, y, core = i // (2 * around), i // 2 % around, i % 2
            return (side * around + (y + k) % around) * 2 + core

        part = ngy // 4 if ngy % 4 == 0 else ngy

        def mirrored(i):
            x, y = i // ngy, i % ngy
            y = (ngy // part - 1 - y // part) * part + y % part
            return (x + ngx // 2) % ngx * ngy + y

        w_line = [weight]
        for k in range(1, around):
            w_line.append(lax.ppermute(weight, "gx", [(i, along_y(i, k)) for i in range(ngx)]))
        w_line = jnp.concatenate(w_line, axis=0)
        w_far = lax.ppermute(w_line, AXES, [(i, mirrored(i)) for i in range(devices)])
        w_mine = jnp.concatenate([w_line, w_far], axis=0)
        w_mate = lax.ppermute(w_mine, "gx", swap)

        skip = skip_input.transpose(1, 0, 2)
        cot = cotangent.transpose(1, 0, 2)
        to_left, to_right = call(
            pool_kernel, [((10, 32, 128), BF)] * 2, [], 0, skip, cot, c["pool_tile"]
        )
        right = shift(to_left, "gy", ngy, -1)
        left = shift(to_right, "gy", ngy, 1)
        (own,) = call(widen_kernel, [((28, 32, 128), BF)], [], 0, skip, cot, to_left, right, left)
        core = gx % 2
        mate = lax.ppermute(own, "gx", swap)
        rise = jnp.where(core == 0, own[0:12], mate[12:24])
        fall = jnp.where(core == 0, mate[0:12], own[12:24])
        up = shift(jnp.concatenate([fall, own[24:28]], axis=0), "gx", ngx, 2)
        down = shift(jnp.concatenate([rise, own[24:28]], axis=0), "gx", ngx, -2)
        far_up = shift(own[24:28], "gx", ngx, 4)
        far_down = shift(own[24:28], "gx", ngx, -4)
        beyond = [
            jnp.where(core == 0, down[0:12], up[0:12]),
            up[12:16],
            down[12:16],
            jnp.where(core == 0, far_down, far_up),
        ]
        beyond = lax.ppermute(jnp.concatenate(beyond, axis=0), "gx", swap)
        fine, pools, w_bot, _, w_flat = call(
            lambda *refs: gather_kernel(ngx, block, *refs),
            [
                ((2, 24, 32, 128), BF),
                ((11, 4, 32, 128), BF),
                ((384, 576), BF),
                ((ngx, slabs, 32, 128), BF),
                ((ngx * block, lanes * 128), BF),
            ],
            [],
            1,
            ids,
            own,
            up,
            down,
            far_up,
            far_down,
            mate,
            beyond,
            w_mine,
            w_mate,
        )
        w_enc, t_enc, w_mid, t_mid, w_top, t_top = call(
            lambda *refs: weight_kernel((1, 1, 1), (1, 1, 1), *refs),
            [
                ((192, 288), BF),
                ((96, 576), BF),
                ((192, 1728), BF),
                ((576, 576), BF),
                ((96, 864), BF),
                ((288, 288), BF),
            ],
            [],
            0,
            w_encoder,
            w_middle,
            w_upper,
            cost=4,
        )
        (t_bot,) = call(
            lambda *refs: weight_kernel((0,), (1,), *refs),
            [((192, 1152), BF)],
            [],
            0,
            w_flat,
            cost=2,
        )

        outs = [
            ((4, 32, 256), BF),
            ((4, 32, 256), F32),
            ((192, 128), BF),
            ((4, 64, 128), F32),
            ((4, 288, 128), BF),
            ((96, 896), BF),
            ((192, 1792), BF),
            ((384, 640), BF),
        ]
        scratch = [
            ((16, 32, 256), BF),
            ((16, 288, 256), BF),
            ((16, 192, 256), F32),
            ((14, 64, 256), BF),
            ((7, 576, 128), BF),
            ((7, 384, 128), F32),
            ((5, 128, 128), BF),
            ((8, 1728, 128), BF),
            ((8, 192, 128), F32),
            ((6, 64, 384), BF),
            ((6, 64, 128), F32),
            ((12, 864, 384), BF),
            ((12, 96, 384), F32),
            ((10, 32, 384), BF),
            ((10, 288, 384), BF),
            ((10, 288, 384), F32),
            ((4, 64, 128), BF),
            ((4, 192, 128), BF),
            ((4, 576, 128), BF),
            ((4, 576, 128), F32),
        ]
        feat, dskip, packed, pre_one, taps_one, g_top, g_mid, g_bot = call(
            lambda *refs: main_kernel(sizes, scales, *refs),
            outs,
            scratch,
            1,
            ids,
            own,
            fine,
            pools,
            w_enc,
            w_bot,
            w_mid,
            w_top,
            t_top,
            t_mid,
            c["up_low"],
            c["sum_low"],
            c["up_mid"],
            c["sum_mid"],
            c["pool_low"],
            cost=20,
            grant=33,
        )

        from_left = shift(packed, "gy", ngy, 1)
        from_right = shift(packed, "gy", ngy, -1)
        (line,) = call(join_kernel, [((256, 128), BF)], [], 0, packed, from_left, from_right)
        mate = lax.ppermute(line, "gx", swap)
        fall = jnp.concatenate([line[0:128], line[192:256]], axis=0)
        line_up = shift(fall, "gx", ngx, 2)
        line_down = shift(line[0:192], "gx", ngx, -2)
        beyond = lax.ppermute(jnp.where(core == 0, line_down, line_up), "gx", swap)
        grad_skip, g_enc = call(
            lambda *refs: tail_kernel(sizes, scales[1], *refs),
            [((4, 32, 256), BF), ((432, 128), BF)],
            [
                ((5, 1152, 128), BF),
                ((5, 192, 128), F32),
                ((4, 64, 128), BF),
                ((4, 576, 128), BF),
                ((4, 96, 128), F32),
            ],
            1,
            ids,
            line,
            line_up,
            line_down,
            mate,
            beyond,
            pre_one,
            taps_one,
            dskip,
            t_bot,
            t_enc,
            c["up_low"],
            c["up_mid"],
            cost=4,
        )

        grads = ((g_top, 864), (g_mid, 1728), (g_bot, 576), (g_enc, 128))
        tiles = [tiles_of(g) for g, _ in grads]
        spare = -sum(t.shape[0] for t in tiles) % devices
        flat = jnp.concatenate(tiles + [jnp.zeros((spare, 8, 128), BF)], axis=0)
        half = flat.shape[0] // 2
        keep = lax.dynamic_slice_in_dim(flat, core * half, half, 0)
        other = lax.dynamic_slice_in_dim(flat, (1 - core) * half, half, 0)
        other = lax.ppermute(other, "gx", swap)
        mine = (keep.astype(F32) + other.astype(F32)).astype(BF)
        parts = mine.reshape(devices // 2, -1, 128)
        groups = [[i for i in range(devices) if i // ngy % 2 == k] for k in range(2)]
        parts = lax.all_to_all(
            parts, AXES, split_axis=0, concat_axis=0, axis_index_groups=groups, tiled=True
        )
        total = parts.astype(F32).sum(axis=0).astype(BF)
        spread = jnp.broadcast_to(total[None], parts.shape)
        spread = lax.all_to_all(
            spread, AXES, split_axis=0, concat_axis=0, axis_index_groups=groups, tiled=True
        )
        mine = spread.reshape(half, 8, 128)
        other = lax.ppermute(mine, "gx", swap)
        first = jnp.where(core == 0, mine, other)
        second = jnp.where(core == 0, other, mine)
        whole = jnp.concatenate([first, second], axis=0)

        full = []
        start = 0
        for (g, width), t in zip(grads, tiles):
            full.append(from_tiles(whole[start : start + t.shape[0]], g.shape[0], width))
            start += t.shape[0]
        full_top, full_mid, full_bot, full_enc = full
        (full_enc,) = call(finish_kernel, [((64, 864), F32)], [], 0, full_enc)
        mine_bot = full_bot.reshape(3, ngx, block, -1)
        mine_bot = lax.dynamic_index_in_dim(mine_bot, gx, 1, keepdims=False)
        mine_bot = mine_bot.reshape(3 * block, -1)
        return (
            feat.transpose(1, 0, 2),
            grad_skip.transpose(1, 0, 2),
            full_enc,
            full_gradient(mine_bot),
            full_gradient(full_mid),
            full_gradient(full_top),
        )

    in_specs = (P(None, "gx", "gy"), P(), P("gx", None), P(), P(), P(None, "gx", "gy"))
    out_specs = (P(None, "gx", "gy"), P(None, "gx", "gy"), P(), P("gx", None), P(), P())
    return jax.shard_map(step, mesh=mesh, in_specs=in_specs, out_specs=out_specs, check_vma=False)
```

```python
import math

import jax
import jax.numpy as jnp
import numpy as np
from jax import lax
from jax.experimental import pallas as pl
from jax.experimental.pallas import tpu as pltpu
from jax.sharding import PartitionSpec as P

AXES = ("gx", "gy")
BF = jnp.bfloat16
F32 = jnp.float32


def columns(lanes, depth, split):
    col = np.arange(lanes) // depth
    return np.where(col >= split, col - lanes // depth, col), np.arange(lanes) % depth


def upsampling(coarse, fine):
    (col_c, z_c), (col_f, z_f) = (columns(*coarse), columns(*fine))
    hit = (col_c[:, None] == col_f[None, :] // 2) & (z_c[:, None] == z_f[None, :] // 2)
    return hit.astype(np.float32)


TOP = (384, 16, 20)
WIDE = (256, 8, 16)
MID = (128, 8, 12)
LOW = (128, 4, 16)


def constants():
    low_mid = upsampling(LOW, MID)
    mid_top = upsampling(MID, TOP)
    wide_low = upsampling(LOW, WIDE).T / 8.0
    tile_pool = mid_top[:64, :256].T / 8.0
    tile_pool = np.concatenate([tile_pool, tile_pool], axis=1)
    return {
        "up_low": low_mid,
        "sum_low": low_mid.T,
        "up_mid": mid_top,
        "sum_mid": mid_top.T,
        "pool_low": wide_low,
        "pool_tile": tile_pool,
    }


def dot(a, b):
    return jnp.dot(a, b, preferred_element_type=F32)


def dot_nt(a, b):
    return lax.dot_general(a, b, (((1,), (1,)), ((), ())), preferred_element_type=F32)


def dot_split(a, b):
    head = a.astype(BF)
    rest = (a - head.astype(F32)).astype(BF)
    return dot(head, b) + dot(rest, b)


def loop(count, body, unroll=1):
    def step(i, carry):
        for u in range(unroll):
            body(i * unroll + u)
        return carry

    if unroll == count:
        step(0, 0)
    else:
        lax.fori_loop(0, count // unroll, step, 0)


def lane(length):
    return lax.broadcasted_iota(jnp.int32, (1, length), 1)


def inside(region, tile_cols, total_cols, index):
    lanes, depth, split = region
    col = lane(lanes) // depth
    col = jnp.where(col >= split, col - lanes // depth, col) + index * tile_cols
    return jnp.where((col >= 0) & (col < total_cols), 1.0, 0.0)


def row_ok(row, total):
    return jnp.where((row >= 0) & (row < total), 1.0, 0.0)


def depth_masks(shape, depth):
    z = lax.broadcasted_iota(jnp.int32, shape, 1) % depth
    below = jnp.where(z == depth - 1, 0.0, 1.0).astype(BF)
    above = jnp.where(z == 0, 0.0, 1.0).astype(BF)
    return below, above


def put_taps(dst, row, first, width, value, depth):
    chans, lanes = value.shape
    below, above = depth_masks(value.shape, depth)
    kinds = (value * below, value, value * above)
    for b in range(3):
        for e in range(3):
            shift = (b - 1) * depth + (e - 1)
            piece = kinds[e]
            if shift:
                piece = pltpu.roll(piece, (-shift) % lanes, 1)
            start = (3 * b + e) * width + first
            dst[row, start : start + chans, :] = piece


def sigmoid(v):
    return 1.0 / (1.0 + jnp.exp(-v))


def silu(v):
    return v * sigmoid(v)


def slope(v):
    s = sigmoid(v)
    return s * (1.0 + v * (1.0 - s))


def row_sum(ref, row, chans):
    return (
        ref[row, 0:chans, :]
        + ref[row + 1, chans : 2 * chans, :]
        + ref[row + 2, 2 * chans : 3 * chans, :]
    )


def put_padded(out, row, value):
    rows, width = value.shape
    out[row : row + rows, 0:width] = value.astype(BF)
    out[row : row + rows, width:] = jnp.zeros((rows, out.shape[1] - width), BF)


def pool_kernel(skip, cot, pool_tile, to_left, to_right):
    for r in range(4):
        to_left[r] = skip[r, :, 0:128]
        to_left[4 + r] = cot[r, :, 0:128]
        to_right[r] = skip[r, :, 128:256]
        to_right[4 + r] = cot[r, :, 128:256]
    for q in range(2):
        pooled = dot(skip[2 * q], pool_tile[...]) + dot(skip[2 * q + 1], pool_tile[...])
        pooled = pooled.astype(BF)
        to_left[8 + q] = pooled
        to_right[8 + q] = pooled


def widen_kernel(skip, cot, own, right, left, out):
    first = jnp.where(lax.broadcasted_iota(jnp.int32, (32, 128), 1) < 64, 1.0, 0.0)
    head = first.astype(BF)
    tail = (1.0 - first).astype(BF)
    for r in range(4):
        for k, tile in enumerate((skip, cot)):
            base = 12 * k + 3 * r
            out[base] = tile[r, :, 0:128]
            out[base + 1] = tile[r, :, 128:256]
            out[base + 2] = right[4 * k + r] * head + left[4 * k + r] * tail
    for q in range(2):
        out[24 + 2 * q] = own[8 + q] * head + right[8 + q] * tail
        out[25 + 2 * q] = left[8 + q] * tail


def gather_kernel(tiles, block, *refs):
    (ids, own, mate, got, got_m, far, far_m, w_mine, w_mate) = refs[:9]
    (fine, pools, w_out, w_all, w_flat) = refs[9:14]
    gx = ids[0]
    core = gx % 2
    low = jnp.where(core == 0, 1.0, 0.0)
    below = jnp.full((32, 32, 128), low).astype(BF)
    above = jnp.full((32, 32, 128), 1.0 - low).astype(BF)
    lower = got[...] * below + got_m[...] * above
    upper = got_m[...] * below + got[...] * above
    fine[0] = upper[0:24] * below[0:24] + mate[0:24] * above[0:24]
    fine[1] = mate[0:24] * below[0:24] + lower[0:24] * above[0:24]
    far_lower = far[...] * below[0:8] + far_m[...] * above[0:8]
    far_upper = far_m[...] * below[0:8] + far[...] * above[0:8]
    first = own[24:28] * below[0:4] + mate[24:28] * above[0:4]
    second = mate[24:28] * below[0:4] + own[24:28] * above[0:4]
    for step, tile in (
        (-4, far_upper[4:8]),
        (-3, far_upper[0:4]),
        (-2, upper[28:32]),
        (-1, upper[24:28]),
        (0, first),
        (1, second),
        (2, lower[24:28]),
        (3, lower[28:32]),
        (4, far_lower[0:4]),
        (5, far_lower[4:8]),
    ):
        pools[step + 5 - core] = tile

    slabs = w_all.shape[1]
    around = tiles // 4
    y = (gx // 2) % around
    side = gx // (2 * around)
    for lane_core, ref in ((core, w_mine), (1 - core, w_mate)):
        for far in range(2):
            for k in range(around):
                z_part = (side + far) % 2
                y_part = (y + around - k) % around
                at = (far * around + k) * slabs
                w_all[(z_part * around + y_part) * 2 + lane_core] = ref[at : at + slabs]
    lanes = w_flat.shape[1] // 128
    for b in range(tiles):
        rows = w_all[b].reshape(lanes * block, 128)
        for l in range(lanes):
            w_flat[b * block : b * block + block, 128 * l : 128 * l + 128] = rows[
                l * block : l * block + block
            ]
    put_forward(w_flat, w_out)


def put_forward(w, out):
    rows = w.shape[0]
    width = out.shape[1]
    for a in range(3):
        out[rows * a : rows * a + rows, :] = w[:, a * width : (a + 1) * width]


def put_backward(w, out):
    chans = out.shape[0] // 3
    i = lax.broadcasted_iota(jnp.int32, (chans, chans), 0)
    j = lax.broadcasted_iota(jnp.int32, (chans, chans), 1)
    unit = jnp.where(i == j, 1.0, 0.0).astype(BF)
    for a in range(3):
        taps = [26 - 9 * a - k for k in range(9)]
        stacked = jnp.concatenate([w[:, t * chans : t * chans + chans] for t in taps], axis=0)
        out[chans * a : chans * a + chans, :] = dot_nt(unit, stacked).astype(BF)


def weight_kernel(forward, backward, *refs):
    sources, outs = refs[: len(forward)], refs[len(forward) :]
    k = 0
    for w, fwd, bwd in zip(sources, forward, backward):
        if fwd:
            put_forward(w, outs[k])
            k += 1
        if bwd:
            put_backward(w, outs[k])
            k += 1


def main_kernel(sizes, scales, *refs):
    (ids, own, fine, pools) = refs[:4]
    up, down = fine.at[0], fine.at[1]
    (w_enc, w_bot, w_mid, w_top, t_top, t_mid) = refs[4:10]
    (up_low, sum_low, up_mid, sum_mid, pool_low) = refs[10:15]
    (feat, dskip, packed, pre_one, taps_out, g_top, g_mid, g_bot) = refs[15:23]
    (pool_s, taps_a, sum_a, act_a, taps_b, sum_b, act_b) = refs[23:30]
    (taps_c, sum_c, act_c, pre_c, taps_d, sum_d, err_d) = refs[30:37]
    (taps_e, sum_e, err_c, stack, taps_f, sum_f) = refs[37:43]
    (rows_all, cols_all) = sizes
    (scale_top, scale_mid, scale_low) = scales
    gx, gy = ids[0], ids[1]
    rows_mid, rows_low = rows_all // 2, rows_all // 4

    for k in range(16):
        tile, slab = 5 + (k - 7) // 2, 2 * ((k - 7) % 2)
        pool_s[k, :, 0:128] = pools[tile, slab]
        pool_s[k, :, 128:256] = pools[tile, slab + 1]

    def enc_taps(k):
        put_taps(taps_a, k, 0, 32, pool_s[k], 8)
        sum_a[k] = dot(w_enc[...], taps_a[k])

    loop(16, enc_taps, 4)
    wide_in = inside(WIDE, 8, cols_all // 2, gy)

    def enc_act(k):
        value = silu(row_sum(sum_a, k, 64)) * (wide_in * row_ok(gx * 2 + k - 6, rows_mid))
        act_a[k] = value.astype(BF)

    loop(14, enc_act, 2)
    for m in range(4):
        pre = row_sum(sum_a, m + 5, 64)
        pre_one[m] = jnp.where(lane(128) < 96, pre[:, 0:128], pre[:, 128:256])
        taps_out[m] = taps_a[m + 6, :, 0:128]

    def low_taps(k):
        pooled = dot(act_a[2 * k], pool_low[...]) + dot(act_a[2 * k + 1], pool_low[...])
        put_taps(taps_b, k, 0, 64, pooled.astype(BF), 4)
        sum_b[k] = dot(w_bot[...], taps_b[k])

    loop(7, low_taps, 7)
    low_in = inside(LOW, 4, cols_all // 4, gy)
    mid_in = inside(MID, 8, cols_all // 2, gy)
    pick = jnp.where(lax.broadcasted_iota(jnp.int32, (64, 128), 1) < 96, 1.0, 0.0)
    near = pick.astype(BF)
    away = (1.0 - pick).astype(BF)

    def low_act(k):
        value = silu(row_sum(sum_b, k, 128)) * (low_in * row_ok(gx + k - 2, rows_low))
        act_b[k] = dot(value.astype(BF), up_low[...]).astype(BF)

    loop(5, low_act, 5)

    def mid_taps(k):
        put_taps(taps_c, k, 0, 192, act_b[(k + 1) // 2], 8)
        narrow = act_a[k + 3, :, 0:128] * near + act_a[k + 3, :, 128:256] * away
        put_taps(taps_c, k, 128, 192, narrow, 8)
        sum_c[k] = dot(w_mid[...], taps_c[k])

    loop(8, mid_taps, 2)

    def mid_act(k):
        pre = row_sum(sum_c, k, 64)
        pre_c[k] = pre
        value = silu(pre) * (mid_in * row_ok(gx * 2 + k - 2, rows_mid))
        act_c[k] = dot(value.astype(BF), up_mid[...]).astype(BF)

    loop(6, mid_act, 6)

    def skip_row(kind, k):
        part = (up, own, down)[k // 4]
        base = 12 * kind + 3 * (k % 4)
        return jnp.concatenate([part[base], part[base + 1], part[base + 2]], axis=1)

    for k in range(12):
        put_taps(taps_d, k, 64, 96, skip_row(0, k), 16)

    def top_taps(j):
        for half in range(2):
            put_taps(taps_d, 2 * j + half, 0, 96, act_c[j], 16)
            sum_d[2 * j + half] = dot(w_top[...], taps_d[2 * j + half])

    loop(6, top_taps, 2)
    for k in range(10):
        pre = row_sum(sum_d, k, 32)
        s = sigmoid(pre)
        if 3 <= k < 7:
            feat[k - 3] = (pre * s)[:, 0:256].astype(BF)
        cot = skip_row(1, k + 1).astype(F32)
        err_d[k] = (cot * (s * (1.0 + pre * (1.0 - s)))).astype(BF)

    def top_back(k):
        put_taps(taps_e, k, 0, 32, err_d[k], 16)
        sum_e[k] = dot(t_top[...], taps_e[k])

    loop(10, top_back, 2)

    total = None
    for k in range(6):
        parts = []
        for a in range(3):
            r = k - a
            own_row = 0 <= r < 4
            parts.append(err_d[r + 3, :, 0:256] if own_row else jnp.zeros((32, 256), BF))
        term = dot_nt(jnp.concatenate(parts, axis=0), taps_d[k + 3, :, 0:256])
        total = term if total is None else total + term
    put_padded(g_top, 0, total * scale_top)

    def mid_err(m):
        one = row_sum(sum_e, 2 * m, 96)
        two = row_sum(sum_e, 2 * m + 1, 96)
        whole = dot_split(one[0:64] + two[0:64], sum_mid[...])
        keep = mid_in * row_ok(gx * 2 + m - 1, rows_mid)
        err_c[m] = (whole * slope(pre_c[m + 1]) * keep).astype(BF)

    loop(4, mid_err, 4)
    for r in range(4):
        dskip[r] = row_sum(sum_e, r + 2, 96)[64:96, 0:256]

    def mid_back(m):
        put_taps(taps_f, m, 0, 64, err_c[m], 8)
        sum_f[m] = dot(t_mid[...], taps_f[m])

    loop(4, mid_back, 2)
    own_mid = jnp.where(lax.broadcasted_iota(jnp.int32, (64, 128), 1) < 64, 1.0, 0.0).astype(BF)
    for k in range(4):
        for a in range(3):
            r = k - a
            piece = err_c[r + 1] * own_mid if 0 <= r < 2 else jnp.zeros((64, 128), BF)
            stack[k, 64 * a : 64 * a + 64, :] = piece
    total = None
    for k in range(4):
        term = dot_nt(stack[k], taps_c[k + 2])
        total = term if total is None else total + term
    put_padded(g_mid, 0, total * scale_mid)

    one = row_sum(sum_f, 0, 192)
    two = row_sum(sum_f, 1, 192)
    whole = dot_split(one[0:128] + two[0:128], sum_low[...])
    keep = jnp.where(lane(128) < 16, 1.0, 0.0)
    err_low = (whole * slope(row_sum(sum_b, 2, 128)) * keep).astype(BF)
    packed[0:128, :] = err_low
    both = jnp.where(lane(128) < 64, one[128:192], pltpu.roll(two[128:192], 64, 1))
    packed[128:192, :] = both.astype(BF)
    for a in range(3):
        put_padded(g_bot, 128 * a, dot_nt(err_low, taps_b[a + 2]) * scale_low)


def join_kernel(own, left, right, out):
    wide = [ref[0:128, :].astype(F32) for ref in (own, right, left)]
    err = wide[0] + pltpu.roll(wide[1], 16, 1) + pltpu.roll(wide[2], 112, 1)
    out[0:128, :] = err.astype(BF)
    at = lane(128)
    mine, right, left = [ref[128:192, :].astype(F32) for ref in (own, right, left)]
    turned = [pltpu.roll(v, 64, 1) for v in (mine, right, left)]
    for row, (a, b, c) in enumerate(((mine, turned[1], turned[2]), (turned[0], right, left))):
        value = jnp.where(at < 64, a, jnp.where(at < 96, b, c))
        out[128 + 64 * row : 192 + 64 * row, :] = value.astype(BF)


def tail_kernel(sizes, scale_mid, *refs):
    (ids, own, mate, got, got_m, pre_one, taps_in, dskip) = refs[:8]
    (t_bot, t_enc, up_low, up_mid) = refs[8:12]
    (grad_skip, g_enc) = refs[12:14]
    (taps_a, sum_a, err_s, taps_b, sum_b) = refs[14:19]
    (rows_all, cols_all) = sizes
    gx, gy = ids[0], ids[1]
    rows_mid = rows_all // 2
    mid_in = inside(MID, 8, cols_all // 2, gy)

    low = jnp.where(gx % 2 == 0, 1.0, 0.0)
    high = 1.0 - low
    below = jnp.full((320, 128), low).astype(BF)
    above = jnp.full((320, 128), high).astype(BF)
    lower = got[...] * below + got_m[...] * above
    upper = got_m[...] * below + got[...] * above
    below, above = below[0:128], above[0:128]
    rows = (
        upper[128:256] * below + upper[0:128] * above,
        upper[0:128] * below + mate[0:128, :] * above,
        own[0:128, :],
        mate[0:128, :] * below + lower[0:128] * above,
        lower[0:128] * below + lower[128:256] * above,
    )
    for k, value in enumerate(rows):
        put_taps(taps_a, k, 0, 128, value, 4)
        sum_a[k] = dot(t_bot[...], taps_a[k])
    ups = [dot_split(row_sum(sum_a, k, 64), up_low[...]) * 0.125 for k in range(3)]
    parts = (
        upper[256:320].astype(F32) * low + mate[192:256, :].astype(F32) * high,
        own[128:192, :].astype(F32),
        own[192:256, :].astype(F32),
        mate[128:192, :].astype(F32) * low + lower[256:320].astype(F32) * high,
    )
    for m in range(4):
        part = parts[m]
        keep = mid_in * row_ok(gx * 2 + m - 1, rows_mid)
        err = (part + ups[(m + 1) // 2]) * slope(pre_one[m]) * keep
        err = err.astype(BF)
        err_s[m] = err
        put_taps(taps_b, m, 0, 64, err, 8)
        sum_b[m] = dot(t_enc[...], taps_b[m])
    own_mid = jnp.where(lax.broadcasted_iota(jnp.int32, (64, 128), 1) < 64, 1.0, 0.0).astype(BF)
    total = None
    for k in range(4):
        parts = []
        for a in range(3):
            r = k - a
            parts.append(err_s[r + 1] * own_mid if 0 <= r < 2 else jnp.zeros((64, 128), BF))
        term = dot_nt(jnp.concatenate(parts, axis=0), taps_in[k])
        total = term if total is None else total + term
    total = (total * scale_mid).astype(BF)
    g_enc[0:192, :] = total[:, 0:128]
    g_enc[192:384, :] = total[:, 128:256]
    rest = [total[48 * q : 48 * q + 48, 256:288] for q in range(4)]
    g_enc[384:432, :] = jnp.concatenate(rest, axis=1)
    for q in range(2):
        fine = dot_split(row_sum(sum_b, q, 32), up_mid[:, 0:256]) * 0.125
        for half in range(2):
            r = 2 * q + half
            grad_skip[r] = (dskip[r] + fine).astype(BF)


def finish_kernel(g, out):
    rest = jnp.concatenate([g[384:432, 32 * q : 32 * q + 32] for q in range(4)], axis=0)
    pieces = []
    for a in range(3):
        at = 64 * a
        pieces += [g[at : at + 64, :], g[192 + at : 256 + at, :], rest[at : at + 64, :]]
    out[...] = jnp.concatenate(pieces, axis=1).astype(F32)


VMEM = pl.BlockSpec(memory_space=pltpu.VMEM)
SMEM = pl.BlockSpec(memory_space=pltpu.SMEM)


def call(kernel, outs, scratch, scalars, *args, cost=1, grant=8):
    return pl.pallas_call(
        kernel,
        out_shape=[jax.ShapeDtypeStruct(s, d) for s, d in outs],
        in_specs=[SMEM] * scalars + [VMEM] * (len(args) - scalars),
        out_specs=[VMEM] * len(outs),
        scratch_shapes=[pltpu.VMEM(s, d) for s, d in scratch],
        compiler_params=pltpu.CompilerParams(vmem_limit_bytes=grant * 1024 * 1024),
        cost_estimate=pl.CostEstimate(
            flops=cost * 500_000_000, bytes_accessed=cost * 1_000_000, transcendentals=0
        ),
    )(*args)


def shift(value, axis, count, step):
    return lax.ppermute(value, axis, [(i, i + step) for i in range(count) if 0 <= i + step < count])


def outward(value, count, step):
    pairs = [(i, i + step if i % 2 else i - step) for i in range(count)]
    return lax.ppermute(value, "gx", [(i, j) for i, j in pairs if 0 <= j < count])


def tiles_of(g):
    rows, width = g.shape
    return g.reshape(rows // 8, 8, width // 128, 128).transpose(0, 2, 1, 3).reshape(-1, 8, 128)


def from_tiles(tiles, rows, width):
    wide = -(-width // 128)
    g = tiles.reshape(rows // 8, wide, 8, 128).transpose(0, 2, 1, 3).reshape(rows, wide * 128)
    return g[:, :width]


def full_gradient(g):
    rows, _ = g.shape
    out = rows // 3
    return jnp.concatenate([g[out * a : out * a + out] for a in range(3)], axis=1).astype(F32)


def solution(mesh):
    ngx, ngy = mesh.shape["gx"], mesh.shape["gy"]
    devices = ngx * ngy
    const = {k: np.asarray(v) for k, v in constants().items()}

    def step(skip_input, w_encoder, w_bottom, w_middle, w_upper, cotangent):
        gx, gy = lax.axis_index("gx"), lax.axis_index("gy")
        ids = jnp.stack([gx, gy]).astype(jnp.int32)
        rows_all, cols_all = 4 * ngx, 16 * ngy
        sizes = (rows_all, cols_all)
        cells = rows_all * cols_all * 16
        scales = tuple(1.0 / math.sqrt(cells // k) for k in (1, 8, 64))
        c = {k: jnp.asarray(v, BF) for k, v in const.items()}

        block, width = w_bottom.shape
        slabs = block * 2048 // 4096
        weight = jnp.pad(w_bottom, ((0, 0), (0, 2048 - width)))
        lanes = weight.shape[1] // 128
        weight = weight.reshape(block, lanes, 128).transpose(1, 0, 2).reshape(slabs, 32, 128)

        swap = [(i, i ^ 1) for i in range(ngx)]
        around = ngx // 4

        def along_y(i, k):
            side, y, core = i // (2 * around), i // 2 % around, i % 2
            return (side * around + (y + k) % around) * 2 + core

        part = ngy // 4 if ngy % 4 == 0 else ngy

        def mirrored(i):
            x, y = i // ngy, i % ngy
            y = (ngy // part - 1 - y // part) * part + y % part
            return (x + ngx // 2) % ngx * ngy + y

        w_line = [weight]
        for k in range(1, around):
            w_line.append(lax.ppermute(weight, "gx", [(i, along_y(i, k)) for i in range(ngx)]))
        w_line = jnp.concatenate(w_line, axis=0)
        w_far = lax.ppermute(w_line, AXES, [(i, mirrored(i)) for i in range(devices)])
        w_mine = jnp.concatenate([w_line, w_far], axis=0)
        w_mate = lax.ppermute(w_mine, "gx", swap)

        skip = skip_input.transpose(1, 0, 2)
        cot = cotangent.transpose(1, 0, 2)
        to_left, to_right = call(
            pool_kernel, [((10, 32, 128), BF)] * 2, [], 0, skip, cot, c["pool_tile"]
        )
        right = shift(to_left, "gy", ngy, -1)
        left = shift(to_right, "gy", ngy, 1)
        (own,) = call(widen_kernel, [((28, 32, 128), BF)], [], 0, skip, cot, to_left, right, left)
        core = gx % 2
        mate = lax.ppermute(own, "gx", swap)
        got = outward(jnp.concatenate([own, mate[24:28]], axis=0), ngx, 2)
        far = outward(jnp.concatenate([own[24:28], mate[24:28]], axis=0), ngx, 4)
        got_m = lax.ppermute(got, "gx", swap)
        far_m = lax.ppermute(far, "gx", swap)
        fine, pools, w_bot, _, w_flat = call(
            lambda *refs: gather_kernel(ngx, block, *refs),
            [
                ((2, 24, 32, 128), BF),
                ((11, 4, 32, 128), BF),
                ((384, 576), BF),
                ((ngx, slabs, 32, 128), BF),
                ((ngx * block, lanes * 128), BF),
            ],
            [],
            1,
            ids,
            own,
            mate,
            got,
            got_m,
            far,
            far_m,
            w_mine,
            w_mate,
        )
        w_enc, t_enc, w_mid, t_mid, w_top, t_top = call(
            lambda *refs: weight_kernel((1, 1, 1), (1, 1, 1), *refs),
            [
                ((192, 288), BF),
                ((96, 576), BF),
                ((192, 1728), BF),
                ((576, 576), BF),
                ((96, 864), BF),
                ((288, 288), BF),
            ],
            [],
            0,
            w_encoder,
            w_middle,
            w_upper,
            cost=4,
        )
        (t_bot,) = call(
            lambda *refs: weight_kernel((0,), (1,), *refs),
            [((192, 1152), BF)],
            [],
            0,
            w_flat,
            cost=2,
        )

        outs = [
            ((4, 32, 256), BF),
            ((4, 32, 256), F32),
            ((192, 128), BF),
            ((4, 64, 128), F32),
            ((4, 288, 128), BF),
            ((96, 896), BF),
            ((192, 1792), BF),
            ((384, 640), BF),
        ]
        scratch = [
            ((16, 32, 256), BF),
            ((16, 288, 256), BF),
            ((16, 192, 256), F32),
            ((14, 64, 256), BF),
            ((7, 576, 128), BF),
            ((7, 384, 128), F32),
            ((5, 128, 128), BF),
            ((8, 1728, 128), BF),
            ((8, 192, 128), F32),
            ((6, 64, 384), BF),
            ((6, 64, 128), F32),
            ((12, 864, 384), BF),
            ((12, 96, 384), F32),
            ((10, 32, 384), BF),
            ((10, 288, 384), BF),
            ((10, 288, 384), F32),
            ((4, 64, 128), BF),
            ((4, 192, 128), BF),
            ((4, 576, 128), BF),
            ((4, 576, 128), F32),
        ]
        feat, dskip, packed, pre_one, taps_one, g_top, g_mid, g_bot = call(
            lambda *refs: main_kernel(sizes, scales, *refs),
            outs,
            scratch,
            1,
            ids,
            own,
            fine,
            pools,
            w_enc,
            w_bot,
            w_mid,
            w_top,
            t_top,
            t_mid,
            c["up_low"],
            c["sum_low"],
            c["up_mid"],
            c["sum_mid"],
            c["pool_low"],
            cost=20,
            grant=33,
        )

        from_left = shift(packed, "gy", ngy, 1)
        from_right = shift(packed, "gy", ngy, -1)
        (line,) = call(join_kernel, [((256, 128), BF)], [], 0, packed, from_left, from_right)
        mate = lax.ppermute(line, "gx", swap)
        edge = jnp.where(core == 0, line[128:192], line[192:256])
        got = outward(jnp.concatenate([line[0:128], mate[0:128], edge], axis=0), ngx, 2)
        got_m = lax.ppermute(got, "gx", swap)
        grad_skip, g_enc = call(
            lambda *refs: tail_kernel(sizes, scales[1], *refs),
            [((4, 32, 256), BF), ((432, 128), BF)],
            [
                ((5, 1152, 128), BF),
                ((5, 192, 128), F32),
                ((4, 64, 128), BF),
                ((4, 576, 128), BF),
                ((4, 96, 128), F32),
            ],
            1,
            ids,
            line,
            mate,
            got,
            got_m,
            pre_one,
            taps_one,
            dskip,
            t_bot,
            t_enc,
            c["up_low"],
            c["up_mid"],
            cost=4,
        )

        grads = ((g_top, 864), (g_mid, 1728), (g_bot, 576), (g_enc, 128))
        tiles = [tiles_of(g) for g, _ in grads]
        spare = -sum(t.shape[0] for t in tiles) % devices
        flat = jnp.concatenate(tiles + [jnp.zeros((spare, 8, 128), BF)], axis=0)
        half = flat.shape[0] // 2
        keep = lax.dynamic_slice_in_dim(flat, core * half, half, 0)
        other = lax.dynamic_slice_in_dim(flat, (1 - core) * half, half, 0)
        other = lax.ppermute(other, "gx", swap)
        mine = (keep.astype(F32) + other.astype(F32)).astype(BF)
        parts = mine.reshape(devices // 2, -1, 128)
        groups = [[i for i in range(devices) if i // ngy % 2 == k] for k in range(2)]
        parts = lax.all_to_all(
            parts, AXES, split_axis=0, concat_axis=0, axis_index_groups=groups, tiled=True
        )
        total = parts.astype(F32).sum(axis=0).astype(BF)
        spread = jnp.broadcast_to(total[None], parts.shape)
        spread = lax.all_to_all(
            spread, AXES, split_axis=0, concat_axis=0, axis_index_groups=groups, tiled=True
        )
        mine = spread.reshape(half, 8, 128)
        other = lax.ppermute(mine, "gx", swap)
        first = jnp.where(core == 0, mine, other)
        second = jnp.where(core == 0, other, mine)
        whole = jnp.concatenate([first, second], axis=0)

        full = []
        start = 0
        for (g, width), t in zip(grads, tiles):
            full.append(from_tiles(whole[start : start + t.shape[0]], g.shape[0], width))
            start += t.shape[0]
        full_top, full_mid, full_bot, full_enc = full
        (full_enc,) = call(finish_kernel, [((64, 864), F32)], [], 0, full_enc)
        mine_bot = full_bot.reshape(3, ngx, block, -1)
        mine_bot = lax.dynamic_index_in_dim(mine_bot, gx, 1, keepdims=False)
        mine_bot = mine_bot.reshape(3 * block, -1)
        return (
            feat.transpose(1, 0, 2),
            grad_skip.transpose(1, 0, 2),
            full_enc,
            full_gradient(mine_bot),
            full_gradient(full_mid),
            full_gradient(full_top),
        )

    in_specs = (P(None, "gx", "gy"), P(), P("gx", None), P(), P(), P(None, "gx", "gy"))
    out_specs = (P(None, "gx", "gy"), P(None, "gx", "gy"), P(), P("gx", None), P(), P())
    return jax.shard_map(step, mesh=mesh, in_specs=in_specs, out_specs=out_specs, check_vma=False)
```

```python
import math

import jax
import jax.numpy as jnp
import numpy as np
from jax import lax
from jax.experimental import pallas as pl
from jax.experimental.pallas import tpu as pltpu
from jax.sharding import PartitionSpec as P


AXES = ("gx", "gy")
BF = jnp.bfloat16
F32 = jnp.float32


def columns(lanes, depth, split):
    col = np.arange(lanes) // depth
    return np.where(col >= split, col - lanes // depth, col), np.arange(lanes) % depth


def upsampling(coarse, fine):
    (col_c, z_c), (col_f, z_f) = (columns(*coarse), columns(*fine))
    hit = (col_c[:, None] == col_f[None, :] // 2) & (z_c[:, None] == z_f[None, :] // 2)
    return hit.astype(np.float32)


TOP = (384, 16, 20)
WIDE = (256, 8, 16)
MID = (128, 8, 12)
LOW = (128, 4, 16)


def constants():
    low_mid = upsampling(LOW, MID)
    mid_top = upsampling(MID, TOP)
    wide_low = upsampling(LOW, WIDE).T / 8.0
    tile_pool = mid_top[:64, :256].T / 8.0
    tile_pool = np.concatenate([tile_pool, tile_pool], axis=1)
    return {
        "up_low": low_mid,
        "sum_low": low_mid.T,
        "up_mid": mid_top,
        "sum_mid": mid_top.T,
        "pool_low": wide_low,
        "pool_tile": tile_pool,
    }


def dot(a, b):
    return jnp.dot(a, b, preferred_element_type=F32)


def dot_nt(a, b):
    return lax.dot_general(a, b, (((1,), (1,)), ((), ())), preferred_element_type=F32)


def dot_split(a, b):
    head = a.astype(BF)
    rest = (a - head.astype(F32)).astype(BF)
    return dot(head, b) + dot(rest, b)


def loop(count, body, unroll=1):
    def step(i, carry):
        for u in range(unroll):
            body(i * unroll + u)
        return carry

    if unroll == count:
        step(0, 0)
    else:
        lax.fori_loop(0, count // unroll, step, 0)


def lane(length):
    return lax.broadcasted_iota(jnp.int32, (1, length), 1)


def inside(region, tile_cols, total_cols, index):
    lanes, depth, split = region
    col = lane(lanes) // depth
    col = jnp.where(col >= split, col - lanes // depth, col) + index * tile_cols
    return jnp.where((col >= 0) & (col < total_cols), 1.0, 0.0)


def row_ok(row, total):
    return jnp.where((row >= 0) & (row < total), 1.0, 0.0)


def depth_masks(shape, depth):
    z = lax.broadcasted_iota(jnp.int32, shape, 1) % depth
    below = jnp.where(z == depth - 1, 0.0, 1.0).astype(BF)
    above = jnp.where(z == 0, 0.0, 1.0).astype(BF)
    return below, above


def put_taps(dst, row, first, width, value, depth):
    chans, lanes = value.shape
    below, above = depth_masks(value.shape, depth)
    kinds = (value * below, value, value * above)
    for b in range(3):
        for e in range(3):
            shift = (b - 1) * depth + (e - 1)
            piece = kinds[e]
            if shift:
                piece = pltpu.roll(piece, (-shift) % lanes, 1)
            start = (3 * b + e) * width + first
            dst[row, start : start + chans, :] = piece


def sigmoid(v):
    return 1.0 / (1.0 + jnp.exp(-v))


def silu(v):
    return v * sigmoid(v)


def slope(v):
    s = sigmoid(v)
    return s * (1.0 + v * (1.0 - s))


def row_sum(ref, row, chans):
    return (
        ref[row, 0:chans, :]
        + ref[row + 1, chans : 2 * chans, :]
        + ref[row + 2, 2 * chans : 3 * chans, :]
    )


def put_padded(out, row, value):
    rows, width = value.shape
    out[row : row + rows, 0:width] = value.astype(BF)
    out[row : row + rows, width:] = jnp.zeros((rows, out.shape[1] - width), BF)


def pool_kernel(skip, cot, pool_tile, to_left, to_right):
    for r in range(4):
        to_left[r] = skip[r, :, 0:128]
        to_left[4 + r] = cot[r, :, 0:128]
        to_right[r] = skip[r, :, 128:256]
        to_right[4 + r] = cot[r, :, 128:256]
    for q in range(2):
        pooled = dot(skip[2 * q], pool_tile[...]) + dot(skip[2 * q + 1], pool_tile[...])
        pooled = pooled.astype(BF)
        to_left[8 + q] = pooled
        to_right[8 + q] = pooled


def widen_kernel(skip, cot, own, right, left, out):
    first = jnp.where(lax.broadcasted_iota(jnp.int32, (32, 128), 1) < 64, 1.0, 0.0)
    head = first.astype(BF)
    tail = (1.0 - first).astype(BF)
    for r in range(4):
        for k, tile in enumerate((skip, cot)):
            base = 12 * k + 3 * r
            out[base] = tile[r, :, 0:128]
            out[base + 1] = tile[r, :, 128:256]
            out[base + 2] = right[4 * k + r] * head + left[4 * k + r] * tail
    for q in range(2):
        out[24 + 2 * q] = own[8 + q] * head + right[8 + q] * tail
        out[25 + 2 * q] = left[8 + q] * tail


def gather_kernel(tiles, block, *refs):
    (ids, own, mate, got, got_m, far, far_m, w_mine, w_mate) = refs[:9]
    (fine, pools, w_out, w_all, w_flat) = refs[9:14]
    gx = ids[0]
    core = gx % 2
    low = jnp.where(core == 0, 1.0, 0.0)
    below = jnp.full((32, 32, 128), low).astype(BF)
    above = jnp.full((32, 32, 128), 1.0 - low).astype(BF)
    lower = got[...] * below + got_m[...] * above
    upper = got_m[...] * below + got[...] * above
    fine[0] = upper[0:24] * below[0:24] + mate[0:24] * above[0:24]
    fine[1] = mate[0:24] * below[0:24] + lower[0:24] * above[0:24]
    far_lower = far[...] * below[0:8] + far_m[...] * above[0:8]
    far_upper = far_m[...] * below[0:8] + far[...] * above[0:8]
    first = own[24:28] * below[0:4] + mate[24:28] * above[0:4]
    second = mate[24:28] * below[0:4] + own[24:28] * above[0:4]
    for step, tile in (
        (-4, far_upper[4:8]),
        (-3, far_upper[0:4]),
        (-2, upper[28:32]),
        (-1, upper[24:28]),
        (0, first),
        (1, second),
        (2, lower[24:28]),
        (3, lower[28:32]),
        (4, far_lower[0:4]),
        (5, far_lower[4:8]),
    ):
        pools[step + 5 - core] = tile

    slabs = w_all.shape[1]
    around = tiles // 4
    y = (gx // 2) % around
    side = gx // (2 * around)
    for lane_core, ref in ((core, w_mine), (1 - core, w_mate)):
        for far in range(2):
            for k in range(around):
                z_part = (side + far) % 2
                y_part = (y + around - k) % around
                at = (far * around + k) * slabs
                w_all[(z_part * around + y_part) * 2 + lane_core] = ref[at : at + slabs]
    lanes = w_flat.shape[1] // 128
    for b in range(tiles):
        rows = w_all[b].reshape(lanes * block, 128)
        for l in range(lanes):
            w_flat[b * block : b * block + block, 128 * l : 128 * l + 128] = rows[
                l * block : l * block + block
            ]
    put_forward(w_flat, w_out)


def put_forward(w, out):
    rows = w.shape[0]
    width = out.shape[1]
    for a in range(3):
        out[rows * a : rows * a + rows, :] = w[:, a * width : (a + 1) * width]


def put_backward(w, out):
    chans = out.shape[0] // 3
    i = lax.broadcasted_iota(jnp.int32, (chans, chans), 0)
    j = lax.broadcasted_iota(jnp.int32, (chans, chans), 1)
    unit = jnp.where(i == j, 1.0, 0.0).astype(BF)
    for a in range(3):
        taps = [26 - 9 * a - k for k in range(9)]
        stacked = jnp.concatenate([w[:, t * chans : t * chans + chans] for t in taps], axis=0)
        out[chans * a : chans * a + chans, :] = dot_nt(unit, stacked).astype(BF)


def weight_kernel(forward, backward, *refs):
    sources, outs = refs[: len(forward)], refs[len(forward) :]
    k = 0
    for w, fwd, bwd in zip(sources, forward, backward):
        if fwd:
            put_forward(w, outs[k])
            k += 1
        if bwd:
            put_backward(w, outs[k])
            k += 1


def main_kernel(sizes, scales, *refs):
    (ids, own, fine, pools) = refs[:4]
    up, down = fine.at[0], fine.at[1]
    (w_enc, w_bot, w_mid, w_top, t_top, t_mid) = refs[4:10]
    (up_low, sum_low, up_mid, sum_mid, pool_low) = refs[10:15]
    (feat, dskip, packed, pre_one, taps_out, g_top, g_mid, g_bot) = refs[15:23]
    (pool_s, taps_a, sum_a, act_a, taps_b, sum_b, act_b) = refs[23:30]
    (taps_c, sum_c, act_c, pre_c, taps_d, sum_d, err_d) = refs[30:37]
    (taps_e, sum_e, err_c, stack, taps_f, sum_f) = refs[37:43]
    (rows_all, cols_all) = sizes
    (scale_top, scale_mid, scale_low) = scales
    gx, gy = ids[0], ids[1]
    rows_mid, rows_low = rows_all // 2, rows_all // 4

    for k in range(16):
        tile, slab = 5 + (k - 7) // 2, 2 * ((k - 7) % 2)
        pool_s[k, :, 0:128] = pools[tile, slab]
        pool_s[k, :, 128:256] = pools[tile, slab + 1]

    def enc_taps(k):
        put_taps(taps_a, k, 0, 32, pool_s[k], 8)
        sum_a[k] = dot(w_enc[...], taps_a[k])

    loop(16, enc_taps, 4)
    wide_in = inside(WIDE, 8, cols_all // 2, gy)

    def enc_act(k):
        value = silu(row_sum(sum_a, k, 64)) * (wide_in * row_ok(gx * 2 + k - 6, rows_mid))
        act_a[k] = value.astype(BF)

    loop(14, enc_act, 2)
    for m in range(4):
        pre = row_sum(sum_a, m + 5, 64)
        pre_one[m] = jnp.where(lane(128) < 96, pre[:, 0:128], pre[:, 128:256])
        taps_out[m] = taps_a[m + 6, :, 0:128]

    def low_taps(k):
        pooled = dot(act_a[2 * k], pool_low[...]) + dot(act_a[2 * k + 1], pool_low[...])
        put_taps(taps_b, k, 0, 64, pooled.astype(BF), 4)
        sum_b[k] = dot(w_bot[...], taps_b[k])

    loop(7, low_taps, 7)
    low_in = inside(LOW, 4, cols_all // 4, gy)
    mid_in = inside(MID, 8, cols_all // 2, gy)
    pick = jnp.where(lax.broadcasted_iota(jnp.int32, (64, 128), 1) < 96, 1.0, 0.0)
    near = pick.astype(BF)
    away = (1.0 - pick).astype(BF)

    def low_act(k):
        value = silu(row_sum(sum_b, k, 128)) * (low_in * row_ok(gx + k - 2, rows_low))
        act_b[k] = dot(value.astype(BF), up_low[...]).astype(BF)

    loop(5, low_act, 5)

    def mid_taps(k):
        put_taps(taps_c, k, 0, 192, act_b[(k + 1) // 2], 8)
        narrow = act_a[k + 3, :, 0:128] * near + act_a[k + 3, :, 128:256] * away
        put_taps(taps_c, k, 128, 192, narrow, 8)
        sum_c[k] = dot(w_mid[...], taps_c[k])

    loop(8, mid_taps, 2)

    def mid_act(k):
        pre = row_sum(sum_c, k, 64)
        pre_c[k] = pre
        value = silu(pre) * (mid_in * row_ok(gx * 2 + k - 2, rows_mid))
        act_c[k] = dot(value.astype(BF), up_mid[...]).astype(BF)

    loop(6, mid_act, 6)

    def skip_row(kind, k):
        part = (up, own, down)[k // 4]
        base = 12 * kind + 3 * (k % 4)
        return jnp.concatenate([part[base], part[base + 1], part[base + 2]], axis=1)

    for k in range(12):
        put_taps(taps_d, k, 64, 96, skip_row(0, k), 16)

    def top_taps(j):
        for half in range(2):
            put_taps(taps_d, 2 * j + half, 0, 96, act_c[j], 16)
            sum_d[2 * j + half] = dot(w_top[...], taps_d[2 * j + half])

    loop(6, top_taps, 2)
    for k in range(10):
        pre = row_sum(sum_d, k, 32)
        s = sigmoid(pre)
        if 3 <= k < 7:
            feat[k - 3] = (pre * s)[:, 0:256].astype(BF)
        cot = skip_row(1, k + 1).astype(F32)
        err_d[k] = (cot * (s * (1.0 + pre * (1.0 - s)))).astype(BF)

    def top_back(k):
        put_taps(taps_e, k, 0, 32, err_d[k], 16)
        sum_e[k] = dot(t_top[...], taps_e[k])

    loop(10, top_back, 2)

    total = None
    for k in range(6):
        parts = []
        for a in range(3):
            r = k - a
            own_row = 0 <= r < 4
            parts.append(err_d[r + 3, :, 0:256] if own_row else jnp.zeros((32, 256), BF))
        term = dot_nt(jnp.concatenate(parts, axis=0), taps_d[k + 3, :, 0:256])
        total = term if total is None else total + term
    put_padded(g_top, 0, total * scale_top)

    def mid_err(m):
        one = row_sum(sum_e, 2 * m, 96)
        two = row_sum(sum_e, 2 * m + 1, 96)
        whole = dot_split(one[0:64] + two[0:64], sum_mid[...])
        keep = mid_in * row_ok(gx * 2 + m - 1, rows_mid)
        err_c[m] = (whole * slope(pre_c[m + 1]) * keep).astype(BF)

    loop(4, mid_err, 4)
    for r in range(4):
        dskip[r] = row_sum(sum_e, r + 2, 96)[64:96, 0:256]

    def mid_back(m):
        put_taps(taps_f, m, 0, 64, err_c[m], 8)
        sum_f[m] = dot(t_mid[...], taps_f[m])

    loop(4, mid_back, 2)
    own_mid = jnp.where(lax.broadcasted_iota(jnp.int32, (64, 128), 1) < 64, 1.0, 0.0).astype(BF)
    for k in range(4):
        for a in range(3):
            r = k - a
            piece = err_c[r + 1] * own_mid if 0 <= r < 2 else jnp.zeros((64, 128), BF)
            stack[k, 64 * a : 64 * a + 64, :] = piece
    total = None
    for k in range(4):
        term = dot_nt(stack[k], taps_c[k + 2])
        total = term if total is None else total + term
    put_padded(g_mid, 0, total * scale_mid)

    one = row_sum(sum_f, 0, 192)
    two = row_sum(sum_f, 1, 192)
    whole = dot_split(one[0:128] + two[0:128], sum_low[...])
    keep = jnp.where(lane(128) < 16, 1.0, 0.0)
    err_low = (whole * slope(row_sum(sum_b, 2, 128)) * keep).astype(BF)
    packed[0:128, :] = err_low
    both = jnp.where(lane(128) < 64, one[128:192], pltpu.roll(two[128:192], 64, 1))
    packed[128:192, :] = both.astype(BF)
    for a in range(3):
        put_padded(g_bot, 128 * a, dot_nt(err_low, taps_b[a + 2]) * scale_low)


def join_kernel(own, left, right, out):
    wide = [ref[0:128, :].astype(F32) for ref in (own, right, left)]
    err = wide[0] + pltpu.roll(wide[1], 16, 1) + pltpu.roll(wide[2], 112, 1)
    out[0:128, :] = err.astype(BF)
    at = lane(128)
    mine, right, left = [ref[128:192, :].astype(F32) for ref in (own, right, left)]
    turned = [pltpu.roll(v, 64, 1) for v in (mine, right, left)]
    for row, (a, b, c) in enumerate(((mine, turned[1], turned[2]), (turned[0], right, left))):
        value = jnp.where(at < 64, a, jnp.where(at < 96, b, c))
        out[128 + 64 * row : 192 + 64 * row, :] = value.astype(BF)


def tail_kernel(sizes, scale_mid, *refs):
    (ids, own, mate, got, got_m, pre_one, taps_in, dskip) = refs[:8]
    (t_bot, t_enc, up_low, up_mid) = refs[8:12]
    (grad_skip, g_enc) = refs[12:14]
    (taps_a, sum_a, err_s, taps_b, sum_b) = refs[14:19]
    (rows_all, cols_all) = sizes
    gx, gy = ids[0], ids[1]
    rows_mid = rows_all // 2
    mid_in = inside(MID, 8, cols_all // 2, gy)

    low = jnp.where(gx % 2 == 0, 1.0, 0.0)
    high = 1.0 - low
    below = jnp.full((320, 128), low).astype(BF)
    above = jnp.full((320, 128), high).astype(BF)
    lower = got[...] * below + got_m[...] * above
    upper = got_m[...] * below + got[...] * above
    below, above = below[0:128], above[0:128]
    rows = (
        upper[128:256] * below + upper[0:128] * above,
        upper[0:128] * below + mate[0:128, :] * above,
        own[0:128, :],
        mate[0:128, :] * below + lower[0:128] * above,
        lower[0:128] * below + lower[128:256] * above,
    )
    for k, value in enumerate(rows):
        put_taps(taps_a, k, 0, 128, value, 4)
        sum_a[k] = dot(t_bot[...], taps_a[k])
    ups = [dot_split(row_sum(sum_a, k, 64), up_low[...]) * 0.125 for k in range(3)]
    parts = (
        upper[256:320].astype(F32) * low + mate[192:256, :].astype(F32) * high,
        own[128:192, :].astype(F32),
        own[192:256, :].astype(F32),
        mate[128:192, :].astype(F32) * low + lower[256:320].astype(F32) * high,
    )
    for m in range(4):
        part = parts[m]
        keep = mid_in * row_ok(gx * 2 + m - 1, rows_mid)
        err = (part + ups[(m + 1) // 2]) * slope(pre_one[m]) * keep
        err = err.astype(BF)
        err_s[m] = err
        put_taps(taps_b, m, 0, 64, err, 8)
        sum_b[m] = dot(t_enc[...], taps_b[m])
    own_mid = jnp.where(lax.broadcasted_iota(jnp.int32, (64, 128), 1) < 64, 1.0, 0.0).astype(BF)
    total = None
    for k in range(4):
        parts = []
        for a in range(3):
            r = k - a
            parts.append(err_s[r + 1] * own_mid if 0 <= r < 2 else jnp.zeros((64, 128), BF))
        term = dot_nt(jnp.concatenate(parts, axis=0), taps_in[k])
        total = term if total is None else total + term
    total = (total * scale_mid).astype(BF)
    g_enc[0:192, :] = total[:, 0:128]
    g_enc[192:384, :] = total[:, 128:256]
    rest = [total[48 * q : 48 * q + 48, 256:288] for q in range(4)]
    g_enc[384:432, :] = jnp.concatenate(rest, axis=1)
    for q in range(2):
        fine = dot_split(row_sum(sum_b, q, 32), up_mid[:, 0:256]) * 0.125
        for half in range(2):
            r = 2 * q + half
            grad_skip[r] = (dskip[r] + fine).astype(BF)


def finish_kernel(g, out):
    rest = jnp.concatenate([g[384:432, 32 * q : 32 * q + 32] for q in range(4)], axis=0)
    pieces = []
    for a in range(3):
        at = 64 * a
        pieces += [g[at : at + 64, :], g[192 + at : 256 + at, :], rest[at : at + 64, :]]
    out[...] = jnp.concatenate(pieces, axis=1).astype(F32)


VMEM = pl.BlockSpec(memory_space=pltpu.VMEM)
SMEM = pl.BlockSpec(memory_space=pltpu.SMEM)


def call(kernel, outs, scratch, scalars, *args, cost=1, grant=8):
    return pl.pallas_call(
        kernel,
        out_shape=[jax.ShapeDtypeStruct(s, d) for s, d in outs],
        in_specs=[SMEM] * scalars + [VMEM] * (len(args) - scalars),
        out_specs=[VMEM] * len(outs),
        scratch_shapes=[pltpu.VMEM(s, d) for s, d in scratch],
        compiler_params=pltpu.CompilerParams(vmem_limit_bytes=grant * 1024 * 1024),
        cost_estimate=pl.CostEstimate(
            flops=cost * 500_000_000, bytes_accessed=cost * 1_000_000, transcendentals=0
        ),
    )(*args)


def shift(value, axis, count, step):
    return lax.ppermute(value, axis, [(i, i + step) for i in range(count) if 0 <= i + step < count])


def outward(value, count, step):
    pairs = [(i, i + step if i % 2 else i - step) for i in range(count)]
    return lax.ppermute(value, "gx", [(i, j) for i, j in pairs if 0 <= j < count])


def tiles_of(g):
    rows, width = g.shape
    return g.reshape(rows // 8, 8, width // 128, 128).transpose(0, 2, 1, 3).reshape(-1, 8, 128)


def from_tiles(tiles, rows, width):
    wide = -(-width // 128)
    g = tiles.reshape(rows // 8, wide, 8, 128).transpose(0, 2, 1, 3).reshape(rows, wide * 128)
    return g[:, :width]


def full_gradient(g):
    rows, _ = g.shape
    out = rows // 3
    return jnp.concatenate([g[out * a : out * a + out] for a in range(3)], axis=1).astype(F32)


def solution(mesh):
    ngx, ngy = mesh.shape["gx"], mesh.shape["gy"]
    devices = ngx * ngy
    const = {k: np.asarray(v) for k, v in constants().items()}

    def step(skip_input, w_encoder, w_bottom, w_middle, w_upper, cotangent):
        gx, gy = lax.axis_index("gx"), lax.axis_index("gy")
        ids = jnp.stack([gx, gy]).astype(jnp.int32)
        rows_all, cols_all = 4 * ngx, 16 * ngy
        sizes = (rows_all, cols_all)
        cells = rows_all * cols_all * 16
        scales = tuple(1.0 / math.sqrt(cells // k) for k in (1, 8, 64))
        c = {k: jnp.asarray(v, BF) for k, v in const.items()}

        block, width = w_bottom.shape
        slabs = block * 2048 // 4096
        weight = jnp.pad(w_bottom, ((0, 0), (0, 2048 - width)))
        lanes = weight.shape[1] // 128
        weight = weight.reshape(block, lanes, 128).transpose(1, 0, 2).reshape(slabs, 32, 128)

        swap = [(i, i ^ 1) for i in range(ngx)]
        around = ngx // 4

        def along_y(i, k):
            side, y, core = i // (2 * around), i // 2 % around, i % 2
            return (side * around + (y + k) % around) * 2 + core

        part = ngy // 4 if ngy % 4 == 0 else ngy

        def mirrored(i):
            x, y = i // ngy, i % ngy
            y = (ngy // part - 1 - y // part) * part + y % part
            return (x + ngx // 2) % ngx * ngy + y

        w_line = [weight]
        for k in range(1, around):
            w_line.append(lax.ppermute(weight, "gx", [(i, along_y(i, k)) for i in range(ngx)]))
        w_line = jnp.concatenate(w_line, axis=0)
        w_far = lax.ppermute(w_line, AXES, [(i, mirrored(i)) for i in range(devices)])

        skip = skip_input.transpose(1, 0, 2)
        cot = cotangent.transpose(1, 0, 2)
        to_left, to_right = call(
            pool_kernel, [((10, 32, 128), BF)] * 2, [], 0, skip, cot, c["pool_tile"]
        )
        right = shift(to_left, "gy", ngy, -1)
        left = shift(to_right, "gy", ngy, 1)
        (own,) = call(widen_kernel, [((28, 32, 128), BF)], [], 0, skip, cot, to_left, right, left)
        core = gx % 2
        mate = lax.ppermute(own, "gx", swap)
        got = outward(jnp.concatenate([own, mate[24:28]], axis=0), ngx, 2)
        far = outward(jnp.concatenate([own[24:28], mate[24:28]], axis=0), ngx, 4)
        got, w_far = lax.optimization_barrier((got, w_far))
        w_mine = jnp.concatenate([w_line, w_far], axis=0)
        w_mate = lax.ppermute(w_mine, "gx", swap)
        got_m = lax.ppermute(got, "gx", swap)
        far_m = lax.ppermute(far, "gx", swap)
        fine, pools, w_bot, _, w_flat = call(
            lambda *refs: gather_kernel(ngx, block, *refs),
            [
                ((2, 24, 32, 128), BF),
                ((11, 4, 32, 128), BF),
                ((384, 576), BF),
                ((ngx, slabs, 32, 128), BF),
                ((ngx * block, lanes * 128), BF),
            ],
            [],
            1,
            ids,
            own,
            mate,
            got,
            got_m,
            far,
            far_m,
            w_mine,
            w_mate,
        )
        w_enc, t_enc, w_mid, t_mid, w_top, t_top = call(
            lambda *refs: weight_kernel((1, 1, 1), (1, 1, 1), *refs),
            [
                ((192, 288), BF),
                ((96, 576), BF),
                ((192, 1728), BF),
                ((576, 576), BF),
                ((96, 864), BF),
                ((288, 288), BF),
            ],
            [],
            0,
            w_encoder,
            w_middle,
            w_upper,
            cost=4,
        )
        (t_bot,) = call(
            lambda *refs: weight_kernel((0,), (1,), *refs),
            [((192, 1152), BF)],
            [],
            0,
            w_flat,
            cost=2,
        )

        outs = [
            ((4, 32, 256), BF),
            ((4, 32, 256), F32),
            ((192, 128), BF),
            ((4, 64, 128), F32),
            ((4, 288, 128), BF),
            ((96, 896), BF),
            ((192, 1792), BF),
            ((384, 640), BF),
        ]
        scratch = [
            ((16, 32, 256), BF),
            ((16, 288, 256), BF),
            ((16, 192, 256), F32),
            ((14, 64, 256), BF),
            ((7, 576, 128), BF),
            ((7, 384, 128), F32),
            ((5, 128, 128), BF),
            ((8, 1728, 128), BF),
            ((8, 192, 128), F32),
            ((6, 64, 384), BF),
            ((6, 64, 128), F32),
            ((12, 864, 384), BF),
            ((12, 96, 384), F32),
            ((10, 32, 384), BF),
            ((10, 288, 384), BF),
            ((10, 288, 384), F32),
            ((4, 64, 128), BF),
            ((4, 192, 128), BF),
            ((4, 576, 128), BF),
            ((4, 576, 128), F32),
        ]
        feat, dskip, packed, pre_one, taps_one, g_top, g_mid, g_bot = call(
            lambda *refs: main_kernel(sizes, scales, *refs),
            outs,
            scratch,
            1,
            ids,
            own,
            fine,
            pools,
            w_enc,
            w_bot,
            w_mid,
            w_top,
            t_top,
            t_mid,
            c["up_low"],
            c["sum_low"],
            c["up_mid"],
            c["sum_mid"],
            c["pool_low"],
            cost=20,
            grant=33,
        )

        def between_cores(tiles):
            half = tiles.shape[0] // 2
            keep = lax.dynamic_slice_in_dim(tiles, core * half, half, 0)
            other = lax.dynamic_slice_in_dim(tiles, (1 - core) * half, half, 0)
            other = lax.ppermute(other, "gx", swap)
            return (keep.astype(F32) + other.astype(F32)).astype(BF)

        grads = ((g_top, 864), (g_mid, 1728), (g_bot, 576))
        tiles = [tiles_of(g) for g, _ in grads]
        mine_main = between_cores(jnp.concatenate(tiles, axis=0))
        cut = mine_main.shape[0]
        last = cut + 27
        spare = -last % (devices // 2) + 27
        mine_main = jnp.pad(mine_main, ((0, spare), (0, 0), (0, 0)))

        from_left = shift(packed, "gy", ngy, 1)
        from_right = shift(packed, "gy", ngy, -1)
        (line,) = call(join_kernel, [((256, 128), BF)], [], 0, packed, from_left, from_right)
        mate = lax.ppermute(line, "gx", swap)
        edge = jnp.where(core == 0, line[128:192], line[192:256])
        got = outward(jnp.concatenate([line[0:128], mate[0:128], edge], axis=0), ngx, 2)
        got_m = lax.ppermute(got, "gx", swap)
        got_m, mine_main = lax.optimization_barrier((got_m, mine_main))
        grad_skip, g_enc = call(
            lambda *refs: tail_kernel(sizes, scales[1], *refs),
            [((4, 32, 256), BF), ((432, 128), BF)],
            [
                ((5, 1152, 128), BF),
                ((5, 192, 128), F32),
                ((4, 64, 128), BF),
                ((4, 576, 128), BF),
                ((4, 96, 128), F32),
            ],
            1,
            ids,
            line,
            mate,
            got,
            got_m,
            pre_one,
            taps_one,
            dskip,
            t_bot,
            t_enc,
            c["up_low"],
            c["up_mid"],
            cost=4,
        )

        mine_enc = between_cores(tiles_of(g_enc))
        mine = lax.dynamic_update_slice(mine_main, mine_enc, (cut, 0, 0))
        parts = mine.reshape(devices // 2, -1, 128)
        groups = [[i for i in range(devices) if i // ngy % 2 == k] for k in range(2)]
        parts = lax.all_to_all(
            parts, AXES, split_axis=0, concat_axis=0, axis_index_groups=groups, tiled=True
        )
        total = parts.astype(F32).sum(axis=0).astype(BF)
        spread = jnp.broadcast_to(total[None], parts.shape)
        spread = lax.all_to_all(
            spread, AXES, split_axis=0, concat_axis=0, axis_index_groups=groups, tiled=True
        )
        mine = spread.reshape(-1, 8, 128)
        other = lax.ppermute(mine, "gx", swap)
        first = jnp.where(core == 0, mine, other)
        second = jnp.where(core == 0, other, mine)
        whole = jnp.concatenate([first[:cut], second[:cut]], axis=0)
        full_enc = jnp.concatenate([first[cut:last], second[cut:last]], axis=0)
        full_enc = from_tiles(full_enc, 432, 128)

        full = []
        start = 0
        for (g, width), t in zip(grads, tiles):
            full.append(from_tiles(whole[start : start + t.shape[0]], g.shape[0], width))
            start += t.shape[0]
        full_top, full_mid, full_bot = full
        (full_enc,) = call(finish_kernel, [((64, 864), F32)], [], 0, full_enc)
        mine_bot = full_bot.reshape(3, ngx, block, -1)
        mine_bot = lax.dynamic_index_in_dim(mine_bot, gx, 1, keepdims=False)
        mine_bot = mine_bot.reshape(3 * block, -1)
        return (
            feat.transpose(1, 0, 2),
            grad_skip.transpose(1, 0, 2),
            full_enc,
            full_gradient(mine_bot),
            full_gradient(full_mid),
            full_gradient(full_top),
        )

    in_specs = (P(None, "gx", "gy"), P(), P("gx", None), P(), P(), P(None, "gx", "gy"))
    out_specs = (P(None, "gx", "gy"), P(None, "gx", "gy"), P(), P("gx", None), P(), P())
    return jax.shard_map(step, mesh=mesh, in_specs=in_specs, out_specs=out_specs, check_vma=False)
```

```python
import math

import jax
import jax.numpy as jnp
import numpy as np
from jax import lax
from jax.experimental import pallas as pl
from jax.experimental.pallas import tpu as pltpu
from jax.sharding import PartitionSpec as P


AXES = ("gx", "gy")
BF = jnp.bfloat16
F32 = jnp.float32


def columns(lanes, depth, split):
    col = np.arange(lanes) // depth
    return np.where(col >= split, col - lanes // depth, col), np.arange(lanes) % depth


def upsampling(coarse, fine):
    (col_c, z_c), (col_f, z_f) = (columns(*coarse), columns(*fine))
    hit = (col_c[:, None] == col_f[None, :] // 2) & (z_c[:, None] == z_f[None, :] // 2)
    return hit.astype(np.float32)


TOP = (384, 16, 20)
WIDE = (256, 8, 16)
MID = (128, 8, 12)
LOW = (128, 4, 16)


def constants():
    low_mid = upsampling(LOW, MID)
    mid_top = upsampling(MID, TOP)
    wide_low = upsampling(LOW, WIDE).T / 8.0
    tile_pool = mid_top[:64, :256].T / 8.0
    tile_pool = np.concatenate([tile_pool, tile_pool], axis=1)
    return {
        "up_low": low_mid,
        "sum_low": low_mid.T,
        "up_mid": mid_top,
        "sum_mid": mid_top.T,
        "pool_low": wide_low,
        "pool_tile": tile_pool,
    }


def dot(a, b):
    return jnp.dot(a, b, preferred_element_type=F32)


def dot_nt(a, b):
    return lax.dot_general(a, b, (((1,), (1,)), ((), ())), preferred_element_type=F32)


def dot_split(a, b):
    head = a.astype(BF)
    rest = (a - head.astype(F32)).astype(BF)
    return dot(head, b) + dot(rest, b)


def loop(count, body, unroll=1):
    def step(i, carry):
        for u in range(unroll):
            body(i * unroll + u)
        return carry

    if unroll == count:
        step(0, 0)
    else:
        lax.fori_loop(0, count // unroll, step, 0)


def lane(length):
    return lax.broadcasted_iota(jnp.int32, (1, length), 1)


def inside(region, tile_cols, total_cols, index):
    lanes, depth, split = region
    col = lane(lanes) // depth
    col = jnp.where(col >= split, col - lanes // depth, col) + index * tile_cols
    return jnp.where((col >= 0) & (col < total_cols), 1.0, 0.0)


def row_ok(row, total):
    return jnp.where((row >= 0) & (row < total), 1.0, 0.0)


def depth_masks(shape, depth):
    z = lax.broadcasted_iota(jnp.int32, shape, 1) % depth
    below = jnp.where(z == depth - 1, 0.0, 1.0).astype(BF)
    above = jnp.where(z == 0, 0.0, 1.0).astype(BF)
    return below, above


def put_taps(dst, row, first, width, value, depth):
    chans, lanes = value.shape
    below, above = depth_masks(value.shape, depth)
    kinds = (value * below, value, value * above)
    for b in range(3):
        for e in range(3):
            shift = (b - 1) * depth + (e - 1)
            piece = kinds[e]
            if shift:
                piece = pltpu.roll(piece, (-shift) % lanes, 1)
            start = (3 * b + e) * width + first
            dst[row, start : start + chans, :] = piece


def sigmoid(v):
    return 1.0 / (1.0 + jnp.exp(-v))


def silu(v):
    return v * sigmoid(v)


def slope(v):
    s = sigmoid(v)
    return s * (1.0 + v * (1.0 - s))


def row_sum(ref, row, chans):
    return (
        ref[row, 0:chans, :]
        + ref[row + 1, chans : 2 * chans, :]
        + ref[row + 2, 2 * chans : 3 * chans, :]
    )


def put_padded(out, row, value):
    rows, width = value.shape
    out[row : row + rows, 0:width] = value.astype(BF)
    out[row : row + rows, width:] = jnp.zeros((rows, out.shape[1] - width), BF)


def pool_kernel(skip, cot, pool_tile, to_left, to_right):
    for r in range(4):
        to_left[r] = skip[r, :, 0:128]
        to_left[4 + r] = cot[r, :, 0:128]
        to_right[r] = skip[r, :, 128:256]
        to_right[4 + r] = cot[r, :, 128:256]
    for q in range(2):
        pooled = dot(skip[2 * q], pool_tile[...]) + dot(skip[2 * q + 1], pool_tile[...])
        pooled = pooled.astype(BF)
        to_left[8 + q] = pooled
        to_right[8 + q] = pooled


def widen_kernel(skip, cot, own, right, left, out):
    first = jnp.where(lax.broadcasted_iota(jnp.int32, (32, 128), 1) < 64, 1.0, 0.0)
    head = first.astype(BF)
    tail = (1.0 - first).astype(BF)
    for r in range(4):
        for k, tile in enumerate((skip, cot)):
            base = 12 * k + 3 * r
            out[base] = tile[r, :, 0:128]
            out[base + 1] = tile[r, :, 128:256]
            out[base + 2] = right[4 * k + r] * head + left[4 * k + r] * tail
    for q in range(2):
        out[24 + 2 * q] = own[8 + q] * head + right[8 + q] * tail
        out[25 + 2 * q] = left[8 + q] * tail


def gather_kernel(tiles, block, *refs):
    (ids, own, mate, got, got_m, far, far_m, w_mine, w_mate) = refs[:9]
    (fine, pools, w_out, w_all, w_flat) = refs[9:14]
    gx = ids[0]
    core = gx % 2
    low = jnp.where(core == 0, 1.0, 0.0)
    below = jnp.full((32, 32, 128), low).astype(BF)
    above = jnp.full((32, 32, 128), 1.0 - low).astype(BF)
    lower = got[...] * below + got_m[...] * above
    upper = got_m[...] * below + got[...] * above
    fine[0] = upper[0:24] * below[0:24] + mate[0:24] * above[0:24]
    fine[1] = mate[0:24] * below[0:24] + lower[0:24] * above[0:24]
    far_lower = far[...] * below[0:8] + far_m[...] * above[0:8]
    far_upper = far_m[...] * below[0:8] + far[...] * above[0:8]
    first = own[24:28] * below[0:4] + mate[24:28] * above[0:4]
    second = mate[24:28] * below[0:4] + own[24:28] * above[0:4]
    for step, tile in (
        (-4, far_upper[4:8]),
        (-3, far_upper[0:4]),
        (-2, upper[28:32]),
        (-1, upper[24:28]),
        (0, first),
        (1, second),
        (2, lower[24:28]),
        (3, lower[28:32]),
        (4, far_lower[0:4]),
        (5, far_lower[4:8]),
    ):
        pools[step + 5 - core] = tile

    slabs = w_all.shape[1]
    around = tiles // 4
    y = (gx // 2) % around
    side = gx // (2 * around)
    for lane_core, ref in ((core, w_mine), (1 - core, w_mate)):
        for far in range(2):
            for k in range(around):
                z_part = (side + far) % 2
                y_part = (y + around - k) % around
                at = (far * around + k) * slabs
                w_all[(z_part * around + y_part) * 2 + lane_core] = ref[at : at + slabs]
    lanes = w_flat.shape[1] // 128
    for b in range(tiles):
        rows = w_all[b].reshape(lanes * block, 128)
        for l in range(lanes):
            w_flat[b * block : b * block + block, 128 * l : 128 * l + 128] = rows[
                l * block : l * block + block
            ]
    put_forward(w_flat, w_out)


def put_forward(w, out):
    rows = w.shape[0]
    width = out.shape[1]
    for a in range(3):
        out[rows * a : rows * a + rows, :] = w[:, a * width : (a + 1) * width]


def put_backward(w, out):
    chans = out.shape[0] // 3
    i = lax.broadcasted_iota(jnp.int32, (chans, chans), 0)
    j = lax.broadcasted_iota(jnp.int32, (chans, chans), 1)
    unit = jnp.where(i == j, 1.0, 0.0).astype(BF)
    for a in range(3):
        taps = [26 - 9 * a - k for k in range(9)]
        stacked = jnp.concatenate([w[:, t * chans : t * chans + chans] for t in taps], axis=0)
        out[chans * a : chans * a + chans, :] = dot_nt(unit, stacked).astype(BF)


def weight_kernel(forward, backward, *refs):
    sources, outs = refs[: len(forward)], refs[len(forward) :]
    k = 0
    for w, fwd, bwd in zip(sources, forward, backward):
        if fwd:
            put_forward(w, outs[k])
            k += 1
        if bwd:
            put_backward(w, outs[k])
            k += 1


def main_kernel(sizes, scales, *refs):
    (ids, own, fine, pools) = refs[:4]
    up, down = fine.at[0], fine.at[1]
    (w_enc, w_bot, w_mid, w_top, t_top, t_mid) = refs[4:10]
    (up_low, sum_low, up_mid, sum_mid, pool_low) = refs[10:15]
    (feat, dskip, packed, pre_one, taps_out, g_top, g_mid, g_bot) = refs[15:23]
    (pool_s, taps_a, sum_a, act_a, taps_b, sum_b, act_b) = refs[23:30]
    (taps_c, sum_c, act_c, pre_c, taps_d, sum_d, err_d) = refs[30:37]
    (taps_e, sum_e, err_c, stack, taps_f, sum_f) = refs[37:43]
    (rows_all, cols_all) = sizes
    (scale_top, scale_mid, scale_low) = scales
    gx, gy = ids[0], ids[1]
    rows_mid, rows_low = rows_all // 2, rows_all // 4

    for k in range(16):
        tile, slab = 5 + (k - 7) // 2, 2 * ((k - 7) % 2)
        pool_s[k, :, 0:128] = pools[tile, slab]
        pool_s[k, :, 128:256] = pools[tile, slab + 1]

    def enc_taps(k):
        put_taps(taps_a, k, 0, 32, pool_s[k], 8)
        sum_a[k] = dot(w_enc[...], taps_a[k])

    loop(16, enc_taps, 4)
    wide_in = inside(WIDE, 8, cols_all // 2, gy)

    def enc_act(k):
        value = silu(row_sum(sum_a, k, 64)) * (wide_in * row_ok(gx * 2 + k - 6, rows_mid))
        act_a[k] = value.astype(BF)

    loop(14, enc_act, 7)
    for m in range(4):
        pre = row_sum(sum_a, m + 5, 64)
        pre_one[m] = jnp.where(lane(128) < 96, pre[:, 0:128], pre[:, 128:256])
        taps_out[m] = taps_a[m + 6, :, 0:128]

    def low_taps(k):
        pooled = dot(act_a[2 * k], pool_low[...]) + dot(act_a[2 * k + 1], pool_low[...])
        put_taps(taps_b, k, 0, 64, pooled.astype(BF), 4)
        sum_b[k] = dot(w_bot[...], taps_b[k])

    loop(7, low_taps, 7)
    low_in = inside(LOW, 4, cols_all // 4, gy)
    mid_in = inside(MID, 8, cols_all // 2, gy)
    pick = jnp.where(lax.broadcasted_iota(jnp.int32, (64, 128), 1) < 96, 1.0, 0.0)
    near = pick.astype(BF)
    away = (1.0 - pick).astype(BF)

    def low_act(k):
        value = silu(row_sum(sum_b, k, 128)) * (low_in * row_ok(gx + k - 2, rows_low))
        act_b[k] = dot(value.astype(BF), up_low[...]).astype(BF)

    loop(5, low_act, 5)

    def mid_taps(k):
        put_taps(taps_c, k, 0, 192, act_b[(k + 1) // 2], 8)
        narrow = act_a[k + 3, :, 0:128] * near + act_a[k + 3, :, 128:256] * away
        put_taps(taps_c, k, 128, 192, narrow, 8)
        sum_c[k] = dot(w_mid[...], taps_c[k])

    loop(8, mid_taps, 4)

    def mid_act(k):
        pre = row_sum(sum_c, k, 64)
        pre_c[k] = pre
        value = silu(pre) * (mid_in * row_ok(gx * 2 + k - 2, rows_mid))
        act_c[k] = dot(value.astype(BF), up_mid[...]).astype(BF)

    loop(6, mid_act, 6)

    def skip_row(kind, k):
        part = (up, own, down)[k // 4]
        base = 12 * kind + 3 * (k % 4)
        return jnp.concatenate([part[base], part[base + 1], part[base + 2]], axis=1)

    for k in range(12):
        put_taps(taps_d, k, 64, 96, skip_row(0, k), 16)

    def top_taps(j):
        for half in range(2):
            put_taps(taps_d, 2 * j + half, 0, 96, act_c[j], 16)
            sum_d[2 * j + half] = dot(w_top[...], taps_d[2 * j + half])

    loop(6, top_taps, 3)
    for k in range(10):
        pre = row_sum(sum_d, k, 32)
        s = sigmoid(pre)
        if 3 <= k < 7:
            feat[k - 3] = (pre * s)[:, 0:256].astype(BF)
        cot = skip_row(1, k + 1).astype(F32)
        err_d[k] = (cot * (s * (1.0 + pre * (1.0 - s)))).astype(BF)

    def top_back(k):
        put_taps(taps_e, k, 0, 32, err_d[k], 16)
        sum_e[k] = dot(t_top[...], taps_e[k])

    loop(10, top_back, 5)

    total = None
    for k in range(6):
        parts = []
        for a in range(3):
            r = k - a
            own_row = 0 <= r < 4
            parts.append(err_d[r + 3, :, 0:256] if own_row else jnp.zeros((32, 256), BF))
        term = dot_nt(jnp.concatenate(parts, axis=0), taps_d[k + 3, :, 0:256])
        total = term if total is None else total + term
    put_padded(g_top, 0, total * scale_top)

    def mid_err(m):
        one = row_sum(sum_e, 2 * m, 96)
        two = row_sum(sum_e, 2 * m + 1, 96)
        whole = dot_split(one[0:64] + two[0:64], sum_mid[...])
        keep = mid_in * row_ok(gx * 2 + m - 1, rows_mid)
        err_c[m] = (whole * slope(pre_c[m + 1]) * keep).astype(BF)

    loop(4, mid_err, 4)
    for r in range(4):
        dskip[r] = row_sum(sum_e, r + 2, 96)[64:96, 0:256]

    def mid_back(m):
        put_taps(taps_f, m, 0, 64, err_c[m], 8)
        sum_f[m] = dot(t_mid[...], taps_f[m])

    loop(4, mid_back, 4)
    own_mid = jnp.where(lax.broadcasted_iota(jnp.int32, (64, 128), 1) < 64, 1.0, 0.0).astype(BF)
    for k in range(4):
        for a in range(3):
            r = k - a
            piece = err_c[r + 1] * own_mid if 0 <= r < 2 else jnp.zeros((64, 128), BF)
            stack[k, 64 * a : 64 * a + 64, :] = piece
    total = None
    for k in range(4):
        term = dot_nt(stack[k], taps_c[k + 2])
        total = term if total is None else total + term
    put_padded(g_mid, 0, total * scale_mid)

    one = row_sum(sum_f, 0, 192)
    two = row_sum(sum_f, 1, 192)
    whole = dot_split(one[0:128] + two[0:128], sum_low[...])
    keep = jnp.where(lane(128) < 16, 1.0, 0.0)
    err_low = (whole * slope(row_sum(sum_b, 2, 128)) * keep).astype(BF)
    packed[0:128, :] = err_low
    both = jnp.where(lane(128) < 64, one[128:192], pltpu.roll(two[128:192], 64, 1))
    packed[128:192, :] = both.astype(BF)
    for a in range(3):
        put_padded(g_bot, 128 * a, dot_nt(err_low, taps_b[a + 2]) * scale_low)


def join_kernel(own, left, right, out):
    wide = [ref[0:128, :].astype(F32) for ref in (own, right, left)]
    err = wide[0] + pltpu.roll(wide[1], 16, 1) + pltpu.roll(wide[2], 112, 1)
    out[0:128, :] = err.astype(BF)
    at = lane(128)
    mine, right, left = [ref[128:192, :].astype(F32) for ref in (own, right, left)]
    turned = [pltpu.roll(v, 64, 1) for v in (mine, right, left)]
    for row, (a, b, c) in enumerate(((mine, turned[1], turned[2]), (turned[0], right, left))):
        value = jnp.where(at < 64, a, jnp.where(at < 96, b, c))
        out[128 + 64 * row : 192 + 64 * row, :] = value.astype(BF)


def tail_kernel(sizes, scale_mid, *refs):
    (ids, own, mate, got, got_m, pre_one, taps_in, dskip) = refs[:8]
    (t_bot, t_enc, up_low, up_mid) = refs[8:12]
    (grad_skip, g_enc) = refs[12:14]
    (taps_a, sum_a, err_s, taps_b, sum_b) = refs[14:19]
    (rows_all, cols_all) = sizes
    gx, gy = ids[0], ids[1]
    rows_mid = rows_all // 2
    mid_in = inside(MID, 8, cols_all // 2, gy)

    low = jnp.where(gx % 2 == 0, 1.0, 0.0)
    high = 1.0 - low
    below = jnp.full((320, 128), low).astype(BF)
    above = jnp.full((320, 128), high).astype(BF)
    lower = got[...] * below + got_m[...] * above
    upper = got_m[...] * below + got[...] * above
    below, above = below[0:128], above[0:128]
    rows = (
        upper[128:256] * below + upper[0:128] * above,
        upper[0:128] * below + mate[0:128, :] * above,
        own[0:128, :],
        mate[0:128, :] * below + lower[0:128] * above,
        lower[0:128] * below + lower[128:256] * above,
    )
    for k, value in enumerate(rows):
        put_taps(taps_a, k, 0, 128, value, 4)
        sum_a[k] = dot(t_bot[...], taps_a[k])
    ups = [dot_split(row_sum(sum_a, k, 64), up_low[...]) * 0.125 for k in range(3)]
    parts = (
        upper[256:320].astype(F32) * low + mate[192:256, :].astype(F32) * high,
        own[128:192, :].astype(F32),
        own[192:256, :].astype(F32),
        mate[128:192, :].astype(F32) * low + lower[256:320].astype(F32) * high,
    )
    for m in range(4):
        part = parts[m]
        keep = mid_in * row_ok(gx * 2 + m - 1, rows_mid)
        err = (part + ups[(m + 1) // 2]) * slope(pre_one[m]) * keep
        err = err.astype(BF)
        err_s[m] = err
        put_taps(taps_b, m, 0, 64, err, 8)
        sum_b[m] = dot(t_enc[...], taps_b[m])
    own_mid = jnp.where(lax.broadcasted_iota(jnp.int32, (64, 128), 1) < 64, 1.0, 0.0).astype(BF)
    total = None
    for k in range(4):
        parts = []
        for a in range(3):
            r = k - a
            parts.append(err_s[r + 1] * own_mid if 0 <= r < 2 else jnp.zeros((64, 128), BF))
        term = dot_nt(jnp.concatenate(parts, axis=0), taps_in[k])
        total = term if total is None else total + term
    total = (total * scale_mid).astype(BF)
    g_enc[0:192, :] = total[:, 0:128]
    g_enc[192:384, :] = total[:, 128:256]
    rest = [total[48 * q : 48 * q + 48, 256:288] for q in range(4)]
    g_enc[384:432, :] = jnp.concatenate(rest, axis=1)
    for q in range(2):
        fine = dot_split(row_sum(sum_b, q, 32), up_mid[:, 0:256]) * 0.125
        for half in range(2):
            r = 2 * q + half
            grad_skip[r] = (dskip[r] + fine).astype(BF)


def finish_kernel(g, out):
    rest = jnp.concatenate([g[384:432, 32 * q : 32 * q + 32] for q in range(4)], axis=0)
    pieces = []
    for a in range(3):
        at = 64 * a
        pieces += [g[at : at + 64, :], g[192 + at : 256 + at, :], rest[at : at + 64, :]]
    out[...] = jnp.concatenate(pieces, axis=1).astype(F32)


VMEM = pl.BlockSpec(memory_space=pltpu.VMEM)
SMEM = pl.BlockSpec(memory_space=pltpu.SMEM)


def call(kernel, outs, scratch, scalars, *args, cost=1, grant=8):
    return pl.pallas_call(
        kernel,
        out_shape=[jax.ShapeDtypeStruct(s, d) for s, d in outs],
        in_specs=[SMEM] * scalars + [VMEM] * (len(args) - scalars),
        out_specs=[VMEM] * len(outs),
        scratch_shapes=[pltpu.VMEM(s, d) for s, d in scratch],
        compiler_params=pltpu.CompilerParams(vmem_limit_bytes=grant * 1024 * 1024),
        cost_estimate=pl.CostEstimate(
            flops=cost * 500_000_000, bytes_accessed=cost * 1_000_000, transcendentals=0
        ),
    )(*args)


def shift(value, axis, count, step):
    return lax.ppermute(value, axis, [(i, i + step) for i in range(count) if 0 <= i + step < count])


def outward(value, count, step):
    pairs = [(i, i + step if i % 2 else i - step) for i in range(count)]
    return lax.ppermute(value, "gx", [(i, j) for i, j in pairs if 0 <= j < count])


def tiles_of(g):
    rows, width = g.shape
    return g.reshape(rows // 8, 8, width // 128, 128).transpose(0, 2, 1, 3).reshape(-1, 8, 128)


def from_tiles(tiles, rows, width):
    wide = -(-width // 128)
    g = tiles.reshape(rows // 8, wide, 8, 128).transpose(0, 2, 1, 3).reshape(rows, wide * 128)
    return g[:, :width]


def full_gradient(g):
    rows, _ = g.shape
    out = rows // 3
    return jnp.concatenate([g[out * a : out * a + out] for a in range(3)], axis=1).astype(F32)


def solution(mesh):
    ngx, ngy = mesh.shape["gx"], mesh.shape["gy"]
    devices = ngx * ngy
    const = {k: np.asarray(v) for k, v in constants().items()}

    def step(skip_input, w_encoder, w_bottom, w_middle, w_upper, cotangent):
        gx, gy = lax.axis_index("gx"), lax.axis_index("gy")
        ids = jnp.stack([gx, gy]).astype(jnp.int32)
        rows_all, cols_all = 4 * ngx, 16 * ngy
        sizes = (rows_all, cols_all)
        cells = rows_all * cols_all * 16
        scales = tuple(1.0 / math.sqrt(cells // k) for k in (1, 8, 64))
        c = {k: jnp.asarray(v, BF) for k, v in const.items()}

        block, width = w_bottom.shape
        slabs = block * 2048 // 4096
        weight = jnp.pad(w_bottom, ((0, 0), (0, 2048 - width)))
        lanes = weight.shape[1] // 128
        weight = weight.reshape(block, lanes, 128).transpose(1, 0, 2).reshape(slabs, 32, 128)

        swap = [(i, i ^ 1) for i in range(ngx)]
        around = ngx // 4

        def along_y(i, k):
            side, y, core = i // (2 * around), i // 2 % around, i % 2
            return (side * around + (y + k) % around) * 2 + core

        part = ngy // 4 if ngy % 4 == 0 else ngy

        def mirrored(i):
            x, y = i // ngy, i % ngy
            y = (ngy // part - 1 - y // part) * part + y % part
            return (x + ngx // 2) % ngx * ngy + y

        w_line = [weight]
        for k in range(1, around):
            w_line.append(lax.ppermute(weight, "gx", [(i, along_y(i, k)) for i in range(ngx)]))
        w_line = jnp.concatenate(w_line, axis=0)
        w_far = lax.ppermute(w_line, AXES, [(i, mirrored(i)) for i in range(devices)])

        skip = skip_input.transpose(1, 0, 2)
        cot = cotangent.transpose(1, 0, 2)
        to_left, to_right = call(
            pool_kernel, [((10, 32, 128), BF)] * 2, [], 0, skip, cot, c["pool_tile"]
        )
        right = shift(to_left, "gy", ngy, -1)
        left = shift(to_right, "gy", ngy, 1)
        (own,) = call(widen_kernel, [((28, 32, 128), BF)], [], 0, skip, cot, to_left, right, left)
        core = gx % 2
        mate = lax.ppermute(own, "gx", swap)
        got = outward(jnp.concatenate([own, mate[24:28]], axis=0), ngx, 2)
        far = outward(jnp.concatenate([own[24:28], mate[24:28]], axis=0), ngx, 4)
        got, w_far = lax.optimization_barrier((got, w_far))
        w_mine = jnp.concatenate([w_line, w_far], axis=0)
        w_mate = lax.ppermute(w_mine, "gx", swap)
        got_m = lax.ppermute(got, "gx", swap)
        far_m = lax.ppermute(far, "gx", swap)
        fine, pools, w_bot, _, w_flat = call(
            lambda *refs: gather_kernel(ngx, block, *refs),
            [
                ((2, 24, 32, 128), BF),
                ((11, 4, 32, 128), BF),
                ((384, 576), BF),
                ((ngx, slabs, 32, 128), BF),
                ((ngx * block, lanes * 128), BF),
            ],
            [],
            1,
            ids,
            own,
            mate,
            got,
            got_m,
            far,
            far_m,
            w_mine,
            w_mate,
        )
        w_enc, t_enc, w_mid, t_mid, w_top, t_top = call(
            lambda *refs: weight_kernel((1, 1, 1), (1, 1, 1), *refs),
            [
                ((192, 288), BF),
                ((96, 576), BF),
                ((192, 1728), BF),
                ((576, 576), BF),
                ((96, 864), BF),
                ((288, 288), BF),
            ],
            [],
            0,
            w_encoder,
            w_middle,
            w_upper,
            cost=4,
        )
        (t_bot,) = call(
            lambda *refs: weight_kernel((0,), (1,), *refs),
            [((192, 1152), BF)],
            [],
            0,
            w_flat,
            cost=2,
        )

        outs = [
            ((4, 32, 256), BF),
            ((4, 32, 256), F32),
            ((192, 128), BF),
            ((4, 64, 128), F32),
            ((4, 288, 128), BF),
            ((96, 896), BF),
            ((192, 1792), BF),
            ((384, 640), BF),
        ]
        scratch = [
            ((16, 32, 256), BF),
            ((16, 288, 256), BF),
            ((16, 192, 256), F32),
            ((14, 64, 256), BF),
            ((7, 576, 128), BF),
            ((7, 384, 128), F32),
            ((5, 128, 128), BF),
            ((8, 1728, 128), BF),
            ((8, 192, 128), F32),
            ((6, 64, 384), BF),
            ((6, 64, 128), F32),
            ((12, 864, 384), BF),
            ((12, 96, 384), F32),
            ((10, 32, 384), BF),
            ((10, 288, 384), BF),
            ((10, 288, 384), F32),
            ((4, 64, 128), BF),
            ((4, 192, 128), BF),
            ((4, 576, 128), BF),
            ((4, 576, 128), F32),
        ]
        feat, dskip, packed, pre_one, taps_one, g_top, g_mid, g_bot = call(
            lambda *refs: main_kernel(sizes, scales, *refs),
            outs,
            scratch,
            1,
            ids,
            own,
            fine,
            pools,
            w_enc,
            w_bot,
            w_mid,
            w_top,
            t_top,
            t_mid,
            c["up_low"],
            c["sum_low"],
            c["up_mid"],
            c["sum_mid"],
            c["pool_low"],
            cost=20,
            grant=33,
        )

        def between_cores(tiles):
            half = tiles.shape[0] // 2
            keep = lax.dynamic_slice_in_dim(tiles, core * half, half, 0)
            other = lax.dynamic_slice_in_dim(tiles, (1 - core) * half, half, 0)
            other = lax.ppermute(other, "gx", swap)
            return (keep.astype(F32) + other.astype(F32)).astype(BF)

        grads = ((g_top, 864), (g_mid, 1728), (g_bot, 576))
        tiles = [tiles_of(g) for g, _ in grads]
        mine_main = between_cores(jnp.concatenate(tiles, axis=0))
        cut = mine_main.shape[0]
        last = cut + 27
        spare = -last % (devices // 2) + 27
        mine_main = jnp.pad(mine_main, ((0, spare), (0, 0), (0, 0)))

        from_left = shift(packed, "gy", ngy, 1)
        from_right = shift(packed, "gy", ngy, -1)
        (line,) = call(join_kernel, [((256, 128), BF)], [], 0, packed, from_left, from_right)
        mate = lax.ppermute(line, "gx", swap)
        edge = jnp.where(core == 0, line[128:192], line[192:256])
        got = outward(jnp.concatenate([line[0:128], mate[0:128], edge], axis=0), ngx, 2)
        got_m = lax.ppermute(got, "gx", swap)
        got_m, mine_main = lax.optimization_barrier((got_m, mine_main))
        grad_skip, g_enc = call(
            lambda *refs: tail_kernel(sizes, scales[1], *refs),
            [((4, 32, 256), BF), ((432, 128), BF)],
            [
                ((5, 1152, 128), BF),
                ((5, 192, 128), F32),
                ((4, 64, 128), BF),
                ((4, 576, 128), BF),
                ((4, 96, 128), F32),
            ],
            1,
            ids,
            line,
            mate,
            got,
            got_m,
            pre_one,
            taps_one,
            dskip,
            t_bot,
            t_enc,
            c["up_low"],
            c["up_mid"],
            cost=4,
        )

        mine_enc = between_cores(tiles_of(g_enc))
        mine = lax.dynamic_update_slice(mine_main, mine_enc, (cut, 0, 0))
        parts = mine.reshape(devices // 2, -1, 128)
        groups = [[i for i in range(devices) if i // ngy % 2 == k] for k in range(2)]
        parts = lax.all_to_all(
            parts, AXES, split_axis=0, concat_axis=0, axis_index_groups=groups, tiled=True
        )
        total = parts.astype(F32).sum(axis=0).astype(BF)
        spread = jnp.broadcast_to(total[None], parts.shape)
        spread = lax.all_to_all(
            spread, AXES, split_axis=0, concat_axis=0, axis_index_groups=groups, tiled=True
        )
        mine = spread.reshape(-1, 8, 128)
        other = lax.ppermute(mine, "gx", swap)
        first = jnp.where(core == 0, mine, other)
        second = jnp.where(core == 0, other, mine)
        whole = jnp.concatenate([first[:cut], second[:cut]], axis=0)
        full_enc = jnp.concatenate([first[cut:last], second[cut:last]], axis=0)
        full_enc = from_tiles(full_enc, 432, 128)

        full = []
        start = 0
        for (g, width), t in zip(grads, tiles):
            full.append(from_tiles(whole[start : start + t.shape[0]], g.shape[0], width))
            start += t.shape[0]
        full_top, full_mid, full_bot = full
        (full_enc,) = call(finish_kernel, [((64, 864), F32)], [], 0, full_enc)
        mine_bot = full_bot.reshape(3, ngx, block, -1)
        mine_bot = lax.dynamic_index_in_dim(mine_bot, gx, 1, keepdims=False)
        mine_bot = mine_bot.reshape(3 * block, -1)
        return (
            feat.transpose(1, 0, 2),
            grad_skip.transpose(1, 0, 2),
            full_enc,
            full_gradient(mine_bot),
            full_gradient(full_mid),
            full_gradient(full_top),
        )

    in_specs = (P(None, "gx", "gy"), P(), P("gx", None), P(), P(), P(None, "gx", "gy"))
    out_specs = (P(None, "gx", "gy"), P(None, "gx", "gy"), P(), P("gx", None), P(), P())
    return jax.shard_map(step, mesh=mesh, in_specs=in_specs, out_specs=out_specs, check_vma=False)
```
